128 devices in a mesh: tile: 16 (over y, x), slab: 8 (over z, core).
Axes of the slice: x: 4, y: 4, z: 4, core: 2. Of those that a mesh axis runs over, the one named last changes fastest.
Arguments:
- intensities: bfloat16 [1792, 256, 256], P(('tile', 'slab')), may hold values from 0 to 0.5
- object_field: float32 [2, 2, 4096, 384], P(None, None, ('tile', 'slab')), may hold values from -3 to 3
- probe_wave: float32 [256, 512], replicated, may hold values from -6 to 6
- owner_tile: int32 [1792], replicated, may hold values from 0 to 15, as said below
- row_offset: int32 [1792], replicated, may hold values from 0 to 255
- col_offset: int32 [1792], replicated, may hold values from 0 to 1
Outputs:
- gradient: float32 [2, 2, 4096, 384], P(None, None, ('tile', 'slab'))
The draws below stay inside these ranges and needn't reach their ends.
Inputs may be any that keep to these rules, and one draw needn't show every extreme that they name: `owner_tile`: read row r is read by device r // 14 of the tile+slab order. Among the 16 devices of one slab index, the rows of one device name one tile at most 2 times, and each tile is named by at most 16 of their rows; some tile reaches 16 and some device reaches 2 for some tile, for every slab index.
All inputs are finite; a program needn't handle non-finite values.
Results may differ from the reference program's by a relative error of at most 0.006.
The reference program's roundings to bfloat16 on the way count: a program that leaves them out, or rounds other values in their place, can miss the bound.
Values may be sent and summed in bfloat16 or wider, within the bound.
A program may use at most 64 MiB of HBM per device.

```python
import math
import jax
import jax.numpy as jnp
from jax import lax

PAT = 256
SLICES = 2
TH = 256
OW = 384
COL_STEP = 128
RD = 14
K = 16
ROWS = 4096
READS = 1792
N_TILE = 16
N_SLAB = 8


def column_owners(key):
    first_count = K // N_TILE
    keys = jax.random.split(key, 4)
    busiest = jax.random.randint(keys[0], (), 0, N_TILE).astype(jnp.int32)
    relabel = jax.random.permutation(keys[1], N_TILE).astype(jnp.int32)
    others = jax.random.permutation(keys[2], N_TILE - 1).astype(jnp.int32)
    position = jnp.arange(RD, dtype=jnp.int32)[None, :]
    later = jnp.maximum(position - first_count, 0)
    residue = (relabel[:, None] + later // 2) % (N_TILE - 1)
    other_tile = others[residue]
    other_tile = other_tile + (other_tile >= busiest).astype(jnp.int32)
    tile_holders = jnp.where(position < first_count, busiest, other_tile)
    shuffles = jax.vmap(lambda one_key: jax.random.permutation(one_key, RD).astype(jnp.int32))(jax.random.split(keys[3], N_TILE))
    return jnp.take_along_axis(tile_holders, shuffles, 1)


def draw_owner_tile(key, part):
    keys = jax.random.split(jax.random.fold_in(key, 17), N_SLAB)
    owner_table = jax.vmap(column_owners)(keys)
    return jnp.transpose(owner_table, (1, 0, 2)).reshape(-1).astype(jnp.int32)


def touch_ends(entries, rng, least, largest):
    shape = entries.shape
    spot = [jax.random.randint(jax.random.fold_in(rng, axis), (), 0, shape[axis]) for axis in range(len(shape))]
    entries = entries.at[tuple(spot)].set(least)
    longest = shape.index(max(shape))
    spot[longest] = (spot[longest] + 1) % shape[longest]
    return entries.at[tuple(spot)].set(largest)


def block_scale(key, shape, cuts, smallest, high):
    gain, own = 1.0, jax.random.fold_in(key, 6)
    for dim, shards_of in cuts:
        steps = jnp.exp(jax.random.uniform(jax.random.fold_in(own, dim), (shards_of,), jnp.float32, smallest / len(cuts), high / len(cuts)))
        gain = gain * jnp.repeat(steps, shape[dim] // shards_of).reshape([-1 if axis == dim else 1 for axis in range(len(shape))])
    return gain


def noise(rng, shape, width, bound, cuts=(), kind=jnp.bfloat16):
    values = width * jax.random.normal(rng, shape, jnp.float32)
    if cuts:
        values = values * block_scale(rng, shape, cuts, -0.22, 0.18)
    return jnp.clip(values, -bound, bound).astype(kind)


def setup_inputs(seed: int = 0) -> dict:
    seeds = jax.random.split(jax.random.key(seed), 7)
    return {
        "intensities": jnp.clip(0.5 * jax.random.uniform(seeds[0], (READS, PAT, PAT), jnp.float32) ** block_scale(seeds[0], (READS, PAT, PAT), ((0, 128),), -0.2, 0.2), 0.0, 0.5).astype(jnp.bfloat16),
        "object_field": noise(seeds[1], (SLICES, 2, ROWS, OW), 0.5, 3.0, ((2, 128),), jnp.float32),
        "probe_wave": noise(seeds[2], (PAT, 2 * PAT), 1.0, 6.0, (), jnp.float32),
        "owner_tile": draw_owner_tile(jax.random.fold_in(seeds[6], 71), 0),
        "row_offset": touch_ends(jax.random.randint(seeds[4], (READS,), 0, TH), jax.random.fold_in(seeds[4], 1), 0, TH - 1).astype(jnp.int32),
        "col_offset": touch_ends(jax.random.randint(seeds[5], (READS,), 0, (OW - PAT) // COL_STEP + 1), jax.random.fold_in(seeds[5], 1), 0, ((OW - PAT) // COL_STEP + 1) - 1).astype(jnp.int32),
    }


chirp_strength = 40.0

def make_tables(extent):
    counter = jnp.arange(extent, dtype=jnp.int32)
    product_index = counter[:, None] * counter[None, :] % extent
    angles = product_index.astype(jnp.float32) * (2.0 * math.pi / extent)
    scaling = 1.0 / math.sqrt(extent)
    cosine = (jnp.cos(angles) * scaling).astype(jnp.bfloat16)
    sine_part = (jnp.sin(angles) * scaling).astype(jnp.bfloat16)
    forward = jnp.concatenate([jnp.concatenate([cosine, -sine_part], 1), jnp.concatenate([sine_part, cosine], 1)], 0)
    inverse = jnp.concatenate([jnp.concatenate([cosine, sine_part], 1), jnp.concatenate([-sine_part, cosine], 1)], 0)
    frequency = ((counter + extent // 2) % extent - extent // 2).astype(jnp.float32) / extent
    phases = chirp_strength * (frequency[:, None] ** 2 + frequency[None, :] ** 2)
    kernel = jnp.concatenate([jnp.cos(phases), -jnp.sin(phases)], 1)
    return (cosine, sine_part, forward, inverse, kernel)

def transform(field, tables, backward):
    cosine, sine_part, forward, inverse, kernel = tables
    extent = cosine.shape[0]
    halfway = jnp.dot(field, inverse if backward else forward, preferred_element_type=jnp.float32).astype(jnp.bfloat16)
    with_cosine = jnp.dot(cosine, halfway, preferred_element_type=jnp.float32)
    with_sine = jnp.dot(sine_part, halfway, preferred_element_type=jnp.float32)
    if backward:
        real_part = with_cosine[:, :extent] - with_sine[:, extent:]
        imag_part = with_cosine[:, extent:] + with_sine[:, :extent]
    else:
        real_part = with_cosine[:, :extent] + with_sine[:, extent:]
        imag_part = with_cosine[:, extent:] - with_sine[:, :extent]
    return jnp.concatenate([real_part, imag_part], 1)

def complex_product(left, right, conjugate):
    extent = left.shape[1] // 2
    left_real = left[:, :extent]
    left_imag = -left[:, extent:] if conjugate else left[:, extent:]
    right_real = right[:, :extent]
    right_imag = right[:, extent:]
    return jnp.concatenate([left_real * right_real - left_imag * right_imag, left_real * right_imag + left_imag * right_real], 1)

def position_gradient(window, probe_wave, measured, tables):
    kernel = tables[4]
    extent = measured.shape[0]
    layers = window.shape[0]
    pieces = [jnp.concatenate([window[slice_index, 0], window[slice_index, 1]], 1) for slice_index in range(layers)]
    incoming = [probe_wave]
    entering = complex_product(probe_wave, pieces[0], False).astype(jnp.bfloat16)
    for slice_index in range(1, layers):
        spread_wave = complex_product(kernel, transform(entering, tables, False), False).astype(jnp.bfloat16)
        arrived = transform(spread_wave, tables, True)
        incoming.append(arrived)
        entering = complex_product(arrived, pieces[slice_index], False).astype(jnp.bfloat16)
    farfield = transform(entering, tables, False)
    modelled = farfield[:, :extent] ** 2 + farfield[:, extent:] ** 2
    misfit = modelled - measured.astype(jnp.float32)
    far_grad = (farfield * jnp.concatenate([misfit, misfit], 1)).astype(jnp.bfloat16)
    exit_grad = transform(far_grad, tables, True)
    slice_terms = [None] * layers
    for slice_index in range(layers - 1, -1, -1):
        slice_terms[slice_index] = complex_product(incoming[slice_index], exit_grad, True)
        if slice_index > 0:
            back_wave = complex_product(pieces[slice_index], exit_grad, True).astype(jnp.bfloat16)
            back_spread = complex_product(kernel, transform(back_wave, tables, False), True).astype(jnp.bfloat16)
            exit_grad = transform(back_spread, tables, True)
    return jnp.stack([jnp.stack([one_term[:, :extent], one_term[:, extent:]]) for one_term in slice_terms])

def reference(intensities, object_field, probe_wave, owner_tile, row_offset, col_offset):
    extent = intensities.shape[1]
    depth = object_field.shape[0]
    total_rows = object_field.shape[2]
    columns_all = object_field.shape[3]
    tables = make_tables(extent)
    extended = jnp.concatenate([object_field, object_field[:, :, :extent]], 2)

    def accumulate(totals, inputs):
        measured, owner, row_part, col_part = inputs
        top_row = (owner * TH + row_part).astype(jnp.int32)
        left_col = (col_part * COL_STEP).astype(jnp.int32)
        zero_index = jnp.zeros((), jnp.int32)
        starting = (zero_index, zero_index, top_row, left_col)
        window = lax.dynamic_slice(extended, starting, (depth, 2, extent, extent))
        gradient_part = position_gradient(window, probe_wave, measured, tables)
        current = lax.dynamic_slice(totals, starting, (depth, 2, extent, extent))
        return (lax.dynamic_update_slice(totals, current + gradient_part, starting), None)
    initial = jnp.zeros((depth, 2, total_rows + extent, columns_all), jnp.float32)
    totals = lax.scan(accumulate, initial, (intensities, owner_tile, row_offset, col_offset))[0]
    folded = jnp.concatenate([totals[:, :, total_rows:], jnp.zeros((depth, 2, total_rows - extent, columns_all), jnp.float32)], 2)
    return totals[:, :, :total_rows] + folded
```

```python
import functools
import math

import jax
import jax.numpy as jnp
import numpy as np
from jax import lax
from jax.experimental import pallas as pl
from jax.experimental.pallas import tpu as pltpu
from jax.sharding import PartitionSpec as P

bf16 = jnp.bfloat16
f32 = jnp.float32
MESH = pl.DeviceIdType.MESH
K = 16
CAP = 2
COL_STEP = 128
CHIRP = 40.0
LANES = 128
CHUNK = 64
VMEM_LIMIT = 60 * 2**20

smem = pl.BlockSpec(memory_space=pltpu.SMEM)
vmem = pl.BlockSpec(memory_space=pltpu.VMEM)
anyspace = pl.BlockSpec(memory_space=pl.ANY)


def make_tables(n):
    count = np.arange(n)
    angles = ((count[:, None] * count[None, :]) % n).astype(np.float32)
    angles = angles * np.float32(2.0 * math.pi / n)
    scale = np.float32(1.0 / math.sqrt(n))
    c = np.cos(angles) * scale
    s = np.sin(angles) * scale
    forward = np.block([[c, -s], [s, c]]).astype(np.float32)
    inverse = np.block([[c, s], [-s, c]]).astype(np.float32)
    f = (((count + n // 2) % n) - n // 2).astype(np.float32) / np.float32(n)
    phases = np.float32(CHIRP) * (f[:, None] ** 2 + f[None, :] ** 2)
    kernel = np.stack([np.cos(phases), -np.sin(phases)]).astype(np.float32)
    return jnp.asarray(forward, bf16), jnp.asarray(inverse, bf16), jnp.asarray(kernel)


def pack_kernel(tiles, slabs, reads, owner, rowoff, coloff, images, field,
                packed, count, slot, row, col, shard, hold, used, insem, outsem):
    tile = lax.axis_index("tile")
    slab = lax.axis_index("slab")
    for k in range(reads):
        pltpu.make_async_copy(images.at[k], hold.at[k], insem.at[k]).start()
    for t in range(tiles):
        used[t] = 0
    for k in range(reads):
        dest = owner[(tile * slabs + slab) * reads + k]
        rank = used[dest]
        used[dest] = rank + 1
        pltpu.make_async_copy(images.at[k], hold.at[k], insem.at[k]).wait()
        pltpu.make_async_copy(hold.at[k], packed.at[dest, rank], outsem.at[k]).start()
    for s in range(2):
        for q in range(2):
            for h in range(3):
                shard[2 * s + q, h] = field[s, q, :, h * LANES:(h + 1) * LANES]

    def sender(i, found):
        base = (i * slabs + slab) * reads

        def one(k, state):
            n, rank = state
            hit = owner[base + k] == tile
            slot[n] = i * CAP + rank
            row[n] = rowoff[base + k]
            col[n] = coloff[base + k]
            step = hit.astype(jnp.int32)
            return n + step, rank + step

        return lax.fori_loop(0, reads, one, (found, jnp.int32(0)), unroll=True)[0]

    count[0] = lax.fori_loop(0, tiles, sender, jnp.int32(0))
    for k in range(reads):
        pltpu.make_async_copy(hold.at[k], packed.at[0, 0], outsem.at[k]).wait()


def pack(owner, rowoff, coloff, images, field, tiles, slabs):
    reads, n, _ = images.shape
    rows = field.shape[2]
    return pl.pallas_call(
        functools.partial(pack_kernel, tiles, slabs, reads),
        out_shape=(
            jax.ShapeDtypeStruct((tiles, CAP, n, n), bf16),
            jax.ShapeDtypeStruct((1,), jnp.int32),
            jax.ShapeDtypeStruct((K + 1,), jnp.int32),
            jax.ShapeDtypeStruct((K + 1,), jnp.int32),
            jax.ShapeDtypeStruct((K + 1,), jnp.int32),
            jax.ShapeDtypeStruct((4, 3, rows, LANES), f32),
        ),
        in_specs=[smem, smem, smem, anyspace, vmem],
        out_specs=(anyspace, smem, smem, smem, smem, vmem),
        scratch_shapes=[
            pltpu.VMEM((reads, n, n), bf16),
            pltpu.SMEM((tiles,), jnp.int32),
            pltpu.SemaphoreType.DMA((reads,)),
            pltpu.SemaphoreType.DMA((reads,)),
        ],
        name="pack",
    )(owner, rowoff, coloff, images, field)


def exchange_kernel(tiles, slabs, rows, packed, shard, got, field,
                    hold, localsem, psend, precv, nsend, nrecv, asend, arecv, bsend, brecv):
    tile = lax.axis_index("tile")
    slab = lax.axis_index("slab")
    before = lax.rem(tile + tiles - 1, tiles)
    barrier = pltpu.get_barrier_semaphore()
    for d in range(1, tiles):
        peer = lax.rem(tile + d, tiles)
        pl.semaphore_signal(barrier, inc=1, device_id={"tile": peer, "slab": slab}, device_id_type=MESH)
    for d in range(1, slabs):
        peer = lax.rem(slab + d, slabs)
        pl.semaphore_signal(barrier, inc=1, device_id={"tile": tile, "slab": peer}, device_id_type=MESH)
    pl.semaphore_wait(barrier, tiles - 1 + slabs - 1)

    height = rows * slabs
    mine = field.at[:, :, pl.ds(pl.multiple_of(slab * rows, rows), rows), :]
    after = field.at[:, :, pl.ds(pl.multiple_of(height + slab * rows, rows), rows), :]
    copies = []

    def push(src, dst, send, recv, t, s):
        copy = pltpu.make_async_remote_copy(
            src_ref=src, dst_ref=dst, send_sem=send, recv_sem=recv,
            device_id={"tile": t, "slab": s}, device_id_type=MESH,
        )
        copy.start()
        return copy

    ahead = push(shard, after, nsend, nrecv, before, slab)
    for d in range(1, slabs):
        copies.append(push(shard, mine, asend.at[d - 1], arecv.at[d - 1], tile, lax.rem(slab + d, slabs)))
    for d in range(1, tiles):
        peer = lax.rem(tile + d, tiles)
        copies.append(push(packed.at[peer], got.at[tile], psend.at[d - 1], precv.at[d - 1], peer, slab))
    keep = pltpu.make_async_copy(shard, mine, localsem.at[0])
    keep.start()
    first = pltpu.make_async_copy(packed.at[tile], hold, localsem.at[1])
    first.start()
    first.wait()
    second = pltpu.make_async_copy(hold, got.at[tile], localsem.at[1])
    second.start()
    ahead.wait()
    for d in range(1, slabs):
        copies.append(push(after, after, bsend.at[d - 1], brecv.at[d - 1], tile, lax.rem(slab + d, slabs)))
    second.wait()
    keep.wait()
    for copy in copies:
        copy.wait()


def exchange(packed, shard, tiles, slabs):
    _, _, n, _ = packed.shape
    planes, cols, rows, lanes = shard.shape
    sem = pltpu.SemaphoreType.DMA
    return pl.pallas_call(
        functools.partial(exchange_kernel, tiles, slabs, rows),
        out_shape=(
            jax.ShapeDtypeStruct(packed.shape, packed.dtype),
            jax.ShapeDtypeStruct((planes, cols, 2 * rows * slabs, lanes), shard.dtype),
        ),
        in_specs=[anyspace, vmem],
        out_specs=(anyspace, anyspace),
        scratch_shapes=[
            pltpu.VMEM((CAP, n, n), bf16),
            sem((2,)),
            sem((tiles - 1,)), sem((tiles - 1,)),
            sem, sem,
            sem((slabs - 1,)), sem((slabs - 1,)),
            sem((slabs - 1,)), sem((slabs - 1,)),
        ],
        compiler_params=pltpu.CompilerParams(collective_id=0, has_side_effects=True),
        name="exchange",
    )(packed, shard)


def grad_kernel(count, slot, row, col, field, images, probe, forward, inverse, kernel,
                total, x, h, y, wave, image, imsem):
    n = 256
    total[...] = jnp.zeros_like(total)

    def fetch(i):
        index = slot[i]
        return pltpu.make_async_copy(
            images.at[lax.div(index, CAP), lax.rem(index, CAP)], image.at[lax.rem(i, 2)], imsem.at[lax.rem(i, 2)]
        )

    def transform(backward):
        right = inverse if backward else forward
        left = forward if backward else inverse
        half = jnp.dot(x[...], right[...], preferred_element_type=f32)
        h[:n, :] = half[:, :n].astype(bf16)
        h[n:, :] = half[:, n:].astype(bf16)
        y[...] = jnp.dot(left[...], h[...], preferred_element_type=f32)

    def product(ar, ai, br, bi):
        return ar * br - ai * bi, ar * bi + ai * br

    def conjugate_product(ar, ai, br, bi):
        return ar * br + ai * bi, ar * bi - ai * br

    def step(i, carry):
        top = row[i]
        left = col[i]
        fetch(i).wait()

        @pl.when(i + 1 < count[0])
        def _():
            fetch(i + 1).start()

        def window(s, q, r, c):
            return field[2 * s + q, left + c, pl.ds(top + r, CHUNK), :].astype(f32)

        def add(s, r, c, re, im):
            total[2 * s, left + c, pl.ds(top + r, CHUNK), :] += re
            total[2 * s + 1, left + c, pl.ds(top + r, CHUNK), :] += im

        def put(r, c, parts):
            x[r:r + CHUNK, c * LANES:(c + 1) * LANES] = parts[0].astype(bf16)
            x[r:r + CHUNK, n + c * LANES:n + (c + 1) * LANES] = parts[1].astype(bf16)

        def pieces():
            for r in range(0, n, CHUNK):
                for c in range(2):
                    yield r, c, slice(r, r + CHUNK), slice(n + r, n + r + CHUNK), slice(c * LANES, (c + 1) * LANES)

        for r, c, a, b, l in pieces():
            put(r, c, product(probe[a, l], probe[a, n + c * LANES:n + (c + 1) * LANES], window(0, 0, r, c), window(0, 1, r, c)))
        transform(False)
        for r, c, a, b, l in pieces():
            put(r, c, product(kernel[0, a, l], kernel[1, a, l], y[a, l], y[b, l]))
        transform(True)
        for r, c, a, b, l in pieces():
            re, im = y[a, l], y[b, l]
            wave[a, l] = re
            wave[b, l] = im
            put(r, c, product(re, im, window(1, 0, r, c), window(1, 1, r, c)))
        transform(False)
        for r, c, a, b, l in pieces():
            re, im = y[a, l], y[b, l]
            misfit = re * re + im * im - image[lax.rem(i, 2), a, l].astype(f32)
            put(r, c, (re * misfit, im * misfit))
        transform(True)
        for r, c, a, b, l in pieces():
            re, im = y[a, l], y[b, l]
            add(1, r, c, *conjugate_product(wave[a, l], wave[b, l], re, im))
            put(r, c, conjugate_product(window(1, 0, r, c), window(1, 1, r, c), re, im))
        transform(False)
        for r, c, a, b, l in pieces():
            put(r, c, conjugate_product(kernel[0, a, l], kernel[1, a, l], y[a, l], y[b, l]))
        transform(True)
        for r, c, a, b, l in pieces():
            add(0, r, c, *conjugate_product(probe[a, l], probe[a, n + c * LANES:n + (c + 1) * LANES], y[a, l], y[b, l]))
        return carry

    @pl.when(count[0] > 0)
    def _():
        fetch(0).start()

    lax.fori_loop(0, count[0], step, 0)


def gradient(count, slot, row, col, field, images, probe):
    n = probe.shape[0]
    forward, inverse, kernel = make_tables(n)
    return pl.pallas_call(
        grad_kernel,
        out_shape=jax.ShapeDtypeStruct(field.shape, f32),
        in_specs=[smem] * 4 + [vmem, anyspace] + [vmem] * 4,
        out_specs=vmem,
        scratch_shapes=[
            pltpu.VMEM((n, 2 * n), bf16),
            pltpu.VMEM((2 * n, n), bf16),
            pltpu.VMEM((2 * n, n), f32),
            pltpu.VMEM((2 * n, n), f32),
            pltpu.VMEM((2, n, n), bf16),
            pltpu.SemaphoreType.DMA((2,)),
        ],
        compiler_params=pltpu.CompilerParams(vmem_limit_bytes=VMEM_LIMIT),
        name="gradient",
    )(count, slot, row, col, field, images, probe, forward, inverse, kernel)


def reduce_kernel(tiles, slabs, cores, total, out, part, near, far, outgoing,
                  localsem, csend, crecv, zsend, zrecv, fsend, frecv):
    tile = lax.axis_index("tile")
    slab = lax.axis_index("slab")
    levels = slabs // cores
    core = lax.rem(slab, cores)
    level = lax.div(slab, cores)
    other = level * cores + (1 - core)
    following = lax.rem(tile + 1, tiles)
    preceding = lax.rem(tile + tiles - 1, tiles)
    barrier = pltpu.get_barrier_semaphore()

    def greet(t, s):
        pl.semaphore_signal(barrier, inc=1, device_id={"tile": t, "slab": s}, device_id_type=MESH)

    greet(tile, other)
    for d in range(1, levels):
        greet(tile, lax.rem(level + d, levels) * cores + core)
    for d in range(levels):
        place = lax.rem(level + d, levels) * cores + core
        greet(following, place)
        greet(preceding, place)
    pl.semaphore_wait(barrier, 1 + levels - 1 + 2 * levels)

    def block(which, d):
        return which * levels + lax.rem(level + d, levels)

    order = [(1, 2), (1, 1), (1, 3), (0, 2), (0, 1), (0, 3), (1, 0), (0, 0)]
    swaps = []
    takes = []
    for k, (which, d) in enumerate(order):
        b = block(which, d)
        copy = pltpu.make_async_remote_copy(
            src_ref=total.at[:, :, b, 1 - core], dst_ref=near.at[k], send_sem=csend.at[k], recv_sem=crecv.at[k],
            device_id={"tile": tile, "slab": other}, device_id_type=MESH,
        )
        copy.start()
        swaps.append(copy)
        take = pltpu.make_async_copy(total.at[:, :, b, core], part.at[k], localsem.at[k])
        take.start()
        takes.append(take)
    sends = []
    for k, (which, d) in enumerate(order):
        takes[k].wait()
        swaps[k].wait_recv()
        if (which, d) == (0, 0):
            continue
        outgoing[k] = (part[k] + near[k]).astype(bf16)
        place = lax.rem(level + d, levels) * cores + core
        if which == 0:
            copy = pltpu.make_async_remote_copy(
                src_ref=outgoing.at[k], dst_ref=far.at[d - 1], send_sem=zsend.at[d - 1], recv_sem=zrecv.at[d - 1],
                device_id={"tile": tile, "slab": place}, device_id_type=MESH,
            )
        else:
            copy = pltpu.make_async_remote_copy(
                src_ref=outgoing.at[k], dst_ref=far.at[levels - 1 + d], send_sem=fsend.at[d], recv_sem=frecv.at[d],
                device_id={"tile": following, "slab": place}, device_id_type=MESH,
            )
        copy.start()
        sends.append(copy)
    for copy in sends:
        copy.wait()
    for copy in swaps:
        copy.wait_send()
    last = len(order) - 1
    for p in range(4):
        for h in range(3):
            value = part[last, p, h] + near[last, p, h]
            for k in range(2 * levels - 1):
                value = value + far[k, p, h].astype(f32)
            out[p // 2, p % 2, :, h * LANES:(h + 1) * LANES] = value


def reduce(total, tiles, slabs):
    cores = 2
    levels = slabs // cores
    planes, cols, rows, lanes = total.shape
    each = rows // (2 * slabs)
    sem = pltpu.SemaphoreType.DMA
    total = total.reshape(planes, cols, 2 * levels, cores, each, lanes)
    count = 2 * levels
    return pl.pallas_call(
        functools.partial(reduce_kernel, tiles, slabs, cores),
        out_shape=jax.ShapeDtypeStruct((2, 2, each, cols * lanes), f32),
        in_specs=[anyspace],
        out_specs=vmem,
        scratch_shapes=[
            pltpu.VMEM((count, planes, cols, each, lanes), f32),
            pltpu.VMEM((count, planes, cols, each, lanes), f32),
            pltpu.VMEM((count - 1, planes, cols, each, lanes), bf16),
            pltpu.VMEM((count, planes, cols, each, lanes), bf16),
            sem((count,)),
            sem((count,)), sem((count,)),
            sem((levels - 1,)), sem((levels - 1,)),
            sem((levels,)), sem((levels,)),
        ],
        compiler_params=pltpu.CompilerParams(collective_id=1, has_side_effects=True, vmem_limit_bytes=VMEM_LIMIT),
        name="reduce",
    )(total)


def shards(intensities, object_field, probe_wave, owner_tile, row_offset, col_offset):
    tiles = lax.axis_size("tile")
    slabs = lax.axis_size("slab")
    packed, count, slot, row, col, shard = pack(
        owner_tile, row_offset, col_offset, intensities, object_field, tiles, slabs
    )
    images, field = exchange(packed, shard, tiles, slabs)
    total = gradient(count, slot, row, col, field, images, probe_wave)
    return reduce(total, tiles, slabs)


def solution(mesh):
    placed = (
        P(("tile", "slab"), None, None),
        P(None, None, ("tile", "slab"), None),
        P(),
        P(),
        P(),
        P(),
    )
    return jax.shard_map(
        shards,
        mesh=mesh,
        in_specs=placed,
        out_specs=P(None, None, ("tile", "slab"), None),
        check_vma=False,
    )
```

```python
import functools
import math

import jax
import jax.numpy as jnp
import numpy as np
from jax import lax
from jax.experimental import pallas as pl
from jax.experimental.pallas import tpu as pltpu
from jax.sharding import PartitionSpec as P

bf16 = jnp.bfloat16
f32 = jnp.float32
MESH = pl.DeviceIdType.MESH
K = 16
CAP = 2
COL_STEP = 128
CHIRP = 40.0
LANES = 128
HALF = 64
VMEM_LIMIT = 60 * 2**20

smem = pl.BlockSpec(memory_space=pltpu.SMEM)
vmem = pl.BlockSpec(memory_space=pltpu.VMEM)
anyspace = pl.BlockSpec(memory_space=pl.ANY)


def make_tables(n):
    count = np.arange(n)
    angles = ((count[:, None] * count[None, :]) % n).astype(np.float32)
    angles = angles * np.float32(2.0 * math.pi / n)
    scale = np.float32(1.0 / math.sqrt(n))
    c = (np.cos(angles) * scale).astype(np.float32)
    s = (np.sin(angles) * scale).astype(np.float32)
    forward = np.block([[c, -s], [s, c]])
    inverse = np.block([[c, s], [-s, c]])
    even = np.arange(0, n, 2)
    odd = even + 1
    low = np.concatenate([even[: n // 4], odd[: n // 4]])

    def left(sign, inputs):
        cc = c[np.ix_(low, inputs)]
        ss = s[np.ix_(low, inputs)] * np.float32(sign)
        return np.block([[cc, ss], [-ss, cc]])

    left_forward = np.stack([left(1, even), left(1, odd)])
    left_inverse = np.stack([left(-1, even), left(-1, odd)])
    f = (((count + n // 2) % n) - n // 2).astype(np.float32) / np.float32(n)
    phases = np.float32(CHIRP) * (f[:, None] ** 2 + f[None, :] ** 2)
    kernel = np.stack([np.cos(phases), -np.sin(phases)]).astype(np.float32)
    kernel = kernel[:, np.concatenate([even, odd]), :]

    def low_precision(a):
        return jnp.asarray(a.astype(np.float32), bf16)

    return (
        low_precision(forward), low_precision(inverse),
        low_precision(left_forward), low_precision(left_inverse), jnp.asarray(kernel),
    )


def pack_kernel(tiles, slabs, reads, owner, rowoff, coloff, images, field,
                packed, count, slot, row, col, shard, hold, used, insem, outsem):
    tile = lax.axis_index("tile")
    slab = lax.axis_index("slab")
    for k in range(reads):
        pltpu.make_async_copy(images.at[k], hold.at[k], insem.at[k]).start()
    for t in range(tiles):
        used[t] = 0
    for k in range(reads):
        dest = owner[(tile * slabs + slab) * reads + k]
        rank = used[dest]
        used[dest] = rank + 1
        pltpu.make_async_copy(images.at[k], hold.at[k], insem.at[k]).wait()
        pltpu.make_async_copy(hold.at[k], packed.at[dest, rank], outsem.at[k]).start()
    for s in range(2):
        for q in range(2):
            for h in range(3):
                shard[2 * s + q, h] = field[s, q, :, h * LANES:(h + 1) * LANES]

    def sender(i, found):
        base = (i * slabs + slab) * reads

        def one(k, state):
            n, rank = state
            hit = owner[base + k] == tile
            slot[n] = i * CAP + rank
            row[n] = rowoff[base + k]
            col[n] = coloff[base + k]
            step = hit.astype(jnp.int32)
            return n + step, rank + step

        return lax.fori_loop(0, reads, one, (found, jnp.int32(0)), unroll=True)[0]

    count[0] = lax.fori_loop(0, tiles, sender, jnp.int32(0))
    for k in range(reads):
        pltpu.make_async_copy(hold.at[k], packed.at[0, 0], outsem.at[k]).wait()


def pack(owner, rowoff, coloff, images, field, tiles, slabs):
    reads, n, _ = images.shape
    rows = field.shape[2]
    return pl.pallas_call(
        functools.partial(pack_kernel, tiles, slabs, reads),
        out_shape=(
            jax.ShapeDtypeStruct((tiles, CAP, n, n), bf16),
            jax.ShapeDtypeStruct((1,), jnp.int32),
            jax.ShapeDtypeStruct((K + 1,), jnp.int32),
            jax.ShapeDtypeStruct((K + 1,), jnp.int32),
            jax.ShapeDtypeStruct((K + 1,), jnp.int32),
            jax.ShapeDtypeStruct((4, 3, rows, LANES), f32),
        ),
        in_specs=[smem, smem, smem, anyspace, vmem],
        out_specs=(anyspace, smem, smem, smem, smem, vmem),
        scratch_shapes=[
            pltpu.VMEM((reads, n, n), bf16),
            pltpu.SMEM((tiles,), jnp.int32),
            pltpu.SemaphoreType.DMA((reads,)),
            pltpu.SemaphoreType.DMA((reads,)),
        ],
        name="pack",
    )(owner, rowoff, coloff, images, field)


ROUTE = (
    (1, 0), (3, 0), (2, 0), (1, 1), (3, 3), (1, 3), (3, 1), (2, 1),
    (2, 3), (1, 2), (3, 2), (2, 2), (0, 1), (0, 3), (0, 2),
)


def exchange_kernel(tiles, slabs, rows, packed, shard, got, field,
                    hold, localsem, psend, precv, nsend, nrecv, asend, arecv, bsend, brecv):
    tile = lax.axis_index("tile")
    slab = lax.axis_index("slab")
    before = lax.rem(tile + tiles - 1, tiles)
    barrier = pltpu.get_barrier_semaphore()
    for d in range(1, tiles):
        peer = lax.rem(tile + d, tiles)
        pl.semaphore_signal(barrier, inc=1, device_id={"tile": peer, "slab": slab}, device_id_type=MESH)
    for d in range(1, slabs):
        peer = lax.rem(slab + d, slabs)
        pl.semaphore_signal(barrier, inc=1, device_id={"tile": tile, "slab": peer}, device_id_type=MESH)
    pl.semaphore_wait(barrier, tiles - 1 + slabs - 1)

    height = rows * slabs
    mine = field.at[:, :, pl.ds(pl.multiple_of(slab * rows, rows), rows), :]
    after = field.at[:, :, pl.ds(pl.multiple_of(height + slab * rows, rows), rows), :]
    copies = []

    def push(src, dst, send, recv, t, s):
        copy = pltpu.make_async_remote_copy(
            src_ref=src, dst_ref=dst, send_sem=send, recv_sem=recv,
            device_id={"tile": t, "slab": s}, device_id_type=MESH,
        )
        copy.start()
        return copy

    ahead = push(shard, after, nsend, nrecv, before, slab)
    for d in range(1, slabs):
        copies.append(push(shard, mine, asend.at[d - 1], arecv.at[d - 1], tile, lax.rem(slab + d, slabs)))
    side = math.isqrt(tiles)
    for k, (dy, dx) in enumerate(ROUTE):
        peer = lax.rem(lax.div(tile, side) + dy, side) * side + lax.rem(lax.rem(tile, side) + dx, side)
        copies.append(push(packed.at[peer], got.at[tile], psend.at[k], precv.at[k], peer, slab))
    keep = pltpu.make_async_copy(shard, mine, localsem.at[0])
    keep.start()
    first = pltpu.make_async_copy(packed.at[tile], hold, localsem.at[1])
    first.start()
    first.wait()
    second = pltpu.make_async_copy(hold, got.at[tile], localsem.at[1])
    second.start()
    ahead.wait()
    for d in range(1, slabs):
        copies.append(push(after, after, bsend.at[d - 1], brecv.at[d - 1], tile, lax.rem(slab + d, slabs)))
    second.wait()
    keep.wait()
    for copy in copies:
        copy.wait()


def exchange(packed, shard, tiles, slabs):
    _, _, n, _ = packed.shape
    planes, cols, rows, lanes = shard.shape
    sem = pltpu.SemaphoreType.DMA
    return pl.pallas_call(
        functools.partial(exchange_kernel, tiles, slabs, rows),
        out_shape=(
            jax.ShapeDtypeStruct(packed.shape, packed.dtype),
            jax.ShapeDtypeStruct((planes, cols, 2 * rows * slabs, lanes), shard.dtype),
        ),
        in_specs=[anyspace, vmem],
        out_specs=(anyspace, anyspace),
        scratch_shapes=[
            pltpu.VMEM((CAP, n, n), bf16),
            sem((2,)),
            sem((tiles - 1,)), sem((tiles - 1,)),
            sem, sem,
            sem((slabs - 1,)), sem((slabs - 1,)),
            sem((slabs - 1,)), sem((slabs - 1,)),
        ],
        compiler_params=pltpu.CompilerParams(collective_id=0, has_side_effects=True),
        name="exchange",
    )(packed, shard)


def product(ar, ai, br, bi):
    return ar * br - ai * bi, ar * bi + ai * br


def conjugate_product(ar, ai, br, bi):
    return ar * br + ai * bi, ar * bi - ai * br


def lanes(c):
    return slice(c * LANES, (c + 1) * LANES)


def rows_of(p, b):
    return slice(2 * HALF * p + HALF * b, 2 * HALF * p + HALF * b + HALF)


def spread_rows(start, p, b):
    return pl.ds(start + p + 2 * HALF * b, HALF, stride=2)


def grad_kernel(count, slot, row, col, field, images, probe_in, rf, ri, lf, li, kernel,
                total, x, h, y, wave, measured, probe, image, imsem):
    n = 4 * HALF
    dump = field.shape[2]
    total[...] = jnp.zeros_like(total)
    live = count[0]
    for g in range(4):
        probe[g] = probe_in[:, lanes(g)]

    def fetch(i):
        index = slot[i]
        return pltpu.make_async_copy(
            images.at[lax.div(index, CAP), lax.rem(index, CAP)], image.at[lax.rem(i, 4)], imsem.at[lax.rem(i, 4)]
        )

    def pattern(i, j, valid):
        top = row[i]
        left = col[i]
        place = top if valid is None else jnp.where(valid, top, dump)
        xj, hj, yj, wj, mj = x.at[j], h.at[j], y.at[j], wave.at[j], measured.at[j]
        source = image.at[lax.rem(i, 4)]

        def window(s, p, b, c):
            where = spread_rows(top, p, b)
            return field[2 * s, left + c, where, :], field[2 * s + 1, left + c, where, :]

        def add(s, p, b, c, parts):
            where = spread_rows(place, p, b)
            total[2 * s, left + c, where, :] += parts[0]
            total[2 * s + 1, left + c, where, :] += parts[1]

        def put(p, b, c, parts):
            xj[rows_of(p, b), lanes(c)] = parts[0].astype(bf16)
            xj[rows_of(p, b), lanes(2 + c)] = parts[1].astype(bf16)

        def lit(p, b, c):
            where = spread_rows(0, p, b)
            return probe[c, where, :], probe[2 + c, where, :]

        def chirp(p, b, c):
            return kernel[0, rows_of(p, b), lanes(c)], kernel[1, rows_of(p, b), lanes(c)]

        def each(use):
            for p in range(2):
                for c in range(2):
                    l = lanes(c)
                    parts = [yj[HALF * k:HALF * k + HALF, l] for k in (p, 2 + p, 4 + p, 6 + p)]
                    use(p, 0, c, parts[0] + parts[2], parts[1] + parts[3])
                    use(p, 1, c, parts[0] - parts[2], parts[1] - parts[3])

        def transform(backward):
            right = ri if backward else rf
            lt = li if backward else lf
            half = jnp.dot(xj[...], right[...], preferred_element_type=f32)
            m = n // 2
            hj[0:m, :] = half[:m, :n].astype(bf16)
            hj[m:n, :] = half[:m, n:].astype(bf16)
            hj[n:n + m, :] = half[m:, :n].astype(bf16)
            hj[n + m:, :] = half[m:, n:].astype(bf16)
            yj[:n, :] = jnp.dot(lt[0], hj[:n, :], preferred_element_type=f32)
            yj[n:, :] = jnp.dot(lt[1], hj[n:, :], preferred_element_type=f32)

        def begin():
            for p in range(2):
                for b in range(2):
                    for c in range(2):
                        put(p, b, c, product(*lit(p, b, c), *window(0, p, b, c)))

        def scatter(p, b, c, re, im):
            put(p, b, c, product(*chirp(p, b, c), re, im))

        def enter(p, b, c, re, im):
            wj[rows_of(p, b), lanes(c)] = re
            wj[rows_of(p, b), lanes(2 + c)] = im
            put(p, b, c, product(re, im, *window(1, p, b, c)))

        def compare(p, b, c, re, im):
            misfit = re * re + im * im - mj[c, spread_rows(0, p, b), :]
            put(p, b, c, (re * misfit, im * misfit))

        def compare_all():
            for c in range(2):
                mj[c] = source[:, lanes(c)].astype(f32)
            each(compare)

        def leave(p, b, c, re, im):
            add(1, p, b, c, conjugate_product(wj[rows_of(p, b), lanes(c)], wj[rows_of(p, b), lanes(2 + c)], re, im))
            put(p, b, c, conjugate_product(*window(1, p, b, c), re, im))

        def gather(p, b, c, re, im):
            put(p, b, c, conjugate_product(*chirp(p, b, c), re, im))

        def finish(p, b, c, re, im):
            add(0, p, b, c, conjugate_product(*lit(p, b, c), re, im))

        points = [begin, lambda: each(scatter), lambda: each(enter), compare_all,
                  lambda: each(leave), lambda: each(gather), lambda: each(finish)]
        return points, transform

    def step(k, carry):
        a = 2 * k
        b = jnp.minimum(2 * k + 1, live - 1)
        valid = 2 * k + 1 < live
        fetch(a).wait()

        @pl.when(valid)
        def _():
            fetch(2 * k + 1).wait()

        for ahead in (2, 3):
            @pl.when(2 * k + ahead < live)
            def _():
                fetch(2 * k + ahead).start()

        first, first_transform = pattern(a, 0, None)
        second, second_transform = pattern(b, 1, valid)
        first[0]()
        for t in range(6):
            first_transform(t % 2 == 1)
            second[t]()
            second_transform(t % 2 == 1)
            first[t + 1]()
        second[6]()
        return carry

    for s in range(2):
        @pl.when(live > s)
        def _():
            fetch(s).start()
    lax.fori_loop(0, lax.div(live + 1, 2), step, 0)


def gradient(count, slot, row, col, field, images, probe):
    n = probe.shape[0]
    planes, cols, rows, width = field.shape
    return pl.pallas_call(
        grad_kernel,
        out_shape=jax.ShapeDtypeStruct((planes, cols, rows + n, width), f32),
        in_specs=[smem] * 4 + [vmem, anyspace] + [vmem] * 6,
        out_specs=vmem,
        scratch_shapes=[
            pltpu.VMEM((2, n, 2 * n), bf16),
            pltpu.VMEM((2, 2 * n, n), bf16),
            pltpu.VMEM((2, 2 * n, n), f32),
            pltpu.VMEM((2, n, 2 * n), f32),
            pltpu.VMEM((2, 2, n, width), f32),
            pltpu.VMEM((4, n, width), f32),
            pltpu.VMEM((4, n, n), bf16),
            pltpu.SemaphoreType.DMA((4,)),
        ],
        compiler_params=pltpu.CompilerParams(vmem_limit_bytes=VMEM_LIMIT),
        name="gradient",
    )(count, slot, row, col, field, images, probe, *make_tables(n))


def reduce_kernel(tiles, slabs, cores, total, out, part, near, far, outgoing,
                  localsem, csend, crecv, zsend, zrecv, fsend, frecv):
    tile = lax.axis_index("tile")
    slab = lax.axis_index("slab")
    levels = slabs // cores
    core = lax.rem(slab, cores)
    level = lax.div(slab, cores)
    other = level * cores + (1 - core)
    following = lax.rem(tile + 1, tiles)
    preceding = lax.rem(tile + tiles - 1, tiles)
    barrier = pltpu.get_barrier_semaphore()

    def greet(t, s):
        pl.semaphore_signal(barrier, inc=1, device_id={"tile": t, "slab": s}, device_id_type=MESH)

    greet(tile, other)
    for d in range(1, levels):
        greet(tile, lax.rem(level + d, levels) * cores + core)
    for d in range(levels):
        place = lax.rem(level + d, levels) * cores + core
        greet(following, place)
        greet(preceding, place)
    pl.semaphore_wait(barrier, 1 + levels - 1 + 2 * levels)

    def block(which, d):
        return which * levels + lax.rem(level + d, levels)

    order = [(1, 2), (1, 1), (1, 3), (0, 2), (0, 1), (0, 3), (1, 0), (0, 0)]
    swaps = []
    takes = []
    for k, (which, d) in enumerate(order):
        b = block(which, d)
        copy = pltpu.make_async_remote_copy(
            src_ref=total.at[:, :, b, 1 - core], dst_ref=near.at[k], send_sem=csend.at[k], recv_sem=crecv.at[k],
            device_id={"tile": tile, "slab": other}, device_id_type=MESH,
        )
        copy.start()
        swaps.append(copy)
        take = pltpu.make_async_copy(total.at[:, :, b, core], part.at[k], localsem.at[k])
        take.start()
        takes.append(take)
    sends = []
    for k, (which, d) in enumerate(order):
        takes[k].wait()
        swaps[k].wait_recv()
        if (which, d) == (0, 0):
            continue
        outgoing[k] = (part[k] + near[k]).astype(bf16)
        place = lax.rem(level + d, levels) * cores + core
        if which == 0:
            copy = pltpu.make_async_remote_copy(
                src_ref=outgoing.at[k], dst_ref=far.at[d - 1], send_sem=zsend.at[d - 1], recv_sem=zrecv.at[d - 1],
                device_id={"tile": tile, "slab": place}, device_id_type=MESH,
            )
        else:
            copy = pltpu.make_async_remote_copy(
                src_ref=outgoing.at[k], dst_ref=far.at[levels - 1 + d], send_sem=fsend.at[d], recv_sem=frecv.at[d],
                device_id={"tile": following, "slab": place}, device_id_type=MESH,
            )
        copy.start()
        sends.append(copy)
    for copy in sends:
        copy.wait()
    for copy in swaps:
        copy.wait_send()
    last = len(order) - 1
    for p in range(4):
        for h in range(3):
            value = part[last, p, h] + near[last, p, h]
            for k in range(2 * levels - 1):
                value = value + far[k, p, h].astype(f32)
            out[p // 2, p % 2, :, h * LANES:(h + 1) * LANES] = value


def reduce(total, tiles, slabs):
    cores = 2
    levels = slabs // cores
    planes, cols, rows, lanes = total.shape
    each = (rows - 256) // (2 * slabs)
    sem = pltpu.SemaphoreType.DMA
    count = 2 * levels
    total = total.reshape(planes, cols, rows // (cores * each), cores, each, lanes)
    return pl.pallas_call(
        functools.partial(reduce_kernel, tiles, slabs, cores),
        out_shape=jax.ShapeDtypeStruct((2, 2, each, cols * lanes), f32),
        in_specs=[anyspace],
        out_specs=vmem,
        scratch_shapes=[
            pltpu.VMEM((count, planes, cols, each, lanes), f32),
            pltpu.VMEM((count, planes, cols, each, lanes), f32),
            pltpu.VMEM((count - 1, planes, cols, each, lanes), bf16),
            pltpu.VMEM((count, planes, cols, each, lanes), bf16),
            sem((count,)),
            sem((count,)), sem((count,)),
            sem((levels - 1,)), sem((levels - 1,)),
            sem((levels,)), sem((levels,)),
        ],
        compiler_params=pltpu.CompilerParams(collective_id=1, has_side_effects=True, vmem_limit_bytes=VMEM_LIMIT),
        name="reduce",
    )(total)


def shards(intensities, object_field, probe_wave, owner_tile, row_offset, col_offset):
    tiles = lax.axis_size("tile")
    slabs = lax.axis_size("slab")
    packed, count, slot, row, col, shard = pack(
        owner_tile, row_offset, col_offset, intensities, object_field, tiles, slabs
    )
    images, field = exchange(packed, shard, tiles, slabs)
    total = gradient(count, slot, row, col, field, images, probe_wave)
    return reduce(total, tiles, slabs)


def solution(mesh):
    placed = (
        P(("tile", "slab"), None, None),
        P(None, None, ("tile", "slab"), None),
        P(),
        P(),
        P(),
        P(),
    )
    return jax.shard_map(
        shards,
        mesh=mesh,
        in_specs=placed,
        out_specs=P(None, None, ("tile", "slab"), None),
        check_vma=False,
    )
```

```python
import functools
import math

import jax
import jax.numpy as jnp
import numpy as np
from jax import lax
from jax.experimental import pallas as pl
from jax.experimental.pallas import tpu as pltpu
from jax.sharding import PartitionSpec as P

bf16 = jnp.bfloat16
f32 = jnp.float32
MESH = pl.DeviceIdType.MESH
K = 16
CAP = 2
COL_STEP = 128
CHIRP = 40.0
LANES = 128
HALF = 64
VMEM_LIMIT = 60 * 2**20

smem = pl.BlockSpec(memory_space=pltpu.SMEM)
vmem = pl.BlockSpec(memory_space=pltpu.VMEM)
anyspace = pl.BlockSpec(memory_space=pl.ANY)


def make_tables(n):
    count = np.arange(n)
    angles = ((count[:, None] * count[None, :]) % n).astype(np.float32)
    angles = angles * np.float32(2.0 * math.pi / n)
    scale = np.float32(1.0 / math.sqrt(n))
    c = (np.cos(angles) * scale).astype(np.float32)
    s = (np.sin(angles) * scale).astype(np.float32)
    forward = np.block([[c, -s], [s, c]])
    inverse = np.block([[c, s], [-s, c]])
    even = np.arange(0, n, 2)
    odd = even + 1
    low = np.concatenate([even[: n // 4], odd[: n // 4]])

    def left(sign, inputs):
        cc = c[np.ix_(low, inputs)]
        ss = s[np.ix_(low, inputs)] * np.float32(sign)
        return np.block([[cc, ss], [-ss, cc]])

    left_forward = np.stack([left(1, even), left(1, odd)])
    left_inverse = np.stack([left(-1, even), left(-1, odd)])
    f = (((count + n // 2) % n) - n // 2).astype(np.float32) / np.float32(n)
    phases = np.float32(CHIRP) * (f[:, None] ** 2 + f[None, :] ** 2)
    kernel = np.stack([np.cos(phases), -np.sin(phases)]).astype(np.float32)
    kernel = kernel[:, np.concatenate([even, odd]), :]

    def low_precision(a):
        return jnp.asarray(a.astype(np.float32), bf16)

    return (
        low_precision(forward), low_precision(inverse),
        low_precision(left_forward), low_precision(left_inverse), jnp.asarray(kernel),
    )


def pack_kernel(tiles, slabs, reads, owner, rowoff, coloff, images, field,
                packed, count, slot, row, col, shard, hold, used, insem, outsem):
    tile = lax.axis_index("tile")
    slab = lax.axis_index("slab")
    for k in range(reads):
        pltpu.make_async_copy(images.at[k], hold.at[k], insem.at[k]).start()
    for t in range(tiles):
        used[t] = 0
    for k in range(K + 1):
        slot[k] = 0
        row[k] = 0
        col[k] = 0
    for k in range(reads):
        dest = owner[(tile * slabs + slab) * reads + k]
        rank = used[dest]
        used[dest] = rank + 1
        pltpu.make_async_copy(images.at[k], hold.at[k], insem.at[k]).wait()
        pltpu.make_async_copy(hold.at[k], packed.at[dest, rank], outsem.at[k]).start()
    for s in range(2):
        for q in range(2):
            for h in range(3):
                shard[2 * s + q, h] = field[s, q, :, h * LANES:(h + 1) * LANES]

    def sender(i, found):
        base = (i * slabs + slab) * reads

        def one(k, state):
            n, rank = state
            hit = owner[base + k] == tile
            slot[n] = jnp.where(hit, i * CAP + rank, 0)
            row[n] = rowoff[base + k]
            col[n] = coloff[base + k]
            step = hit.astype(jnp.int32)
            return n + step, rank + step

        return lax.fori_loop(0, reads, one, (found, jnp.int32(0)), unroll=True)[0]

    count[0] = lax.fori_loop(0, tiles, sender, jnp.int32(0))
    for k in range(reads):
        pltpu.make_async_copy(hold.at[k], packed.at[0, 0], outsem.at[k]).wait()


def pack(owner, rowoff, coloff, images, field, tiles, slabs):
    reads, n, _ = images.shape
    rows = field.shape[2]
    return pl.pallas_call(
        functools.partial(pack_kernel, tiles, slabs, reads),
        out_shape=(
            jax.ShapeDtypeStruct((tiles, CAP, n, n), bf16),
            jax.ShapeDtypeStruct((1,), jnp.int32),
            jax.ShapeDtypeStruct((K + 1,), jnp.int32),
            jax.ShapeDtypeStruct((K + 1,), jnp.int32),
            jax.ShapeDtypeStruct((K + 1,), jnp.int32),
            jax.ShapeDtypeStruct((4, 3, rows, LANES), f32),
        ),
        in_specs=[smem, smem, smem, anyspace, vmem],
        out_specs=(anyspace, smem, smem, smem, smem, vmem),
        scratch_shapes=[
            pltpu.VMEM((reads, n, n), bf16),
            pltpu.SMEM((tiles,), jnp.int32),
            pltpu.SemaphoreType.DMA((reads,)),
            pltpu.SemaphoreType.DMA((reads,)),
        ],
        name="pack",
    )(owner, rowoff, coloff, images, field)


def product(ar, ai, br, bi):
    return ar * br - ai * bi, ar * bi + ai * br


def conjugate_product(ar, ai, br, bi):
    return ar * br + ai * bi, ar * bi - ai * br


def lanes(c):
    return slice(c * LANES, (c + 1) * LANES)


def rows_of(p, b):
    return slice(2 * HALF * p + HALF * b, 2 * HALF * p + HALF * b + HALF)


def spread_rows(start, p, b):
    return pl.ds(start + p + 2 * HALF * b, HALF, stride=2)


def window(field, s, top, left, p, b, c):
    where = spread_rows(top, p, b)
    return field[2 * s, left + c, where, :], field[2 * s + 1, left + c, where, :]


def put(x, p, b, c, parts):
    x[rows_of(p, b), lanes(c)] = parts[0].astype(bf16)
    x[rows_of(p, b), lanes(2 + c)] = parts[1].astype(bf16)


def chirp(kernel, p, b, c):
    return kernel[0, rows_of(p, b), lanes(c)], kernel[1, rows_of(p, b), lanes(c)]


def lit(probe, p, b, c):
    where = spread_rows(0, p, b)
    return probe[c, where, :], probe[2 + c, where, :]


def each(y, use):
    for p in range(2):
        for c in range(2):
            parts = [y[HALF * k:HALF * k + HALF, lanes(c)] for k in (p, 2 + p, 4 + p, 6 + p)]
            use(p, 0, c, parts[0] + parts[2], parts[1] + parts[3])
            use(p, 1, c, parts[0] - parts[2], parts[1] - parts[3])


def transform(x, h, y, right, left):
    n = 4 * HALF
    m = n // 2
    half = jnp.dot(x[...], right[...], preferred_element_type=f32)
    h[0:m, :] = half[:m, :n].astype(bf16)
    h[m:n, :] = half[:m, n:].astype(bf16)
    h[n:n + m, :] = half[m:, :n].astype(bf16)
    h[n + m:, :] = half[m:, n:].astype(bf16)
    y[:n, :] = jnp.dot(left[0], h[:n, :], preferred_element_type=f32)
    y[n:, :] = jnp.dot(left[1], h[n:, :], preferred_element_type=f32)


def interleave(first, second, transforms):
    first[0]()
    for t in range(transforms):
        first[2 * t + 1]()
        second[2 * t]()
        second[2 * t + 1]()
        first[2 * t + 2]()
    second[2 * transforms]()


XORDER = (1, 3, 2)
RELAY_STEPS = ((1, slice(3, 6)), (5, slice(6, 9)))
YORDER = (2, 1, 3)


def exchange_kernel(tiles, slabs, cores, rows, packed, shard, slot, row, col, probe_in, rf, ri, lf, li, kernel,
                    got, field_out, fars, waves,
                    field, probe, x, h, y, far, wave, hold, localsem, outsem,
                    stage, xsend, xrecv, ysend, yrecv, nsend, nrecv, zsend, zrecv, csend, crecv):
    tile = lax.axis_index("tile")
    slab = lax.axis_index("slab")
    levels = slabs // cores
    core = lax.rem(slab, cores)
    level = lax.div(slab, cores)
    other = level * cores + (1 - core)
    before = lax.rem(tile + tiles - 1, tiles)
    side = math.isqrt(tiles)
    barrier = pltpu.get_barrier_semaphore()

    def greet(t, s):
        pl.semaphore_signal(barrier, inc=1, device_id={"tile": t, "slab": s}, device_id_type=MESH)

    for d in range(1, tiles):
        greet(lax.rem(tile + d, tiles), slab)
    for d in range(1, levels):
        greet(tile, lax.rem(level + d, levels) * cores + core)
    greet(tile, other)
    pl.semaphore_wait(barrier, tiles + levels - 1)

    height = rows * slabs

    def block(which, s):
        return field.at[:, :, pl.ds(pl.multiple_of(which * height + s * rows, rows), rows), :]

    copies = []
    rims = []

    def make(src, dst, send, recv, t, s):
        copy = pltpu.make_async_remote_copy(
            src_ref=src, dst_ref=dst, send_sem=send, recv_sem=recv,
            device_id={"tile": t, "slab": s}, device_id_type=MESH,
        )
        copies.append(copy)
        return copy

    def push(*parts):
        copy = make(*parts)
        copy.start()
        return copy

    def share(which, src, k):
        mine = block(which, slab)
        links = []
        for d in (2, 1, 3)[: levels - 1]:
            place = lax.rem(level + d, levels) * cores + core
            links.append((d, push(src, mine, zsend.at[which, d - 1], zrecv.at[which, d - 1], tile, place)))
        rims.append(push(src, mine, csend.at[which, 0], crecv.at[which, 0], tile, other))
        return links

    def pass_on(which, links):
        for d, copy in links:
            copy.wait_recv()
            s = lax.rem(level + levels - d, levels) * cores + core
            rims.append(push(block(which, s), block(which, s), csend.at[which, d], crecv.at[which, d], tile, other))

    ahead = push(shard, block(1, slab), nsend, nrecv, before, slab)
    own = share(0, shard, 0)
    grid_row, grid_col = lax.div(tile, side), lax.rem(tile, side)

    def at(dy, dx):
        return lax.rem(grid_row + dy + side, side) * side + lax.rem(grid_col + dx + side, side)

    steps = XORDER
    for dy in YORDER:
        push(packed.at[at(dy, 0)], got.at[tile], ysend.at[0, dy - 1], yrecv.at[0, dy - 1], at(dy, 0), slab)
    relays = []
    for dy in YORDER:
        for dx in steps:
            copy = push(packed.at[at(dy, dx)], stage.at[dy - 1, dx - 1], xsend.at[dy, dx - 1], xrecv.at[dy, dx - 1], at(0, dx), slab)
            relays.append((dy, dx, copy))
    for dx in steps:
        push(packed.at[at(0, dx)], got.at[tile], xsend.at[0, dx - 1], xrecv.at[0, dx - 1], at(0, dx), slab)
    keep = pltpu.make_async_copy(shard, block(0, slab), localsem.at[0])
    keep.start()
    first = pltpu.make_async_copy(packed.at[tile], hold, localsem.at[1])
    first.start()
    first.wait()
    second = pltpu.make_async_copy(hold, got.at[tile], localsem.at[1])
    second.start()
    ahead.wait_recv()
    following = share(1, block(1, slab), 1)
    def relay(part):
        for (dy, dx, copy), onward in part:
            copy.wait_recv()
            onward.start()

    onwards = [
        make(stage.at[dy - 1, dx - 1], got.at[at(0, -dx)], ysend.at[dx, dy - 1], yrecv.at[dx, dy - 1], at(dy, 0), slab)
        for dy, dx, _ in relays
    ]
    relays = list(zip(relays, onwards))

    for g in range(4):
        probe[g] = probe_in[:, lanes(g)]
    pass_on(0, own)
    relay(relays[:3])
    pass_on(1, following)
    done = [id(c) for _, c in own + following] + [id(ahead)] + [id(r[2]) for r, _ in relays]
    for copy in rims:
        copy.wait_recv()
        done.append(id(copy))
    keep.wait()
    store = pltpu.make_async_copy(field, field_out, localsem.at[0])
    store.start()

    def outputs(k, j):
        turn = lax.rem(k, 2)
        return (
            pltpu.make_async_copy(far.at[turn, j], fars.at[2 * k + j], outsem.at[turn, j, 0]),
            pltpu.make_async_copy(wave.at[turn, j], waves.at[2 * k + j], outsem.at[turn, j, 1]),
        )

    def pattern(k, j):
        top = row[2 * k + j]
        left = col[2 * k + j]
        turn = lax.rem(k, 2)
        xj, hj, yj, fj, wj = x.at[j], h.at[j], y.at[j], far.at[turn, j], wave.at[turn, j]

        def begin():
            for p in range(2):
                for b in range(2):
                    for c in range(2):
                        put(xj, p, b, c, product(*lit(probe, p, b, c), *window(field, 0, top, left, p, b, c)))

        def scatter(p, b, c, re, im):
            put(xj, p, b, c, product(*chirp(kernel, p, b, c), re, im))

        def enter(p, b, c, re, im):
            wj[rows_of(p, b), lanes(c)] = re
            wj[rows_of(p, b), lanes(2 + c)] = im
            put(xj, p, b, c, product(re, im, *window(field, 1, top, left, p, b, c)))

        return [
            begin, lambda: transform(xj, hj, yj, rf, lf), lambda: each(yj, scatter),
            lambda: transform(xj, hj, yj, ri, li), lambda: each(yj, enter),
            lambda: transform(xj, hj, fj, rf, lf), lambda: None,
        ]

    def step(k, carry):
        @pl.when(k >= 2)
        def _():
            for j in range(2):
                for copy in outputs(k - 2, j):
                    copy.wait()

        interleave(pattern(k, 0), pattern(k, 1), 3)
        for j in range(2):
            for copy in outputs(k, j):
                copy.start()

        for when, part in RELAY_STEPS:
            @pl.when(k == when)
            def _():
                relay(relays[part])

        return carry

    pairs = K // 2
    lax.fori_loop(0, pairs, step, 0)
    for k in (pairs - 2, pairs - 1):
        for j in range(2):
            for copy in outputs(k, j):
                copy.wait()
    store.wait()
    second.wait()
    for copy in copies:
        copy.wait_send()
        if id(copy) not in done:
            copy.wait_recv()


def exchange(packed, shard, slot, row, col, probe, tables, tiles, slabs):
    _, _, n, _ = packed.shape
    planes, cols, rows, width = shard.shape
    cores = 2
    levels = slabs // cores
    side = math.isqrt(tiles)
    sem = pltpu.SemaphoreType.DMA
    extended = (planes, cols, 2 * rows * slabs, width)
    return pl.pallas_call(
        functools.partial(exchange_kernel, tiles, slabs, cores, rows),
        out_shape=(
            jax.ShapeDtypeStruct(packed.shape, packed.dtype),
            jax.ShapeDtypeStruct(extended, f32),
            jax.ShapeDtypeStruct((K, 2 * n, n), f32),
            jax.ShapeDtypeStruct((K, n, 2 * n), f32),
        ),
        in_specs=[anyspace, vmem, smem, smem, smem] + [vmem] * 6,
        out_specs=(anyspace,) * 4,
        scratch_shapes=[
            pltpu.VMEM(extended, f32),
            pltpu.VMEM((4, n, width), f32),
            pltpu.VMEM((2, n, 2 * n), bf16),
            pltpu.VMEM((2, 2 * n, n), bf16),
            pltpu.VMEM((2, 2 * n, n), f32),
            pltpu.VMEM((2, 2, 2 * n, n), f32),
            pltpu.VMEM((2, 2, n, 2 * n), f32),
            pltpu.VMEM((CAP, n, n), bf16),
            sem((2,)),
            sem((2, 2, 2)),
            pltpu.VMEM((side - 1, side - 1, CAP, n, n), bf16),
            sem((side, side - 1)), sem((side, side - 1)),
            sem((side, side - 1)), sem((side, side - 1)),
            sem, sem,
            sem((2, levels - 1)), sem((2, levels - 1)),
            sem((2, levels)), sem((2, levels)),
        ],
        compiler_params=pltpu.CompilerParams(collective_id=0, has_side_effects=True, vmem_limit_bytes=VMEM_LIMIT),
        name="exchange",
    )(packed, shard, slot, row, col, probe, *tables)


def grad_kernel(count, slot, row, col, field, images, fars, waves, probe_in, rf, ri, lf, li, kernel,
                total, x, h, y, far, wave, measured, probe, image, insem):
    dump = field.shape[2]
    total[...] = jnp.zeros_like(total)
    live = count[0]
    for g in range(4):
        probe[g] = probe_in[:, lanes(g)]

    def inputs(i):
        index = slot[i]
        place = lax.rem(i, 4)
        return (
            pltpu.make_async_copy(images.at[lax.div(index, CAP), lax.rem(index, CAP)], image.at[place], insem.at[place, 0]),
            pltpu.make_async_copy(fars.at[i], far.at[place], insem.at[place, 1]),
            pltpu.make_async_copy(waves.at[i], wave.at[place], insem.at[place, 2]),
        )

    def pattern(i, j, valid):
        top = row[i]
        left = col[i]
        place = top if valid is None else jnp.where(valid, top, dump)
        at = lax.rem(i, 4)
        xj, hj, yj, mj = x.at[j], h.at[j], y.at[j], measured.at[j]
        wj, fj, source = wave.at[at], far.at[at], image.at[at]

        def add(s, p, b, c, parts):
            where = spread_rows(place, p, b)
            total[2 * s, left + c, where, :] += parts[0]
            total[2 * s + 1, left + c, where, :] += parts[1]

        def compare(p, b, c, re, im):
            misfit = re * re + im * im - mj[c, spread_rows(0, p, b), :]
            put(xj, p, b, c, (re * misfit, im * misfit))

        def compare_all():
            for c in range(2):
                mj[c] = source[:, lanes(c)].astype(f32)
            each(fj, compare)

        def leave(p, b, c, re, im):
            add(1, p, b, c, conjugate_product(wj[rows_of(p, b), lanes(c)], wj[rows_of(p, b), lanes(2 + c)], re, im))
            put(xj, p, b, c, conjugate_product(*window(field, 1, top, left, p, b, c), re, im))

        def gather(p, b, c, re, im):
            put(xj, p, b, c, conjugate_product(*chirp(kernel, p, b, c), re, im))

        def finish(p, b, c, re, im):
            add(0, p, b, c, conjugate_product(*lit(probe, p, b, c), re, im))

        return [
            compare_all, lambda: transform(xj, hj, yj, ri, li), lambda: each(yj, leave),
            lambda: transform(xj, hj, yj, rf, lf), lambda: each(yj, gather),
            lambda: transform(xj, hj, yj, ri, li), lambda: each(yj, finish),
        ]

    def step(k, carry):
        a = 2 * k
        b = jnp.minimum(2 * k + 1, live - 1)
        valid = 2 * k + 1 < live
        for copy in inputs(a):
            copy.wait()

        @pl.when(valid)
        def _():
            for copy in inputs(2 * k + 1):
                copy.wait()

        for ahead in (2, 3):
            @pl.when(2 * k + ahead < live)
            def _():
                for copy in inputs(2 * k + ahead):
                    copy.start()

        interleave(pattern(a, 0, None), pattern(b, 1, valid), 3)
        return carry

    for s in range(2):
        @pl.when(live > s)
        def _():
            for copy in inputs(s):
                copy.start()
    lax.fori_loop(0, lax.div(live + 1, 2), step, 0)


def gradient(count, slot, row, col, field, images, fars, waves, probe, tables):
    n = probe.shape[0]
    planes, cols, rows, width = field.shape
    return pl.pallas_call(
        grad_kernel,
        out_shape=jax.ShapeDtypeStruct((planes, cols, rows + n, width), f32),
        in_specs=[smem] * 4 + [vmem] + [anyspace] * 3 + [vmem] * 6,
        out_specs=vmem,
        scratch_shapes=[
            pltpu.VMEM((2, n, 2 * n), bf16),
            pltpu.VMEM((2, 2 * n, n), bf16),
            pltpu.VMEM((2, 2 * n, n), f32),
            pltpu.VMEM((4, 2 * n, n), f32),
            pltpu.VMEM((4, n, 2 * n), f32),
            pltpu.VMEM((2, 2, n, width), f32),
            pltpu.VMEM((4, n, width), f32),
            pltpu.VMEM((4, n, n), bf16),
            pltpu.SemaphoreType.DMA((4, 3)),
        ],
        compiler_params=pltpu.CompilerParams(vmem_limit_bytes=VMEM_LIMIT),
        name="gradient",
    )(count, slot, row, col, field, images, fars, waves, probe, *tables)


def reduce_kernel(tiles, slabs, cores, total, out, part, near, far, outgoing,
                  localsem, csend, crecv, zsend, zrecv, fsend, frecv):
    tile = lax.axis_index("tile")
    slab = lax.axis_index("slab")
    levels = slabs // cores
    core = lax.rem(slab, cores)
    level = lax.div(slab, cores)
    other = level * cores + (1 - core)
    following = lax.rem(tile + 1, tiles)
    preceding = lax.rem(tile + tiles - 1, tiles)
    barrier = pltpu.get_barrier_semaphore()

    def greet(t, s):
        pl.semaphore_signal(barrier, inc=1, device_id={"tile": t, "slab": s}, device_id_type=MESH)

    greet(tile, other)
    for d in range(1, levels):
        greet(tile, lax.rem(level + d, levels) * cores + core)
    for d in range(levels):
        place = lax.rem(level + d, levels) * cores + core
        greet(following, place)
        greet(preceding, place)
    pl.semaphore_wait(barrier, 1 + levels - 1 + 2 * levels)

    def block(which, d):
        return which * levels + lax.rem(level + d, levels)

    order = [(1, 2), (1, 1), (1, 3), (0, 2), (0, 1), (0, 3), (1, 0), (0, 0)]
    swaps = []
    takes = []
    for k, (which, d) in enumerate(order):
        b = block(which, d)
        copy = pltpu.make_async_remote_copy(
            src_ref=total.at[:, :, b, 1 - core], dst_ref=near.at[k], send_sem=csend.at[k], recv_sem=crecv.at[k],
            device_id={"tile": tile, "slab": other}, device_id_type=MESH,
        )
        copy.start()
        swaps.append(copy)
        take = pltpu.make_async_copy(total.at[:, :, b, core], part.at[k], localsem.at[k])
        take.start()
        takes.append(take)
    sends = []
    for k, (which, d) in enumerate(order):
        takes[k].wait()
        swaps[k].wait_recv()
        if (which, d) == (0, 0):
            continue
        outgoing[k] = (part[k] + near[k]).astype(bf16)
        place = lax.rem(level + d, levels) * cores + core
        if which == 0:
            copy = pltpu.make_async_remote_copy(
                src_ref=outgoing.at[k], dst_ref=far.at[d - 1], send_sem=zsend.at[d - 1], recv_sem=zrecv.at[d - 1],
                device_id={"tile": tile, "slab": place}, device_id_type=MESH,
            )
        else:
            copy = pltpu.make_async_remote_copy(
                src_ref=outgoing.at[k], dst_ref=far.at[levels - 1 + d], send_sem=fsend.at[d], recv_sem=frecv.at[d],
                device_id={"tile": following, "slab": place}, device_id_type=MESH,
            )
        copy.start()
        sends.append(copy)
    for copy in sends:
        copy.wait()
    for copy in swaps:
        copy.wait_send()
    last = len(order) - 1
    for p in range(4):
        for h in range(3):
            value = part[last, p, h] + near[last, p, h]
            for k in range(2 * levels - 1):
                value = value + far[k, p, h].astype(f32)
            out[p // 2, p % 2, :, h * LANES:(h + 1) * LANES] = value


def reduce(total, tiles, slabs):
    cores = 2
    levels = slabs // cores
    planes, cols, rows, lanes = total.shape
    each = (rows - 256) // (2 * slabs)
    sem = pltpu.SemaphoreType.DMA
    count = 2 * levels
    total = total.reshape(planes, cols, rows // (cores * each), cores, each, lanes)
    return pl.pallas_call(
        functools.partial(reduce_kernel, tiles, slabs, cores),
        out_shape=jax.ShapeDtypeStruct((2, 2, each, cols * lanes), f32),
        in_specs=[anyspace],
        out_specs=vmem,
        scratch_shapes=[
            pltpu.VMEM((count, planes, cols, each, lanes), f32),
            pltpu.VMEM((count, planes, cols, each, lanes), f32),
            pltpu.VMEM((count - 1, planes, cols, each, lanes), bf16),
            pltpu.VMEM((count, planes, cols, each, lanes), bf16),
            sem((count,)),
            sem((count,)), sem((count,)),
            sem((levels - 1,)), sem((levels - 1,)),
            sem((levels,)), sem((levels,)),
        ],
        compiler_params=pltpu.CompilerParams(collective_id=1, has_side_effects=True, vmem_limit_bytes=VMEM_LIMIT),
        name="reduce",
    )(total)


def shards(intensities, object_field, probe_wave, owner_tile, row_offset, col_offset):
    tiles = lax.axis_size("tile")
    slabs = lax.axis_size("slab")
    packed, count, slot, row, col, shard = pack(
        owner_tile, row_offset, col_offset, intensities, object_field, tiles, slabs
    )
    tables = make_tables(intensities.shape[1])
    images, field, fars, waves = exchange(packed, shard, slot, row, col, probe_wave, tables, tiles, slabs)
    total = gradient(count, slot, row, col, field, images, fars, waves, probe_wave, tables)
    return reduce(total, tiles, slabs)


def solution(mesh):
    placed = (
        P(("tile", "slab"), None, None),
        P(None, None, ("tile", "slab"), None),
        P(),
        P(),
        P(),
        P(),
    )
    return jax.shard_map(
        shards,
        mesh=mesh,
        in_specs=placed,
        out_specs=P(None, None, ("tile", "slab"), None),
        check_vma=False,
    )
```

```python
import functools
import math

import jax
import jax.numpy as jnp
import numpy as np
from jax import lax
from jax.experimental import pallas as pl
from jax.experimental.pallas import tpu as pltpu
from jax.sharding import PartitionSpec as P

bf16 = jnp.bfloat16
f32 = jnp.float32
MESH = pl.DeviceIdType.MESH
K = 16
CAP = 2
COL_STEP = 128
CHIRP = 40.0
LANES = 128
HALF = 64
CHUNK = 32
VMEM_LIMIT = 60 * 2**20

smem = pl.BlockSpec(memory_space=pltpu.SMEM)
vmem = pl.BlockSpec(memory_space=pltpu.VMEM)
anyspace = pl.BlockSpec(memory_space=pl.ANY)


def make_tables(n):
    count = np.arange(n)
    angles = ((count[:, None] * count[None, :]) % n).astype(np.float32)
    angles = angles * np.float32(2.0 * math.pi / n)
    scale = np.float32(1.0 / math.sqrt(n))
    c = (np.cos(angles) * scale).astype(np.float32)
    s = (np.sin(angles) * scale).astype(np.float32)
    even = np.arange(0, n, 2)
    odd = even + 1
    low = np.concatenate([even[: n // 4], odd[: n // 4]])
    near = np.arange(n // 2)

    def left(sign, inputs):
        cc = c[np.ix_(low, inputs)]
        ss = s[np.ix_(low, inputs)] * np.float32(sign)
        return np.block([[cc, ss], [-ss, cc]])

    def right(sign, inputs, outputs):
        cc = c[np.ix_(inputs, outputs)]
        ss = s[np.ix_(inputs, outputs)] * np.float32(sign)
        return np.block([[cc, -ss], [ss, cc]])

    f = (((count + n // 2) % n) - n // 2).astype(np.float32) / np.float32(n)
    phases = np.float32(CHIRP) * (f[:, None] ** 2 + f[None, :] ** 2)
    kernel = np.stack([np.cos(phases), -np.sin(phases)]).astype(np.float32)
    kernel = kernel[:, np.concatenate([even, odd]), :][:, :, np.concatenate([low, low + n // 2])]

    def low_precision(a):
        return jnp.asarray(a.astype(np.float32), bf16)

    return dict(
        left_forward=low_precision(np.stack([left(1, even), left(1, odd)])),
        left_inverse=low_precision(np.stack([left(-1, even), left(-1, odd)])),
        right_forward=low_precision(np.stack([right(1, even, low), right(1, odd, low)])),
        right_inverse=low_precision(np.stack([right(-1, even, low), right(-1, odd, low)])),
        right_far=low_precision(np.stack([right(1, even, near), right(1, odd, near)])),
        right_back=low_precision(np.concatenate([right(-1, count, low), right(-1, count, low + n // 2)], 1)),
        kernel=jnp.asarray(kernel),
    )


def lane_order():
    order = np.concatenate([np.arange(0, LANES, 2), np.arange(1, LANES, 2)])
    return jnp.asarray(order[None, :] == np.arange(LANES)[:, None], bf16)


def rearrange(value, order):
    high = value.astype(bf16)
    rest = value - high.astype(f32)
    middle = rest.astype(bf16)
    low = (rest - middle.astype(f32)).astype(bf16)
    parts = [jnp.dot(part, order, preferred_element_type=f32) for part in (high, middle, low)]
    return parts[0] + (parts[1] + parts[2])


def pack_kernel(tiles, slabs, reads, owner, rowoff, coloff, images, field, light, order,
                packed, count, slot, row, col, shard, probe, hold, used, insem, outsem):
    tile = lax.axis_index("tile")
    slab = lax.axis_index("slab")
    for k in range(reads):
        pltpu.make_async_copy(images.at[k], hold.at[k], insem.at[k]).start()
    for t in range(tiles):
        used[t] = 0
    for k in range(K + 1):
        slot[k] = 0
        row[k] = 0
        col[k] = 0
    for k in range(reads):
        dest = owner[(tile * slabs + slab) * reads + k]
        rank = used[dest]
        used[dest] = rank + 1
        pltpu.make_async_copy(images.at[k], hold.at[k], insem.at[k]).wait()
        pltpu.make_async_copy(hold.at[k], packed.at[dest, rank], outsem.at[k]).start()
    for s in range(2):
        for q in range(2):
            for h in range(3):
                shard[2 * s + q, h] = rearrange(field[s, q, :, lanes(h)], order[...])
    for g in range(4):
        probe[g] = rearrange(light[:, lanes(g)], order[...])

    def sender(i, found):
        base = (i * slabs + slab) * reads

        def one(k, state):
            n, rank = state
            hit = owner[base + k] == tile
            slot[n] = jnp.where(hit, i * CAP + rank, 0)
            row[n] = rowoff[base + k]
            col[n] = coloff[base + k]
            step = hit.astype(jnp.int32)
            return n + step, rank + step

        return lax.fori_loop(0, reads, one, (found, jnp.int32(0)), unroll=True)[0]

    count[0] = lax.fori_loop(0, tiles, sender, jnp.int32(0))
    for k in range(reads):
        pltpu.make_async_copy(hold.at[k], packed.at[0, 0], outsem.at[k]).wait()


def pack(owner, rowoff, coloff, images, field, light, tiles, slabs):
    reads, n, _ = images.shape
    rows = field.shape[2]
    return pl.pallas_call(
        functools.partial(pack_kernel, tiles, slabs, reads),
        out_shape=(
            jax.ShapeDtypeStruct((tiles, CAP, n, n), bf16),
            jax.ShapeDtypeStruct((1,), jnp.int32),
            jax.ShapeDtypeStruct((K + 1,), jnp.int32),
            jax.ShapeDtypeStruct((K + 1,), jnp.int32),
            jax.ShapeDtypeStruct((K + 1,), jnp.int32),
            jax.ShapeDtypeStruct((4, 3, rows, LANES), f32),
            jax.ShapeDtypeStruct((4, n, LANES), f32),
        ),
        in_specs=[smem, smem, smem, anyspace, vmem, vmem, vmem],
        out_specs=(anyspace, smem, smem, smem, smem, vmem, vmem),
        scratch_shapes=[
            pltpu.VMEM((reads, n, n), bf16),
            pltpu.SMEM((tiles,), jnp.int32),
            pltpu.SemaphoreType.DMA((reads,)),
            pltpu.SemaphoreType.DMA((reads,)),
        ],
        name="pack",
    )(owner, rowoff, coloff, images, field, light, lane_order())


def product(ar, ai, br, bi):
    return ar * br - ai * bi, ar * bi + ai * br


def conjugate_product(ar, ai, br, bi):
    return ar * br + ai * bi, ar * bi - ai * br


def lanes(c):
    return slice(c * LANES, (c + 1) * LANES)


def rows_of(p, b, r):
    start = 2 * HALF * p + HALF * b + r
    return slice(start, start + CHUNK)


def spread_rows(start, p, b, r):
    return pl.ds(start + p + 2 * HALF * b + 2 * r, CHUNK, stride=2)


def window(field, s, top, left, p, b, r, c):
    where = spread_rows(top, p, b, r)
    return field[2 * s, left + c, where, :], field[2 * s + 1, left + c, where, :]


def put_natural(x, p, b, r, parts):
    for c in range(2):
        for q in range(2):
            x[rows_of(p, b, r), lanes(2 * q + c)] = parts[c][q].astype(bf16)


def put(x, p, b, r, parts):
    low = lax.broadcasted_iota(jnp.int32, (CHUNK, LANES), 1) < HALF
    for q in range(2):
        near, far = parts[0][q], parts[1][q]
        even = jnp.where(low, near, pltpu.roll(far, HALF, 1))
        odd = jnp.where(low, pltpu.roll(near, HALF, 1), far)
        x[0, rows_of(p, b, r), lanes(q)] = even.astype(bf16)
        x[1, rows_of(p, b, r), lanes(q)] = odd.astype(bf16)


def chirp(kernel, p, b, r, c):
    return kernel[0, rows_of(p, b, r), lanes(c)], kernel[1, rows_of(p, b, r), lanes(c)]


def lit(probe, p, b, r, c):
    where = spread_rows(0, p, b, r)
    return probe[c, where, :], probe[2 + c, where, :]


def each(y, use):
    for p in range(2):
        for r in range(0, HALF, CHUNK):
            e = [[y[HALF * k + r:HALF * k + r + CHUNK, lanes(c)] for k in (p, 2 + p)] for c in range(2)]
            o = [[y[HALF * k + r:HALF * k + r + CHUNK, lanes(c)] for k in (4 + p, 6 + p)] for c in range(2)]
            use(p, 0, r, [(e[c][0] + o[c][0], e[c][1] + o[c][1]) for c in range(2)])
            use(p, 1, r, [(e[c][0] - o[c][0], e[c][1] - o[c][1]) for c in range(2)])


def finish_transform(h, y, low, high, left):
    n = 4 * HALF
    m = n // 2
    for p in range(2):
        for q in range(2):
            where = slice(p * n + q * m, p * n + q * m + m)
            h[where, lanes(0)] = low[p * m:p * m + m, lanes(q)].astype(bf16)
            h[where, lanes(1)] = high[p * m:p * m + m, lanes(q)].astype(bf16)
    y[:n, :] = jnp.dot(left[0], h[:n, :], preferred_element_type=f32)
    y[n:, :] = jnp.dot(left[1], h[n:, :], preferred_element_type=f32)


def transform(x, h, y, right, left):
    even = jnp.dot(x[0], right[0], preferred_element_type=f32)
    odd = jnp.dot(x[1], right[1], preferred_element_type=f32)
    finish_transform(h, y, even + odd, even - odd, left)


def transform_natural(x, h, y, right, left):
    n = 4 * HALF
    half = jnp.dot(x[...], right[...], preferred_element_type=f32)
    finish_transform(h, y, half[:, :n], half[:, n:], left)


def interleave(first, second, transforms):
    first[0]()
    for t in range(transforms):
        first[2 * t + 1]()
        second[2 * t]()
        second[2 * t + 1]()
        first[2 * t + 2]()
    second[2 * transforms]()


XORDER = (1, 3, 2)
RELAY_STEPS = ((1, slice(3, 5)), (2, slice(5, 6)), (3, slice(6, 7)), (4, slice(7, 8)), (5, slice(8, 9)))
YORDER = (2, 1, 3)


def exchange_kernel(tiles, slabs, cores, rows, packed, shard, slot, row, col, probe, right_forward, right_inverse, right_far, left_forward, left_inverse, kernel,
                    got, field_out, fars, waves,
                    field, x, h, y, far, wave, hold, localsem, outsem,
                    stage, xsend, xrecv, ysend, yrecv, nsend, nrecv, zsend, zrecv, csend, crecv):
    tile = lax.axis_index("tile")
    slab = lax.axis_index("slab")
    levels = slabs // cores
    core = lax.rem(slab, cores)
    level = lax.div(slab, cores)
    other = level * cores + (1 - core)
    before = lax.rem(tile + tiles - 1, tiles)
    side = math.isqrt(tiles)
    barrier = pltpu.get_barrier_semaphore()

    def greet(t, s):
        pl.semaphore_signal(barrier, inc=1, device_id={"tile": t, "slab": s}, device_id_type=MESH)

    for d in range(1, tiles):
        greet(lax.rem(tile + d, tiles), slab)
    for d in range(1, levels):
        greet(tile, lax.rem(level + d, levels) * cores + core)
    greet(tile, other)
    pl.semaphore_wait(barrier, tiles + levels - 1)

    height = rows * slabs

    def block(which, s):
        return field.at[:, :, pl.ds(pl.multiple_of(which * height + s * rows, rows), rows), :]

    copies = []
    rims = []

    def make(src, dst, send, recv, t, s):
        copy = pltpu.make_async_remote_copy(
            src_ref=src, dst_ref=dst, send_sem=send, recv_sem=recv,
            device_id={"tile": t, "slab": s}, device_id_type=MESH,
        )
        copies.append(copy)
        return copy

    def push(*parts):
        copy = make(*parts)
        copy.start()
        return copy

    def share(which, src, k):
        mine = block(which, slab)
        links = []
        for d in (2, 1, 3)[: levels - 1]:
            place = lax.rem(level + d, levels) * cores + core
            links.append((d, push(src, mine, zsend.at[which, d - 1], zrecv.at[which, d - 1], tile, place)))
        rims.append(push(src, mine, csend.at[which, 0], crecv.at[which, 0], tile, other))
        return links

    def pass_on(which, links):
        for d, copy in links:
            copy.wait_recv()
            s = lax.rem(level + levels - d, levels) * cores + core
            rims.append(push(block(which, s), block(which, s), csend.at[which, d], crecv.at[which, d], tile, other))

    ahead = push(shard, block(1, slab), nsend, nrecv, before, slab)
    own = share(0, shard, 0)
    grid_row, grid_col = lax.div(tile, side), lax.rem(tile, side)

    def at(dy, dx):
        return lax.rem(grid_row + dy + side, side) * side + lax.rem(grid_col + dx + side, side)

    steps = XORDER
    for dy in YORDER:
        push(packed.at[at(dy, 0)], got.at[tile], ysend.at[0, dy - 1], yrecv.at[0, dy - 1], at(dy, 0), slab)
    relays = []
    for dy in YORDER:
        for dx in steps:
            copy = push(packed.at[at(dy, dx)], stage.at[dy - 1, dx - 1], xsend.at[dy, dx - 1], xrecv.at[dy, dx - 1], at(0, dx), slab)
            relays.append((dy, dx, copy))
    for dx in steps:
        push(packed.at[at(0, dx)], got.at[tile], xsend.at[0, dx - 1], xrecv.at[0, dx - 1], at(0, dx), slab)
    keep = pltpu.make_async_copy(shard, block(0, slab), localsem.at[0])
    keep.start()
    first = pltpu.make_async_copy(packed.at[tile], hold, localsem.at[1])
    first.start()
    first.wait()
    second = pltpu.make_async_copy(hold, got.at[tile], localsem.at[1])
    second.start()
    ahead.wait_recv()
    following = share(1, block(1, slab), 1)
    def relay(part):
        for (dy, dx, copy), onward in part:
            copy.wait_recv()
            onward.start()

    onwards = [
        make(stage.at[dy - 1, dx - 1], got.at[at(0, -dx)], ysend.at[dx, dy - 1], yrecv.at[dx, dy - 1], at(dy, 0), slab)
        for dy, dx, _ in relays
    ]
    relays = list(zip(relays, onwards))

    pass_on(0, own)
    relay(relays[:3])
    pass_on(1, following)
    done = [id(c) for _, c in own + following] + [id(ahead)] + [id(r[2]) for r, _ in relays]
    for copy in rims:
        copy.wait_recv()
        done.append(id(copy))
    keep.wait()
    store = pltpu.make_async_copy(field, field_out, localsem.at[0])
    store.start()

    def outputs(k, j):
        turn = lax.rem(k, 2)
        return (
            pltpu.make_async_copy(far.at[turn, j], fars.at[2 * k + j], outsem.at[turn, j, 0]),
            pltpu.make_async_copy(wave.at[turn, j], waves.at[2 * k + j], outsem.at[turn, j, 1]),
        )

    def pattern(k, j):
        top = row[2 * k + j]
        left = col[2 * k + j]
        turn = lax.rem(k, 2)
        xj, hj, yj, fj, wj = x.at[j], h.at[j], y.at[j], far.at[turn, j], wave.at[turn, j]

        def begin():
            for p in range(2):
                for b in range(2):
                    for r in range(0, HALF, CHUNK):
                        put(xj, p, b, r, [
                            product(*lit(probe, p, b, r, c), *window(field, 0, top, left, p, b, r, c)) for c in range(2)
                        ])

        def scatter(p, b, r, parts):
            put(xj, p, b, r, [product(*chirp(kernel, p, b, r, c), *parts[c]) for c in range(2)])

        def enter(p, b, r, parts):
            for c in range(2):
                wj[rows_of(p, b, r), lanes(c)] = parts[c][0]
                wj[rows_of(p, b, r), lanes(2 + c)] = parts[c][1]
            put(xj, p, b, r, [product(*parts[c], *window(field, 1, top, left, p, b, r, c)) for c in range(2)])

        return [
            begin, lambda: transform(xj, hj, yj, right_forward, left_forward), lambda: each(yj, scatter),
            lambda: transform(xj, hj, yj, right_inverse, left_inverse), lambda: each(yj, enter),
            lambda: transform(xj, hj, fj, right_far, left_forward), lambda: None,
        ]

    def step(k, carry):
        @pl.when(k >= 2)
        def _():
            for j in range(2):
                for copy in outputs(k - 2, j):
                    copy.wait()

        interleave(pattern(k, 0), pattern(k, 1), 3)
        for j in range(2):
            for copy in outputs(k, j):
                copy.start()

        for when, part in RELAY_STEPS:
            @pl.when(k == when)
            def _():
                relay(relays[part])

        return carry

    pairs = K // 2
    lax.fori_loop(0, pairs, step, 0)
    for k in (pairs - 2, pairs - 1):
        for j in range(2):
            for copy in outputs(k, j):
                copy.wait()
    store.wait()
    second.wait()
    for copy in copies:
        copy.wait_send()
        if id(copy) not in done:
            copy.wait_recv()


def exchange(packed, shard, slot, row, col, probe, tables, tiles, slabs):
    n = packed.shape[2]
    planes, cols, rows, width = shard.shape
    cores = 2
    levels = slabs // cores
    side = math.isqrt(tiles)
    sem = pltpu.SemaphoreType.DMA
    extended = (planes, cols, 2 * rows * slabs, width)
    return pl.pallas_call(
        functools.partial(exchange_kernel, tiles, slabs, cores, rows),
        out_shape=(
            jax.ShapeDtypeStruct(packed.shape, packed.dtype),
            jax.ShapeDtypeStruct(extended, f32),
            jax.ShapeDtypeStruct((K, 2 * n, n), f32),
            jax.ShapeDtypeStruct((K, n, 2 * n), f32),
        ),
        in_specs=[anyspace, vmem, smem, smem, smem] + [vmem] * 7,
        out_specs=(anyspace,) * 4,
        scratch_shapes=[
            pltpu.VMEM(extended, f32),
            pltpu.VMEM((2, 2, n, n), bf16),
            pltpu.VMEM((2, 2 * n, n), bf16),
            pltpu.VMEM((2, 2 * n, n), f32),
            pltpu.VMEM((2, 2, 2 * n, n), f32),
            pltpu.VMEM((2, 2, n, 2 * n), f32),
            pltpu.VMEM((CAP, n, n), bf16),
            sem((2,)),
            sem((2, 2, 2)),
            pltpu.VMEM((side - 1, side - 1, CAP, n, n), bf16),
            sem((side, side - 1)), sem((side, side - 1)),
            sem((side, side - 1)), sem((side, side - 1)),
            sem, sem,
            sem((2, levels - 1)), sem((2, levels - 1)),
            sem((2, levels)), sem((2, levels)),
        ],
        compiler_params=pltpu.CompilerParams(collective_id=0, has_side_effects=True, vmem_limit_bytes=VMEM_LIMIT),
        name="exchange",
    )(
        packed, shard, slot, row, col, probe, tables["right_forward"], tables["right_inverse"], tables["right_far"],
        tables["left_forward"], tables["left_inverse"], tables["kernel"],
    )


def grad_kernel(count, slot, row, col, field, images, fars, waves, probe, right_forward, right_inverse, right_back, left_forward, left_inverse, kernel,
                out, total, x, xfull, h, y, far, wave, measured, image, insem, outsem):
    dump = field.shape[2]
    total[...] = jnp.zeros_like(total)
    live = count[0]

    def inputs(i):
        index = slot[i]
        place = lax.rem(i, 4)
        return (
            pltpu.make_async_copy(images.at[lax.div(index, CAP), lax.rem(index, CAP)], image.at[place], insem.at[place, 0]),
            pltpu.make_async_copy(fars.at[i], far.at[place], insem.at[place, 1]),
            pltpu.make_async_copy(waves.at[i], wave.at[place], insem.at[place, 2]),
        )

    def pattern(i, j, valid):
        top = row[i]
        left = col[i]
        place = top if valid is None else jnp.where(valid, top, dump)
        at = lax.rem(i, 4)
        xf = xfull.at[j]
        xj, hj, yj, mj = x.at[j], h.at[j], y.at[j], measured.at[j]
        wj, fj, source = wave.at[at], far.at[at], image.at[at]

        def add(s, p, b, r, parts):
            where = spread_rows(place, p, b, r)
            for c in range(2):
                total[2 * s, left + c, where, :] += parts[c][0]
                total[2 * s + 1, left + c, where, :] += parts[c][1]

        def compare(p, b, r, parts):
            scaled = []
            for c in range(2):
                re, im = parts[c]
                misfit = re * re + im * im - mj[c, spread_rows(0, p, b, r), :]
                scaled.append((re * misfit, im * misfit))
            put_natural(xf, p, b, r, scaled)

        def compare_all():
            for c in range(2):
                mj[c] = source[:, lanes(c)].astype(f32)
            each(fj, compare)

        def leave(p, b, r, parts):
            where = rows_of(p, b, r)
            add(1, p, b, r, [conjugate_product(wj[where, lanes(c)], wj[where, lanes(2 + c)], *parts[c]) for c in range(2)])
            put(xj, p, b, r, [conjugate_product(*window(field, 1, top, left, p, b, r, c), *parts[c]) for c in range(2)])

        def gather(p, b, r, parts):
            put(xj, p, b, r, [conjugate_product(*chirp(kernel, p, b, r, c), *parts[c]) for c in range(2)])

        def finish(p, b, r, parts):
            add(0, p, b, r, [conjugate_product(*lit(probe, p, b, r, c), *parts[c]) for c in range(2)])

        return [
            compare_all, lambda: transform_natural(xf, hj, yj, right_back, left_inverse), lambda: each(yj, leave),
            lambda: transform(xj, hj, yj, right_forward, left_forward), lambda: each(yj, gather),
            lambda: transform(xj, hj, yj, right_inverse, left_inverse), lambda: each(yj, finish),
        ]

    def step(k, carry):
        a = 2 * k
        b = jnp.minimum(2 * k + 1, live - 1)
        valid = 2 * k + 1 < live
        for copy in inputs(a):
            copy.wait()

        @pl.when(valid)
        def _():
            for copy in inputs(2 * k + 1):
                copy.wait()

        for ahead in (2, 3):
            @pl.when(2 * k + ahead < live)
            def _():
                for copy in inputs(2 * k + ahead):
                    copy.start()

        interleave(pattern(a, 0, None), pattern(b, 1, valid), 3)
        return carry

    for s in range(2):
        @pl.when(live > s)
        def _():
            for copy in inputs(s):
                copy.start()
    lax.fori_loop(0, lax.div(live + 1, 2), step, 0)
    store = pltpu.make_async_copy(total.at[:, :, :dump], out, outsem)
    store.start()
    store.wait()


def gradient(count, slot, row, col, field, images, fars, waves, probe, tables):
    planes, cols, rows, width = field.shape
    n = probe.shape[1]
    return pl.pallas_call(
        grad_kernel,
        out_shape=jax.ShapeDtypeStruct(field.shape, f32),
        in_specs=[smem] * 4 + [vmem] + [anyspace] * 3 + [vmem] * 7,
        out_specs=anyspace,
        scratch_shapes=[
            pltpu.VMEM((planes, cols, rows + n, width), f32),
            pltpu.VMEM((2, 2, n, n), bf16),
            pltpu.VMEM((2, n, 2 * n), bf16),
            pltpu.VMEM((2, 2 * n, n), bf16),
            pltpu.VMEM((2, 2 * n, n), f32),
            pltpu.VMEM((4, 2 * n, n), f32),
            pltpu.VMEM((4, n, 2 * n), f32),
            pltpu.VMEM((2, 2, n, width), f32),
            pltpu.VMEM((4, n, n), bf16),
            pltpu.SemaphoreType.DMA((4, 3)),
            pltpu.SemaphoreType.DMA,
        ],
        compiler_params=pltpu.CompilerParams(vmem_limit_bytes=VMEM_LIMIT),
        name="gradient",
    )(
        count, slot, row, col, field, images, fars, waves, probe, tables["right_forward"], tables["right_inverse"],
        tables["right_back"], tables["left_forward"], tables["left_inverse"], tables["kernel"],
    )


def reduce_kernel(tiles, slabs, cores, total, unsort, out, part, near, far, outgoing,
                  localsem, csend, crecv, zsend, zrecv, fsend, frecv):
    tile = lax.axis_index("tile")
    slab = lax.axis_index("slab")
    levels = slabs // cores
    core = lax.rem(slab, cores)
    level = lax.div(slab, cores)
    other = level * cores + (1 - core)
    following = lax.rem(tile + 1, tiles)
    preceding = lax.rem(tile + tiles - 1, tiles)
    barrier = pltpu.get_barrier_semaphore()

    def greet(t, s):
        pl.semaphore_signal(barrier, inc=1, device_id={"tile": t, "slab": s}, device_id_type=MESH)

    greet(tile, other)
    for d in range(1, levels):
        greet(tile, lax.rem(level + d, levels) * cores + core)
    for d in range(levels):
        place = lax.rem(level + d, levels) * cores + core
        greet(following, place)
        greet(preceding, place)
    pl.semaphore_wait(barrier, 1 + levels - 1 + 2 * levels)

    def block(which, d):
        return which * levels + lax.rem(level + d, levels)

    order = [(1, 2), (1, 1), (1, 3), (0, 2), (0, 1), (0, 3), (1, 0), (0, 0)]
    swaps = []
    takes = []
    for k, (which, d) in enumerate(order):
        b = block(which, d)
        copy = pltpu.make_async_remote_copy(
            src_ref=total.at[:, :, b, 1 - core], dst_ref=near.at[k], send_sem=csend.at[k], recv_sem=crecv.at[k],
            device_id={"tile": tile, "slab": other}, device_id_type=MESH,
        )
        copy.start()
        swaps.append(copy)
        take = pltpu.make_async_copy(total.at[:, :, b, core], part.at[k], localsem.at[k])
        take.start()
        takes.append(take)
    sends = []
    for k, (which, d) in enumerate(order):
        takes[k].wait()
        swaps[k].wait_recv()
        if (which, d) == (0, 0):
            continue
        outgoing[k] = (part[k] + near[k]).astype(bf16)
        place = lax.rem(level + d, levels) * cores + core
        if which == 0:
            copy = pltpu.make_async_remote_copy(
                src_ref=outgoing.at[k], dst_ref=far.at[d - 1], send_sem=zsend.at[d - 1], recv_sem=zrecv.at[d - 1],
                device_id={"tile": tile, "slab": place}, device_id_type=MESH,
            )
        else:
            copy = pltpu.make_async_remote_copy(
                src_ref=outgoing.at[k], dst_ref=far.at[levels - 1 + d], send_sem=fsend.at[d], recv_sem=frecv.at[d],
                device_id={"tile": following, "slab": place}, device_id_type=MESH,
            )
        copy.start()
        sends.append(copy)
    for copy in sends:
        copy.wait()
    for copy in swaps:
        copy.wait_send()
    last = len(order) - 1
    for p in range(4):
        for h in range(3):
            value = part[last, p, h] + near[last, p, h]
            for k in range(2 * levels - 1):
                value = value + far[k, p, h].astype(f32)
            out[p // 2, p % 2, :, lanes(h)] = rearrange(value, unsort[...])


def reduce(total, tiles, slabs):
    cores = 2
    levels = slabs // cores
    planes, cols, rows, lanes = total.shape
    each = rows // (2 * slabs)
    sem = pltpu.SemaphoreType.DMA
    count = 2 * levels
    total = total.reshape(planes, cols, rows // (cores * each), cores, each, lanes)
    return pl.pallas_call(
        functools.partial(reduce_kernel, tiles, slabs, cores),
        out_shape=jax.ShapeDtypeStruct((2, 2, each, cols * lanes), f32),
        in_specs=[anyspace, vmem],
        out_specs=vmem,
        scratch_shapes=[
            pltpu.VMEM((count, planes, cols, each, lanes), f32),
            pltpu.VMEM((count, planes, cols, each, lanes), f32),
            pltpu.VMEM((count - 1, planes, cols, each, lanes), bf16),
            pltpu.VMEM((count, planes, cols, each, lanes), bf16),
            sem((count,)),
            sem((count,)), sem((count,)),
            sem((levels - 1,)), sem((levels - 1,)),
            sem((levels,)), sem((levels,)),
        ],
        compiler_params=pltpu.CompilerParams(collective_id=1, has_side_effects=True, vmem_limit_bytes=VMEM_LIMIT),
        name="reduce",
    )(total, lane_order().T)


def shards(intensities, object_field, probe_wave, owner_tile, row_offset, col_offset):
    tiles = lax.axis_size("tile")
    slabs = lax.axis_size("slab")
    packed, count, slot, row, col, shard, probe = pack(
        owner_tile, row_offset, col_offset, intensities, object_field, probe_wave, tiles, slabs
    )
    tables = make_tables(intensities.shape[1])
    images, field, fars, waves = exchange(packed, shard, slot, row, col, probe, tables, tiles, slabs)
    total = gradient(count, slot, row, col, field, images, fars, waves, probe, tables)
    return reduce(total, tiles, slabs)


def solution(mesh):
    placed = (
        P(("tile", "slab"), None, None),
        P(None, None, ("tile", "slab"), None),
        P(),
        P(),
        P(),
        P(),
    )
    return jax.shard_map(
        shards,
        mesh=mesh,
        in_specs=placed,
        out_specs=P(None, None, ("tile", "slab"), None),
        check_vma=False,
    )
```

```python
import functools
import math

import jax
import jax.numpy as jnp
import numpy as np
from jax import lax
from jax.experimental import pallas as pl
from jax.experimental.pallas import tpu as pltpu
from jax.sharding import PartitionSpec as P

bf16 = jnp.bfloat16
f32 = jnp.float32
MESH = pl.DeviceIdType.MESH
K = 16
CAP = 2
COL_STEP = 128
CHIRP = 40.0
LANES = 128
HALF = 64
CHUNK = 32
VMEM_LIMIT = 60 * 2**20

smem = pl.BlockSpec(memory_space=pltpu.SMEM)
vmem = pl.BlockSpec(memory_space=pltpu.VMEM)
anyspace = pl.BlockSpec(memory_space=pl.ANY)


def make_tables(n):
    count = np.arange(n)
    angles = ((count[:, None] * count[None, :]) % n).astype(np.float32)
    angles = angles * np.float32(2.0 * math.pi / n)
    scale = np.float32(1.0 / math.sqrt(n))
    c = (np.cos(angles) * scale).astype(np.float32)
    s = (np.sin(angles) * scale).astype(np.float32)
    even = np.arange(0, n, 2)
    odd = even + 1
    low = np.concatenate([even[: n // 4], odd[: n // 4]])
    near = np.arange(n // 2)

    def left(sign, inputs):
        cc = c[np.ix_(low, inputs)]
        ss = s[np.ix_(low, inputs)] * np.float32(sign)
        return np.block([[cc, ss], [-ss, cc]])

    def right(sign, inputs, outputs):
        cc = c[np.ix_(inputs, outputs)]
        ss = s[np.ix_(inputs, outputs)] * np.float32(sign)
        return np.block([[cc, -ss], [ss, cc]])

    f = (((count + n // 2) % n) - n // 2).astype(np.float32) / np.float32(n)
    phases = np.float32(CHIRP) * (f[:, None] ** 2 + f[None, :] ** 2)
    kernel = np.stack([np.cos(phases), -np.sin(phases)]).astype(np.float32)
    kernel = kernel[:, np.concatenate([even, odd]), :][:, :, np.concatenate([low, low + n // 2])]

    def low_precision(a):
        return jnp.asarray(a.astype(np.float32), bf16)

    return dict(
        left_forward=low_precision(np.stack([left(1, even), left(1, odd)])),
        left_inverse=low_precision(np.stack([left(-1, even), left(-1, odd)])),
        right_forward=low_precision(np.stack([right(1, even, low), right(1, odd, low)])),
        right_inverse=low_precision(np.stack([right(-1, even, low), right(-1, odd, low)])),
        right_far=low_precision(np.stack([right(1, even, near), right(1, odd, near)])),
        right_back=low_precision(np.concatenate([right(-1, count, low), right(-1, count, low + n // 2)], 1)),
        kernel=jnp.asarray(kernel),
    )


def lane_order():
    order = np.concatenate([np.arange(0, LANES, 2), np.arange(1, LANES, 2)])
    return jnp.asarray(order[None, :] == np.arange(LANES)[:, None], bf16)


def rearrange(value, order):
    high = value.astype(bf16)
    rest = value - high.astype(f32)
    middle = rest.astype(bf16)
    low = (rest - middle.astype(f32)).astype(bf16)
    parts = [jnp.dot(part, order, preferred_element_type=f32) for part in (high, middle, low)]
    return parts[0] + (parts[1] + parts[2])


def pack_kernel(tiles, slabs, reads, owner, rowoff, coloff, images, field, light, order,
                packed, count, slot, row, col, shard, probe, hold, used, insem, outsem):
    tile = lax.axis_index("tile")
    slab = lax.axis_index("slab")
    for k in range(reads):
        pltpu.make_async_copy(images.at[k], hold.at[k], insem.at[k]).start()
    for t in range(tiles):
        used[t] = 0
    for k in range(K + 1):
        slot[k] = 0
        row[k] = 0
        col[k] = 0
    for k in range(reads):
        dest = owner[(tile * slabs + slab) * reads + k]
        rank = used[dest]
        used[dest] = rank + 1
        pltpu.make_async_copy(images.at[k], hold.at[k], insem.at[k]).wait()
        pltpu.make_async_copy(hold.at[k], packed.at[dest, rank], outsem.at[k]).start()
    for s in range(2):
        for q in range(2):
            for h in range(3):
                shard[2 * s + q, h] = rearrange(field[s, q, :, lanes(h)], order[...])
    for g in range(4):
        probe[g] = rearrange(light[:, lanes(g)], order[...])

    def sender(i, found):
        base = (i * slabs + slab) * reads

        def one(k, state):
            n, rank = state
            hit = owner[base + k] == tile
            slot[n] = jnp.where(hit, i * CAP + rank, 0)
            row[n] = rowoff[base + k]
            col[n] = coloff[base + k]
            step = hit.astype(jnp.int32)
            return n + step, rank + step

        return lax.fori_loop(0, reads, one, (found, jnp.int32(0)), unroll=True)[0]

    count[0] = lax.fori_loop(0, tiles, sender, jnp.int32(0))
    for k in range(reads):
        pltpu.make_async_copy(hold.at[k], packed.at[0, 0], outsem.at[k]).wait()


def pack(owner, rowoff, coloff, images, field, light, tiles, slabs):
    reads, n, _ = images.shape
    rows = field.shape[2]
    return pl.pallas_call(
        functools.partial(pack_kernel, tiles, slabs, reads),
        out_shape=(
            jax.ShapeDtypeStruct((tiles, CAP, n, n), bf16),
            jax.ShapeDtypeStruct((1,), jnp.int32),
            jax.ShapeDtypeStruct((K + 1,), jnp.int32),
            jax.ShapeDtypeStruct((K + 1,), jnp.int32),
            jax.ShapeDtypeStruct((K + 1,), jnp.int32),
            jax.ShapeDtypeStruct((4, 3, rows, LANES), f32),
            jax.ShapeDtypeStruct((4, n, LANES), f32),
        ),
        in_specs=[smem, smem, smem, anyspace, vmem, vmem, vmem],
        out_specs=(anyspace, smem, smem, smem, smem, vmem, vmem),
        scratch_shapes=[
            pltpu.VMEM((reads, n, n), bf16),
            pltpu.SMEM((tiles,), jnp.int32),
            pltpu.SemaphoreType.DMA((reads,)),
            pltpu.SemaphoreType.DMA((reads,)),
        ],
        name="pack",
    )(owner, rowoff, coloff, images, field, light, lane_order())


def product(ar, ai, br, bi):
    return ar * br - ai * bi, ar * bi + ai * br


def conjugate_product(ar, ai, br, bi):
    return ar * br + ai * bi, ar * bi - ai * br


def lanes(c):
    return slice(c * LANES, (c + 1) * LANES)


def rows_of(p, b, r):
    start = 2 * HALF * p + HALF * b + r
    return slice(start, start + CHUNK)


def spread_rows(start, p, b, r):
    return pl.ds(start + p + 2 * HALF * b + 2 * r, CHUNK, stride=2)


def window(field, s, top, left, p, b, r, c):
    where = spread_rows(top, p, b, r)
    return field[2 * s, left + c, where, :], field[2 * s + 1, left + c, where, :]


def put_natural(x, p, b, r, parts):
    for c in range(2):
        for q in range(2):
            x[rows_of(p, b, r), lanes(2 * q + c)] = parts[c][q].astype(bf16)


def put(x, p, b, r, parts):
    low = lax.broadcasted_iota(jnp.int32, (CHUNK, LANES), 1) < HALF
    for q in range(2):
        near, far = parts[0][q], parts[1][q]
        even = jnp.where(low, near, pltpu.roll(far, HALF, 1))
        odd = jnp.where(low, pltpu.roll(near, HALF, 1), far)
        x[0, rows_of(p, b, r), lanes(q)] = even.astype(bf16)
        x[1, rows_of(p, b, r), lanes(q)] = odd.astype(bf16)


def chirp(kernel, p, b, r, c):
    return kernel[0, rows_of(p, b, r), lanes(c)], kernel[1, rows_of(p, b, r), lanes(c)]


def lit(probe, p, b, r, c):
    where = spread_rows(0, p, b, r)
    return probe[c, where, :], probe[2 + c, where, :]


def each(y, use):
    for p in range(2):
        for r in range(0, HALF, CHUNK):
            e = [[y[HALF * k + r:HALF * k + r + CHUNK, lanes(c)] for k in (p, 2 + p)] for c in range(2)]
            o = [[y[HALF * k + r:HALF * k + r + CHUNK, lanes(c)] for k in (4 + p, 6 + p)] for c in range(2)]
            use(p, 0, r, [(e[c][0] + o[c][0], e[c][1] + o[c][1]) for c in range(2)])
            use(p, 1, r, [(e[c][0] - o[c][0], e[c][1] - o[c][1]) for c in range(2)])


def finish_transform(h, y, low, high, left):
    n = 4 * HALF
    m = n // 2
    for p in range(2):
        for q in range(2):
            where = slice(p * n + q * m, p * n + q * m + m)
            h[where, lanes(0)] = low[p * m:p * m + m, lanes(q)].astype(bf16)
            h[where, lanes(1)] = high[p * m:p * m + m, lanes(q)].astype(bf16)
    y[:n, :] = jnp.dot(left[0], h[:n, :], preferred_element_type=f32)
    y[n:, :] = jnp.dot(left[1], h[n:, :], preferred_element_type=f32)


def transform(x, h, y, right, left):
    even = jnp.dot(x[0], right[0], preferred_element_type=f32)
    odd = jnp.dot(x[1], right[1], preferred_element_type=f32)
    finish_transform(h, y, even + odd, even - odd, left)


def transform_natural(x, h, y, right, left):
    n = 4 * HALF
    half = jnp.dot(x[...], right[...], preferred_element_type=f32)
    finish_transform(h, y, half[:, :n], half[:, n:], left)


def interleave(first, second, transforms):
    first[0]()
    for t in range(transforms):
        first[2 * t + 1]()
        second[2 * t]()
        second[2 * t + 1]()
        first[2 * t + 2]()
    second[2 * transforms]()


XORDER = (1, 3, 2)
RELAY_STEPS = ((1, slice(3, 5)), (2, slice(5, 6)), (3, slice(6, 7)), (4, slice(7, 8)), (5, slice(8, 9)))
YORDER = (2, 1, 3)


def exchange_kernel(tiles, slabs, cores, rows, packed, shard, slot, row, col, probe, right_forward, right_inverse, right_far, left_forward, left_inverse, kernel,
                    got, field_out, fars, waves,
                    field, x, h, y, far, wave, hold, localsem, outsem,
                    stage, xsend, xrecv, ysend, yrecv, nsend, nrecv, zsend, zrecv, csend, crecv):
    tile = lax.axis_index("tile")
    slab = lax.axis_index("slab")
    levels = slabs // cores
    core = lax.rem(slab, cores)
    level = lax.div(slab, cores)
    other = level * cores + (1 - core)
    before = lax.rem(tile + tiles - 1, tiles)
    side = math.isqrt(tiles)
    barrier = pltpu.get_barrier_semaphore()

    def greet(t, s):
        pl.semaphore_signal(barrier, inc=1, device_id={"tile": t, "slab": s}, device_id_type=MESH)

    for d in range(1, tiles):
        greet(lax.rem(tile + d, tiles), slab)
    for d in range(1, levels):
        greet(tile, lax.rem(level + d, levels) * cores + core)
    greet(tile, other)
    pl.semaphore_wait(barrier, tiles + levels - 1)

    height = rows * slabs

    def block(which, s):
        return field.at[:, :, pl.ds(pl.multiple_of(which * height + s * rows, rows), rows), :]

    copies = []
    rims = []

    def make(src, dst, send, recv, t, s):
        copy = pltpu.make_async_remote_copy(
            src_ref=src, dst_ref=dst, send_sem=send, recv_sem=recv,
            device_id={"tile": t, "slab": s}, device_id_type=MESH,
        )
        copies.append(copy)
        return copy

    def push(*parts):
        copy = make(*parts)
        copy.start()
        return copy

    def share(which, src, k):
        mine = block(which, slab)
        links = []
        for d in (2, 1, 3)[: levels - 1]:
            place = lax.rem(level + d, levels) * cores + core
            links.append((d, push(src, mine, zsend.at[which, d - 1], zrecv.at[which, d - 1], tile, place)))
        rims.append(push(src, mine, csend.at[which, 0], crecv.at[which, 0], tile, other))
        return links

    def pass_on(which, links):
        for d, copy in links:
            copy.wait_recv()
            s = lax.rem(level + levels - d, levels) * cores + core
            rims.append(push(block(which, s), block(which, s), csend.at[which, d], crecv.at[which, d], tile, other))

    ahead = push(shard, block(1, slab), nsend, nrecv, before, slab)
    own = share(0, shard, 0)
    grid_row, grid_col = lax.div(tile, side), lax.rem(tile, side)

    def at(dy, dx):
        return lax.rem(grid_row + dy + side, side) * side + lax.rem(grid_col + dx + side, side)

    steps = XORDER
    for dy in YORDER:
        push(packed.at[at(dy, 0)], got.at[tile], ysend.at[0, dy - 1], yrecv.at[0, dy - 1], at(dy, 0), slab)
    relays = []
    for dy in YORDER:
        for dx in steps:
            copy = push(packed.at[at(dy, dx)], stage.at[dy - 1, dx - 1], xsend.at[dy, dx - 1], xrecv.at[dy, dx - 1], at(0, dx), slab)
            relays.append((dy, dx, copy))
    for dx in steps:
        push(packed.at[at(0, dx)], got.at[tile], xsend.at[0, dx - 1], xrecv.at[0, dx - 1], at(0, dx), slab)
    keep = pltpu.make_async_copy(shard, block(0, slab), localsem.at[0])
    keep.start()
    first = pltpu.make_async_copy(packed.at[tile], hold, localsem.at[1])
    first.start()
    first.wait()
    second = pltpu.make_async_copy(hold, got.at[tile], localsem.at[1])
    second.start()
    ahead.wait_recv()
    following = share(1, block(1, slab), 1)
    def relay(part):
        for (dy, dx, copy), onward in part:
            copy.wait_recv()
            onward.start()

    onwards = [
        make(stage.at[dy - 1, dx - 1], got.at[at(0, -dx)], ysend.at[dx, dy - 1], yrecv.at[dx, dy - 1], at(dy, 0), slab)
        for dy, dx, _ in relays
    ]
    relays = list(zip(relays, onwards))

    pass_on(0, own)
    relay(relays[:3])
    pass_on(1, following)
    done = [id(c) for _, c in own + following] + [id(ahead)] + [id(r[2]) for r, _ in relays]
    for copy in rims:
        copy.wait_recv()
        done.append(id(copy))
    keep.wait()
    store = pltpu.make_async_copy(field, field_out, localsem.at[0])
    store.start()

    def outputs(k, j):
        turn = lax.rem(k, 2)
        return (
            pltpu.make_async_copy(far.at[turn, j], fars.at[2 * k + j], outsem.at[turn, j, 0]),
            pltpu.make_async_copy(wave.at[turn, j], waves.at[2 * k + j], outsem.at[turn, j, 1]),
        )

    def pattern(k, j):
        top = row[2 * k + j]
        left = col[2 * k + j]
        turn = lax.rem(k, 2)
        xj, hj, yj, fj, wj = x.at[j], h.at[j], y.at[j], far.at[turn, j], wave.at[turn, j]

        def begin():
            for p in range(2):
                for b in range(2):
                    for r in range(0, HALF, CHUNK):
                        put(xj, p, b, r, [
                            product(*lit(probe, p, b, r, c), *window(field, 0, top, left, p, b, r, c)) for c in range(2)
                        ])

        def scatter(p, b, r, parts):
            put(xj, p, b, r, [product(*chirp(kernel, p, b, r, c), *parts[c]) for c in range(2)])

        def enter(p, b, r, parts):
            for c in range(2):
                wj[rows_of(p, b, r), lanes(c)] = parts[c][0]
                wj[rows_of(p, b, r), lanes(2 + c)] = parts[c][1]
            put(xj, p, b, r, [product(*parts[c], *window(field, 1, top, left, p, b, r, c)) for c in range(2)])

        return [
            begin, lambda: transform(xj, hj, yj, right_forward, left_forward), lambda: each(yj, scatter),
            lambda: transform(xj, hj, yj, right_inverse, left_inverse), lambda: each(yj, enter),
            lambda: transform(xj, hj, fj, right_far, left_forward), lambda: None,
        ]

    def step(k, carry):
        @pl.when(k >= 2)
        def _():
            for j in range(2):
                for copy in outputs(k - 2, j):
                    copy.wait()

        interleave(pattern(k, 0), pattern(k, 1), 3)
        for j in range(2):
            for copy in outputs(k, j):
                copy.start()

        for when, part in RELAY_STEPS:
            @pl.when(k == when)
            def _():
                relay(relays[part])

        return carry

    pairs = K // 2
    lax.fori_loop(0, pairs, step, 0)
    for k in (pairs - 2, pairs - 1):
        for j in range(2):
            for copy in outputs(k, j):
                copy.wait()
    store.wait()
    second.wait()
    for copy in copies:
        copy.wait_send()
        if id(copy) not in done:
            copy.wait_recv()


def exchange(packed, shard, slot, row, col, probe, tables, tiles, slabs):
    n = packed.shape[2]
    planes, cols, rows, width = shard.shape
    cores = 2
    levels = slabs // cores
    side = math.isqrt(tiles)
    sem = pltpu.SemaphoreType.DMA
    extended = (planes, cols, 2 * rows * slabs, width)
    return pl.pallas_call(
        functools.partial(exchange_kernel, tiles, slabs, cores, rows),
        out_shape=(
            jax.ShapeDtypeStruct(packed.shape, packed.dtype),
            jax.ShapeDtypeStruct(extended, f32),
            jax.ShapeDtypeStruct((K, 2 * n, n), f32),
            jax.ShapeDtypeStruct((K, n, 2 * n), f32),
        ),
        in_specs=[anyspace, vmem, smem, smem, smem] + [vmem] * 7,
        out_specs=(anyspace,) * 4,
        scratch_shapes=[
            pltpu.VMEM(extended, f32),
            pltpu.VMEM((2, 2, n, n), bf16),
            pltpu.VMEM((2, 2 * n, n), bf16),
            pltpu.VMEM((2, 2 * n, n), f32),
            pltpu.VMEM((2, 2, 2 * n, n), f32),
            pltpu.VMEM((2, 2, n, 2 * n), f32),
            pltpu.VMEM((CAP, n, n), bf16),
            sem((2,)),
            sem((2, 2, 2)),
            pltpu.VMEM((side - 1, side - 1, CAP, n, n), bf16),
            sem((side, side - 1)), sem((side, side - 1)),
            sem((side, side - 1)), sem((side, side - 1)),
            sem, sem,
            sem((2, levels - 1)), sem((2, levels - 1)),
            sem((2, levels)), sem((2, levels)),
        ],
        compiler_params=pltpu.CompilerParams(collective_id=0, has_side_effects=True, vmem_limit_bytes=VMEM_LIMIT),
        name="exchange",
    )(
        packed, shard, slot, row, col, probe, tables["right_forward"], tables["right_inverse"], tables["right_far"],
        tables["left_forward"], tables["left_inverse"], tables["kernel"],
    )


def together(*groups):
    steps = max(len(group) for group in groups)
    for i in range(steps):
        for group in groups:
            for unit in group[i * len(group) // steps:(i + 1) * len(group) // steps]:
                unit()


def each_part(y, use, p, r):
    e = [[y[HALF * k + r:HALF * k + r + CHUNK, lanes(c)] for k in (p, 2 + p)] for c in range(2)]
    o = [[y[HALF * k + r:HALF * k + r + CHUNK, lanes(c)] for k in (4 + p, 6 + p)] for c in range(2)]
    use(p, 0, r, [(e[c][0] + o[c][0], e[c][1] + o[c][1]) for c in range(2)])
    use(p, 1, r, [(e[c][0] - o[c][0], e[c][1] - o[c][1]) for c in range(2)])


def grad_kernel(count, slot, row, col, field, images, fars, waves, probe, right_forward, right_inverse, right_back, left_forward, left_inverse, kernel,
                out, total, x, xfull, h, far, wave, measured, image, insem, outsem):
    dump = field.shape[2]
    total[...] = jnp.zeros_like(total)
    live = count[0]

    def inputs(i):
        index = slot[i]
        place = lax.rem(i, 4)
        return (
            pltpu.make_async_copy(images.at[lax.div(index, CAP), lax.rem(index, CAP)], image.at[place], insem.at[place, 0]),
            pltpu.make_async_copy(fars.at[i], far.at[place], insem.at[place, 1]),
            pltpu.make_async_copy(waves.at[i], wave.at[place], insem.at[place, 2]),
        )

    def pattern(i, j, valid, accs):
        top = row[i]
        left = col[i]
        place = top if valid is None else jnp.where(valid, top, dump)
        at = lax.rem(i, 4)
        xj, xf, hj, mj = x.at[j], xfull.at[j], h.at[j], measured.at[j]
        wj, fj, source = wave.at[at], far.at[at], image.at[at]

        def add(s, p, b, r, parts):
            where = spread_rows(place, p, b, r)
            for c in range(2):
                total[2 * s, left + c, where, :] += parts[c][0]
                total[2 * s + 1, left + c, where, :] += parts[c][1]

        def compare(p, b, r, parts):
            scaled = []
            for c in range(2):
                re, im = parts[c]
                misfit = re * re + im * im - mj[c, spread_rows(0, p, b, r), :]
                scaled.append((re * misfit, im * misfit))
            put_natural(xf, p, b, r, scaled)

        def leave(p, b, r, parts):
            where = rows_of(p, b, r)
            add(1, p, b, r, [conjugate_product(wj[where, lanes(c)], wj[where, lanes(2 + c)], *parts[c]) for c in range(2)])
            put(xj, p, b, r, [conjugate_product(*window(field, 1, top, left, p, b, r, c), *parts[c]) for c in range(2)])

        def gather(p, b, r, parts):
            put(xj, p, b, r, [conjugate_product(*chirp(kernel, p, b, r, c), *parts[c]) for c in range(2)])

        def finish(p, b, r, parts):
            add(0, p, b, r, [conjugate_product(*lit(probe, p, b, r, c), *parts[c]) for c in range(2)])

        n = 4 * HALF
        units = n // CHUNK
        acc = [accs[(2 * j + u) * units:(2 * j + u + 1) * units] for u in range(2)]

        def compare_units():
            def convert():
                for c in range(2):
                    mj[c] = source[:, lanes(c)].astype(f32)

            return [convert] + [functools.partial(each_part, fj, compare, p, r) for p in range(2) for r in range(0, HALF, CHUNK)]

        def push(first, second):
            pltpu.matmul_push_rhs(first, j, 0)
            pltpu.matmul_push_rhs(second, j, 1)

        def feed(i, first, second, load):
            pltpu.matmul_acc_lhs(acc[0][i], first, j if load else None)
            pltpu.matmul_acc_lhs(acc[1][i], second, j if load else None)

        def rows(i):
            return slice(i * CHUNK, (i + 1) * CHUNK)

        def right_units(right):
            def unit(i):
                if i == 0:
                    push(right[0], right[1])
                feed(i, xj[0, rows(i), :], xj[1, rows(i), :], i == 0)

            return [functools.partial(unit, i) for i in range(units)]

        def back_units():
            def unit(t, i):
                if i == 0:
                    push(right_back[t * n:(t + 1) * n, :n], right_back[t * n:(t + 1) * n, n:])
                part = xf[rows(i), t * n:(t + 1) * n]
                feed(i, part, part, i == 0)

            return [functools.partial(unit, t, i) for t in range(2) for i in range(units)]

        def half_units(split):
            def unit(i):
                low = pltpu.matmul_pop(acc[0][i])
                high = pltpu.matmul_pop(acc[1][i])
                if split:
                    low, high = low + high, low - high
                m = n // 2
                p, start = divmod(i * CHUNK, m)
                for q in range(2):
                    where = slice(p * n + q * m + start, p * n + q * m + start + CHUNK)
                    hj[where, lanes(0)] = low[:, lanes(q)].astype(bf16)
                    hj[where, lanes(1)] = high[:, lanes(q)].astype(bf16)

            return [functools.partial(unit, i) for i in range(units)]

        order = [(p, r) for p in range(2) for r in range(0, HALF, CHUNK)]

        def left_units(left):
            def unit(i):
                if i == 0:
                    push(hj[:n, :], hj[n:, :])
                p, r = order[i // 2]
                start = (i % 2) * 2 * HALF + p * HALF + r
                feed(i, left[0, start:start + CHUNK, :], left[1, start:start + CHUNK, :], i == 0)

            return [functools.partial(unit, i) for i in range(units)]

        def use_units(use):
            def unit(i):
                p, r = order[i]
                e = [pltpu.matmul_pop(acc[0][2 * i + q]) for q in range(2)]
                o = [pltpu.matmul_pop(acc[1][2 * i + q]) for q in range(2)]
                use(p, 0, r, [(e[0][:, lanes(c)] + o[0][:, lanes(c)], e[1][:, lanes(c)] + o[1][:, lanes(c)]) for c in range(2)])
                use(p, 1, r, [(e[0][:, lanes(c)] - o[0][:, lanes(c)], e[1][:, lanes(c)] - o[1][:, lanes(c)]) for c in range(2)])

            return [functools.partial(unit, i) for i in range(len(order))]

        return compare_units(), [
            (back_units(), half_units(False)), (left_units(left_inverse), use_units(leave)),
            (right_units(right_forward), half_units(True)), (left_units(left_forward), use_units(gather)),
            (right_units(right_inverse), half_units(True)), (left_units(left_inverse), use_units(finish)),
        ]

    def step(k, carry):
        a = 2 * k
        b = jnp.minimum(2 * k + 1, live - 1)
        valid = 2 * k + 1 < live
        for copy in inputs(a):
            copy.wait()

        @pl.when(valid)
        def _():
            for copy in inputs(2 * k + 1):
                copy.wait()

        for ahead in (2, 3):
            @pl.when(2 * k + ahead < live)
            def _():
                for copy in inputs(2 * k + ahead):
                    copy.start()

        def both(*accs):
            first_compare, first = pattern(a, 0, None, accs)
            second_compare, second = pattern(b, 1, valid, accs)
            together(first_compare)
            together(first[0][0], second_compare)
            for s in range(len(first)):
                together(second[s][0], first[s][1])
                together(first[s + 1][0] if s + 1 < len(first) else [], second[s][1])

        n = 4 * HALF
        pl.run_scoped(both, *[
            pltpu.ACC(mxu_id=u)((CHUNK, n), f32) for _ in range(2) for u in range(2) for _ in range(n // CHUNK)
        ])
        return carry

    for s in range(2):
        @pl.when(live > s)
        def _():
            for copy in inputs(s):
                copy.start()
    lax.fori_loop(0, lax.div(live + 1, 2), step, 0)
    store = pltpu.make_async_copy(total.at[:, :, :dump], out, outsem)
    store.start()
    store.wait()


def gradient(count, slot, row, col, field, images, fars, waves, probe, tables):
    planes, cols, rows, width = field.shape
    n = probe.shape[1]
    return pl.pallas_call(
        grad_kernel,
        out_shape=jax.ShapeDtypeStruct(field.shape, f32),
        in_specs=[smem] * 4 + [vmem] + [anyspace] * 3 + [vmem] * 7,
        out_specs=anyspace,
        scratch_shapes=[
            pltpu.VMEM((planes, cols, rows + n, width), f32),
            pltpu.VMEM((2, 2, n, n), bf16),
            pltpu.VMEM((2, n, 2 * n), bf16),
            pltpu.VMEM((2, 2 * n, n), bf16),
            pltpu.VMEM((4, 2 * n, n), f32),
            pltpu.VMEM((4, n, 2 * n), f32),
            pltpu.VMEM((2, 2, n, width), f32),
            pltpu.VMEM((4, n, n), bf16),
            pltpu.SemaphoreType.DMA((4, 3)),
            pltpu.SemaphoreType.DMA,
        ],
        compiler_params=pltpu.CompilerParams(vmem_limit_bytes=VMEM_LIMIT),
        name="gradient",
    )(
        count, slot, row, col, field, images, fars, waves, probe, tables["right_forward"], tables["right_inverse"],
        tables["right_back"], tables["left_forward"], tables["left_inverse"], tables["kernel"],
    )


def reduce_kernel(tiles, slabs, cores, total, unsort, out, part, near, far, outgoing,
                  localsem, csend, crecv, zsend, zrecv, fsend, frecv):
    tile = lax.axis_index("tile")
    slab = lax.axis_index("slab")
    levels = slabs // cores
    core = lax.rem(slab, cores)
    level = lax.div(slab, cores)
    other = level * cores + (1 - core)
    following = lax.rem(tile + 1, tiles)
    preceding = lax.rem(tile + tiles - 1, tiles)
    barrier = pltpu.get_barrier_semaphore()

    def greet(t, s):
        pl.semaphore_signal(barrier, inc=1, device_id={"tile": t, "slab": s}, device_id_type=MESH)

    greet(tile, other)
    for d in range(1, levels):
        greet(tile, lax.rem(level + d, levels) * cores + core)
    for d in range(levels):
        place = lax.rem(level + d, levels) * cores + core
        greet(following, place)
        greet(preceding, place)
    pl.semaphore_wait(barrier, 1 + levels - 1 + 2 * levels)

    def block(which, d):
        return which * levels + lax.rem(level + d, levels)

    order = [(1, 2), (1, 1), (1, 3), (0, 2), (0, 1), (0, 3), (1, 0), (0, 0)]
    swaps = []
    takes = []
    for k, (which, d) in enumerate(order):
        b = block(which, d)
        copy = pltpu.make_async_remote_copy(
            src_ref=total.at[:, :, b, 1 - core], dst_ref=near.at[k], send_sem=csend.at[k], recv_sem=crecv.at[k],
            device_id={"tile": tile, "slab": other}, device_id_type=MESH,
        )
        copy.start()
        swaps.append(copy)
        take = pltpu.make_async_copy(total.at[:, :, b, core], part.at[k], localsem.at[k])
        take.start()
        takes.append(take)
    sends = []
    for k, (which, d) in enumerate(order):
        takes[k].wait()
        swaps[k].wait_recv()
        if (which, d) == (0, 0):
            continue
        outgoing[k] = (part[k] + near[k]).astype(bf16)
        place = lax.rem(level + d, levels) * cores + core
        if which == 0:
            copy = pltpu.make_async_remote_copy(
                src_ref=outgoing.at[k], dst_ref=far.at[d - 1], send_sem=zsend.at[d - 1], recv_sem=zrecv.at[d - 1],
                device_id={"tile": tile, "slab": place}, device_id_type=MESH,
            )
        else:
            copy = pltpu.make_async_remote_copy(
                src_ref=outgoing.at[k], dst_ref=far.at[levels - 1 + d], send_sem=fsend.at[d], recv_sem=frecv.at[d],
                device_id={"tile": following, "slab": place}, device_id_type=MESH,
            )
        copy.start()
        sends.append(copy)
    for copy in sends:
        copy.wait()
    for copy in swaps:
        copy.wait_send()
    last = len(order) - 1
    for p in range(4):
        for h in range(3):
            value = part[last, p, h] + near[last, p, h]
            for k in range(2 * levels - 1):
                value = value + far[k, p, h].astype(f32)
            out[p // 2, p % 2, :, lanes(h)] = rearrange(value, unsort[...])


def reduce(total, tiles, slabs):
    cores = 2
    levels = slabs // cores
    planes, cols, rows, lanes = total.shape
    each = rows // (2 * slabs)
    sem = pltpu.SemaphoreType.DMA
    count = 2 * levels
    total = total.reshape(planes, cols, rows // (cores * each), cores, each, lanes)
    return pl.pallas_call(
        functools.partial(reduce_kernel, tiles, slabs, cores),
        out_shape=jax.ShapeDtypeStruct((2, 2, each, cols * lanes), f32),
        in_specs=[anyspace, vmem],
        out_specs=vmem,
        scratch_shapes=[
            pltpu.VMEM((count, planes, cols, each, lanes), f32),
            pltpu.VMEM((count, planes, cols, each, lanes), f32),
            pltpu.VMEM((count - 1, planes, cols, each, lanes), bf16),
            pltpu.VMEM((count, planes, cols, each, lanes), bf16),
            sem((count,)),
            sem((count,)), sem((count,)),
            sem((levels - 1,)), sem((levels - 1,)),
            sem((levels,)), sem((levels,)),
        ],
        compiler_params=pltpu.CompilerParams(collective_id=1, has_side_effects=True, vmem_limit_bytes=VMEM_LIMIT),
        name="reduce",
    )(total, lane_order().T)


def shards(intensities, object_field, probe_wave, owner_tile, row_offset, col_offset):
    tiles = lax.axis_size("tile")
    slabs = lax.axis_size("slab")
    packed, count, slot, row, col, shard, probe = pack(
        owner_tile, row_offset, col_offset, intensities, object_field, probe_wave, tiles, slabs
    )
    tables = make_tables(intensities.shape[1])
    images, field, fars, waves = exchange(packed, shard, slot, row, col, probe, tables, tiles, slabs)
    total = gradient(count, slot, row, col, field, images, fars, waves, probe, tables)
    return reduce(total, tiles, slabs)


def solution(mesh):
    placed = (
        P(("tile", "slab"), None, None),
        P(None, None, ("tile", "slab"), None),
        P(),
        P(),
        P(),
        P(),
    )
    return jax.shard_map(
        shards,
        mesh=mesh,
        in_specs=placed,
        out_specs=P(None, None, ("tile", "slab"), None),
        check_vma=False,
    )
```

```python
import functools
import math

import jax
import jax.numpy as jnp
import numpy as np
from jax import lax
from jax.experimental import pallas as pl
from jax.experimental.pallas import tpu as pltpu
from jax.sharding import PartitionSpec as P

bf16 = jnp.bfloat16
f32 = jnp.float32
MESH = pl.DeviceIdType.MESH
K = 16
CAP = 2
COL_STEP = 128
CHIRP = 40.0
LANES = 128
HALF = 64
CHUNK = 32
VMEM_LIMIT = 60 * 2**20

smem = pl.BlockSpec(memory_space=pltpu.SMEM)
vmem = pl.BlockSpec(memory_space=pltpu.VMEM)
anyspace = pl.BlockSpec(memory_space=pl.ANY)


def make_tables(n):
    count = np.arange(n)
    angles = ((count[:, None] * count[None, :]) % n).astype(np.float32)
    angles = angles * np.float32(2.0 * math.pi / n)
    scale = np.float32(1.0 / math.sqrt(n))
    c = (np.cos(angles) * scale).astype(np.float32)
    s = (np.sin(angles) * scale).astype(np.float32)
    even = np.arange(0, n, 2)
    odd = even + 1
    low = np.concatenate([even[: n // 4], odd[: n // 4]])
    near = np.arange(n // 2)

    def left(sign, inputs):
        cc = c[np.ix_(low, inputs)]
        ss = s[np.ix_(low, inputs)] * np.float32(sign)
        return np.block([[cc, ss], [-ss, cc]])

    def right(sign, inputs, outputs):
        cc = c[np.ix_(inputs, outputs)]
        ss = s[np.ix_(inputs, outputs)] * np.float32(sign)
        return np.block([[cc, -ss], [ss, cc]])

    f = (((count + n // 2) % n) - n // 2).astype(np.float32) / np.float32(n)
    phases = np.float32(CHIRP) * (f[:, None] ** 2 + f[None, :] ** 2)
    kernel = np.stack([np.cos(phases), -np.sin(phases)]).astype(np.float32)
    kernel = kernel[:, np.concatenate([even, odd]), :][:, :, np.concatenate([low, low + n // 2])]

    def low_precision(a):
        return jnp.asarray(a.astype(np.float32), bf16)

    return dict(
        left_forward=low_precision(np.stack([left(1, even), left(1, odd)])),
        left_inverse=low_precision(np.stack([left(-1, even), left(-1, odd)])),
        right_forward=low_precision(np.stack([right(1, even, low), right(1, odd, low)])),
        right_inverse=low_precision(np.stack([right(-1, even, low), right(-1, odd, low)])),
        right_far=low_precision(np.stack([right(1, even, near), right(1, odd, near)])),
        right_back=low_precision(np.concatenate([right(-1, count, low), right(-1, count, low + n // 2)], 1)),
        kernel=jnp.asarray(kernel),
    )


def lane_order():
    order = np.concatenate([np.arange(0, LANES, 2), np.arange(1, LANES, 2)])
    return jnp.asarray(order[None, :] == np.arange(LANES)[:, None], bf16)


def rearrange(value, order):
    high = value.astype(bf16)
    rest = value - high.astype(f32)
    middle = rest.astype(bf16)
    low = (rest - middle.astype(f32)).astype(bf16)
    parts = [jnp.dot(part, order, preferred_element_type=f32) for part in (high, middle, low)]
    return parts[0] + (parts[1] + parts[2])


def route_kernel(tiles, slabs, reads, owner, rowoff, coloff, pick, count, slot, row, col, used):
    tile = lax.axis_index("tile")
    slab = lax.axis_index("slab")
    for t in range(tiles):
        used[t] = 0
    for k in range(tiles * CAP):
        pick[k] = 0
    for k in range(K + 1):
        slot[k] = 0
        row[k] = 0
        col[k] = 0
    for k in range(reads):
        dest = owner[(tile * slabs + slab) * reads + k]
        rank = used[dest]
        used[dest] = rank + 1
        pick[dest * CAP + rank] = k

    def sender(i, found):
        base = (i * slabs + slab) * reads

        def one(k, state):
            n, rank = state
            hit = owner[base + k] == tile
            slot[n] = jnp.where(hit, i * CAP + rank, 0)
            row[n] = rowoff[base + k]
            col[n] = coloff[base + k]
            step = hit.astype(jnp.int32)
            return n + step, rank + step

        return lax.fori_loop(0, reads, one, (found, jnp.int32(0)), unroll=True)[0]

    count[0] = lax.fori_loop(0, tiles, sender, jnp.int32(0))


def route(owner, rowoff, coloff, reads, tiles, slabs):
    sizes = (tiles * CAP, 1, K + 1, K + 1, K + 1)
    return pl.pallas_call(
        functools.partial(route_kernel, tiles, slabs, reads),
        out_shape=tuple(jax.ShapeDtypeStruct((size,), jnp.int32) for size in sizes),
        in_specs=[smem, smem, smem],
        out_specs=(smem,) * 5,
        scratch_shapes=[pltpu.SMEM((tiles,), jnp.int32)],
        name="route",
    )(owner, rowoff, coloff)


def product(ar, ai, br, bi):
    return ar * br - ai * bi, ar * bi + ai * br


def conjugate_product(ar, ai, br, bi):
    return ar * br + ai * bi, ar * bi - ai * br


def lanes(c):
    return slice(c * LANES, (c + 1) * LANES)


def rows_of(p, b, r):
    start = 2 * HALF * p + HALF * b + r
    return slice(start, start + CHUNK)


def spread_rows(start, p, b, r):
    return pl.ds(start + p + 2 * HALF * b + 2 * r, CHUNK, stride=2)


def window(field, s, top, left, p, b, r, c):
    where = spread_rows(top, p, b, r)
    return field[2 * s, left + c, where, :], field[2 * s + 1, left + c, where, :]


def put_natural(x, p, b, r, parts):
    for c in range(2):
        for q in range(2):
            x[rows_of(p, b, r), lanes(2 * q + c)] = parts[c][q].astype(bf16)


def put(x, p, b, r, parts):
    low = lax.broadcasted_iota(jnp.int32, (CHUNK, LANES), 1) < HALF
    for q in range(2):
        near, far = parts[0][q], parts[1][q]
        even = jnp.where(low, near, pltpu.roll(far, HALF, 1))
        odd = jnp.where(low, pltpu.roll(near, HALF, 1), far)
        x[0, rows_of(p, b, r), lanes(q)] = even.astype(bf16)
        x[1, rows_of(p, b, r), lanes(q)] = odd.astype(bf16)


def chirp(kernel, p, b, r, c):
    return kernel[0, rows_of(p, b, r), lanes(c)], kernel[1, rows_of(p, b, r), lanes(c)]


def lit(probe, p, b, r, c):
    where = spread_rows(0, p, b, r)
    return probe[c, where, :], probe[2 + c, where, :]


def each(y, use):
    for p in range(2):
        for r in range(0, HALF, CHUNK):
            e = [[y[HALF * k + r:HALF * k + r + CHUNK, lanes(c)] for k in (p, 2 + p)] for c in range(2)]
            o = [[y[HALF * k + r:HALF * k + r + CHUNK, lanes(c)] for k in (4 + p, 6 + p)] for c in range(2)]
            use(p, 0, r, [(e[c][0] + o[c][0], e[c][1] + o[c][1]) for c in range(2)])
            use(p, 1, r, [(e[c][0] - o[c][0], e[c][1] - o[c][1]) for c in range(2)])


def finish_transform(h, y, low, high, left):
    n = 4 * HALF
    m = n // 2
    for p in range(2):
        for q in range(2):
            where = slice(p * n + q * m, p * n + q * m + m)
            h[where, lanes(0)] = low[p * m:p * m + m, lanes(q)].astype(bf16)
            h[where, lanes(1)] = high[p * m:p * m + m, lanes(q)].astype(bf16)
    y[:n, :] = jnp.dot(left[0], h[:n, :], preferred_element_type=f32)
    y[n:, :] = jnp.dot(left[1], h[n:, :], preferred_element_type=f32)


def transform(x, h, y, right, left):
    even = jnp.dot(x[0], right[0], preferred_element_type=f32)
    odd = jnp.dot(x[1], right[1], preferred_element_type=f32)
    finish_transform(h, y, even + odd, even - odd, left)


def transform_natural(x, h, y, right, left):
    n = 4 * HALF
    half = jnp.dot(x[...], right[...], preferred_element_type=f32)
    finish_transform(h, y, half[:, :n], half[:, n:], left)


def interleave(first, second, transforms):
    first[0]()
    for t in range(transforms):
        first[2 * t + 1]()
        second[2 * t]()
        second[2 * t + 1]()
        first[2 * t + 2]()
    second[2 * transforms]()


XORDER = (1, 3, 2)
RELAY_STEPS = ((1, slice(3, 5)), (2, slice(5, 6)), (3, slice(6, 7)), (4, slice(7, 8)), (5, slice(8, 9)))
YORDER = (2, 1, 3)


def exchange_kernel(tiles, slabs, cores, rows, images, block_in, light, sort, pick, row, col,
                    right_forward, right_inverse, right_far, left_forward, left_inverse, kernel,
                    got, field_out, fars, waves, probe,
                    field, x, h, y, far, wave, pictures, packed, shard, localsem, outsem, insem,
                    stage, xsend, xrecv, ysend, yrecv, nsend, nrecv, zsend, zrecv, csend, crecv):
    tile = lax.axis_index("tile")
    slab = lax.axis_index("slab")
    levels = slabs // cores
    core = lax.rem(slab, cores)
    level = lax.div(slab, cores)
    other = level * cores + (1 - core)
    before = lax.rem(tile + tiles - 1, tiles)
    side = math.isqrt(tiles)
    barrier = pltpu.get_barrier_semaphore()

    def greet(t, s):
        pl.semaphore_signal(barrier, inc=1, device_id={"tile": t, "slab": s}, device_id_type=MESH)

    for d in range(1, tiles):
        greet(lax.rem(tile + d, tiles), slab)
    for d in range(1, levels):
        greet(tile, lax.rem(level + d, levels) * cores + core)
    greet(tile, other)
    reads = images.shape[0]
    loads = [pltpu.make_async_copy(images.at[k], pictures.at[k], insem.at[k]) for k in range(reads)]
    for load in loads:
        load.start()
    for s in range(2):
        for q in range(2):
            for c in range(3):
                shard[2 * s + q, c] = rearrange(block_in[s, q, :, lanes(c)], sort[...])
    for load in loads:
        load.wait()

    def fill(t, carry):
        for k in range(CAP):
            packed[t, k] = pictures[pick[t * CAP + k]]
        return carry

    lax.fori_loop(0, tiles, fill, 0)
    pl.semaphore_wait(barrier, tiles + levels - 1)

    height = rows * slabs

    def block(which, s):
        return field.at[:, :, pl.ds(pl.multiple_of(which * height + s * rows, rows), rows), :]

    copies = []
    rims = []

    def make(src, dst, send, recv, t, s):
        copy = pltpu.make_async_remote_copy(
            src_ref=src, dst_ref=dst, send_sem=send, recv_sem=recv,
            device_id={"tile": t, "slab": s}, device_id_type=MESH,
        )
        copies.append(copy)
        return copy

    def push(*parts):
        copy = make(*parts)
        copy.start()
        return copy

    def share(which, src, k):
        mine = block(which, slab)
        links = []
        for d in (2, 1, 3)[: levels - 1]:
            place = lax.rem(level + d, levels) * cores + core
            links.append((d, push(src, mine, zsend.at[which, d - 1], zrecv.at[which, d - 1], tile, place)))
        rims.append(push(src, mine, csend.at[which, 0], crecv.at[which, 0], tile, other))
        return links

    def pass_on(which, links):
        for d, copy in links:
            copy.wait_recv()
            s = lax.rem(level + levels - d, levels) * cores + core
            rims.append(push(block(which, s), block(which, s), csend.at[which, d], crecv.at[which, d], tile, other))

    ahead = push(shard, block(1, slab), nsend, nrecv, before, slab)
    own = share(0, shard, 0)
    grid_row, grid_col = lax.div(tile, side), lax.rem(tile, side)

    def at(dy, dx):
        return lax.rem(grid_row + dy + side, side) * side + lax.rem(grid_col + dx + side, side)

    steps = XORDER
    for dy in YORDER:
        push(packed.at[at(dy, 0)], got.at[tile], ysend.at[0, dy - 1], yrecv.at[0, dy - 1], at(dy, 0), slab)
    relays = []
    for dy in YORDER:
        for dx in steps:
            copy = push(packed.at[at(dy, dx)], stage.at[dy - 1, dx - 1], xsend.at[dy, dx - 1], xrecv.at[dy, dx - 1], at(0, dx), slab)
            relays.append((dy, dx, copy))
    for dx in steps:
        push(packed.at[at(0, dx)], got.at[tile], xsend.at[0, dx - 1], xrecv.at[0, dx - 1], at(0, dx), slab)
    keep = pltpu.make_async_copy(shard, block(0, slab), localsem.at[0])
    keep.start()
    second = pltpu.make_async_copy(packed.at[tile], got.at[tile], localsem.at[1])
    second.start()
    for g in range(4):
        probe[g] = rearrange(light[:, lanes(g)], sort[...])
    ahead.wait_recv()
    following = share(1, block(1, slab), 1)
    def relay(part):
        for (dy, dx, copy), onward in part:
            copy.wait_recv()
            onward.start()

    onwards = [
        make(stage.at[dy - 1, dx - 1], got.at[at(0, -dx)], ysend.at[dx, dy - 1], yrecv.at[dx, dy - 1], at(dy, 0), slab)
        for dy, dx, _ in relays
    ]
    relays = list(zip(relays, onwards))

    pass_on(0, own)
    relay(relays[:3])
    pass_on(1, following)
    done = [id(c) for _, c in own + following] + [id(ahead)] + [id(r[2]) for r, _ in relays]
    for copy in rims:
        copy.wait_recv()
        done.append(id(copy))
    keep.wait()
    store = pltpu.make_async_copy(field, field_out, localsem.at[0])
    store.start()

    def outputs(k, j):
        turn = lax.rem(k, 2)
        return (
            pltpu.make_async_copy(far.at[turn, j], fars.at[2 * k + j], outsem.at[turn, j, 0]),
            pltpu.make_async_copy(wave.at[turn, j], waves.at[2 * k + j], outsem.at[turn, j, 1]),
        )

    def pattern(k, j):
        top = row[2 * k + j]
        left = col[2 * k + j]
        turn = lax.rem(k, 2)
        xj, hj, yj, fj, wj = x.at[j], h.at[j], y.at[j], far.at[turn, j], wave.at[turn, j]

        def begin():
            for p in range(2):
                for b in range(2):
                    for r in range(0, HALF, CHUNK):
                        put(xj, p, b, r, [
                            product(*lit(probe, p, b, r, c), *window(field, 0, top, left, p, b, r, c)) for c in range(2)
                        ])

        def scatter(p, b, r, parts):
            put(xj, p, b, r, [product(*chirp(kernel, p, b, r, c), *parts[c]) for c in range(2)])

        def enter(p, b, r, parts):
            for c in range(2):
                wj[rows_of(p, b, r), lanes(c)] = parts[c][0]
                wj[rows_of(p, b, r), lanes(2 + c)] = parts[c][1]
            put(xj, p, b, r, [product(*parts[c], *window(field, 1, top, left, p, b, r, c)) for c in range(2)])

        return [
            begin, lambda: transform(xj, hj, yj, right_forward, left_forward), lambda: each(yj, scatter),
            lambda: transform(xj, hj, yj, right_inverse, left_inverse), lambda: each(yj, enter),
            lambda: transform(xj, hj, fj, right_far, left_forward), lambda: None,
        ]

    def step(k, carry):
        @pl.when(k >= 2)
        def _():
            for j in range(2):
                for copy in outputs(k - 2, j):
                    copy.wait()

        interleave(pattern(k, 0), pattern(k, 1), 3)
        for j in range(2):
            for copy in outputs(k, j):
                copy.start()

        for when, part in RELAY_STEPS:
            @pl.when(k == when)
            def _():
                relay(relays[part])

        return carry

    pairs = K // 2
    lax.fori_loop(0, pairs, step, 0)
    for k in (pairs - 2, pairs - 1):
        for j in range(2):
            for copy in outputs(k, j):
                copy.wait()
    store.wait()
    second.wait()
    for copy in copies:
        copy.wait_send()
        if id(copy) not in done:
            copy.wait_recv()


def exchange(images, block, light, pick, row, col, tables, tiles, slabs):
    reads, n, _ = images.shape
    rows = block.shape[2]
    planes, cols, width = 4, block.shape[3] // LANES, LANES
    cores = 2
    levels = slabs // cores
    side = math.isqrt(tiles)
    sem = pltpu.SemaphoreType.DMA
    extended = (planes, cols, 2 * rows * slabs, width)
    return pl.pallas_call(
        functools.partial(exchange_kernel, tiles, slabs, cores, rows),
        out_shape=(
            jax.ShapeDtypeStruct((tiles, CAP, n, n), bf16),
            jax.ShapeDtypeStruct(extended, f32),
            jax.ShapeDtypeStruct((K, 2 * n, n), f32),
            jax.ShapeDtypeStruct((K, n, 2 * n), f32),
            jax.ShapeDtypeStruct((4, n, width), f32),
        ),
        in_specs=[anyspace, vmem, vmem, vmem, smem, smem, smem] + [vmem] * 6,
        out_specs=(anyspace,) * 4 + (vmem,),
        scratch_shapes=[
            pltpu.VMEM(extended, f32),
            pltpu.VMEM((2, 2, n, n), bf16),
            pltpu.VMEM((2, 2 * n, n), bf16),
            pltpu.VMEM((2, 2 * n, n), f32),
            pltpu.VMEM((2, 2, 2 * n, n), f32),
            pltpu.VMEM((2, 2, n, 2 * n), f32),
            pltpu.VMEM((reads, n, n), bf16),
            pltpu.VMEM((tiles, CAP, n, n), bf16),
            pltpu.VMEM((planes, cols, rows, width), f32),
            sem((2,)),
            sem((2, 2, 2)),
            sem((reads,)),
            pltpu.VMEM((side - 1, side - 1, CAP, n, n), bf16),
            sem((side, side - 1)), sem((side, side - 1)),
            sem((side, side - 1)), sem((side, side - 1)),
            sem, sem,
            sem((2, levels - 1)), sem((2, levels - 1)),
            sem((2, levels)), sem((2, levels)),
        ],
        compiler_params=pltpu.CompilerParams(collective_id=0, has_side_effects=True, vmem_limit_bytes=VMEM_LIMIT),
        name="exchange",
    )(
        images, block, light, lane_order(), pick, row, col,
        tables["right_forward"], tables["right_inverse"], tables["right_far"],
        tables["left_forward"], tables["left_inverse"], tables["kernel"],
    )


def together(*groups):
    steps = max(len(group) for group in groups)
    for i in range(steps):
        for group in groups:
            for unit in group[i * len(group) // steps:(i + 1) * len(group) // steps]:
                unit()


def each_part(y, use, p, r):
    e = [[y[HALF * k + r:HALF * k + r + CHUNK, lanes(c)] for k in (p, 2 + p)] for c in range(2)]
    o = [[y[HALF * k + r:HALF * k + r + CHUNK, lanes(c)] for k in (4 + p, 6 + p)] for c in range(2)]
    use(p, 0, r, [(e[c][0] + o[c][0], e[c][1] + o[c][1]) for c in range(2)])
    use(p, 1, r, [(e[c][0] - o[c][0], e[c][1] - o[c][1]) for c in range(2)])


def grad_kernel(count, slot, row, col, field, images, fars, waves, probe, right_forward, right_inverse, right_back, left_forward, left_inverse, kernel,
                out, total, x, xfull, h, far, wave, measured, image, insem, outsem):
    dump = field.shape[2]
    total[...] = jnp.zeros_like(total)
    live = count[0]

    def inputs(i):
        index = slot[i]
        place = lax.rem(i, 4)
        return (
            pltpu.make_async_copy(images.at[lax.div(index, CAP), lax.rem(index, CAP)], image.at[place], insem.at[place, 0]),
            pltpu.make_async_copy(fars.at[i], far.at[place], insem.at[place, 1]),
            pltpu.make_async_copy(waves.at[i], wave.at[place], insem.at[place, 2]),
        )

    def pattern(i, j, valid, accs):
        top = row[i]
        left = col[i]
        place = top if valid is None else jnp.where(valid, top, dump)
        at = lax.rem(i, 4)
        xj, xf, hj, mj = x.at[j], xfull.at[j], h.at[j], measured.at[j]
        wj, fj, source = wave.at[at], far.at[at], image.at[at]

        def add(s, p, b, r, parts):
            where = spread_rows(place, p, b, r)
            for c in range(2):
                total[2 * s, left + c, where, :] += parts[c][0]
                total[2 * s + 1, left + c, where, :] += parts[c][1]

        def compare(p, b, r, parts):
            scaled = []
            for c in range(2):
                re, im = parts[c]
                misfit = re * re + im * im - mj[c, spread_rows(0, p, b, r), :]
                scaled.append((re * misfit, im * misfit))
            put_natural(xf, p, b, r, scaled)

        def leave(p, b, r, parts):
            where = rows_of(p, b, r)
            add(1, p, b, r, [conjugate_product(wj[where, lanes(c)], wj[where, lanes(2 + c)], *parts[c]) for c in range(2)])
            put(xj, p, b, r, [conjugate_product(*window(field, 1, top, left, p, b, r, c), *parts[c]) for c in range(2)])

        def gather(p, b, r, parts):
            put(xj, p, b, r, [conjugate_product(*chirp(kernel, p, b, r, c), *parts[c]) for c in range(2)])

        def finish(p, b, r, parts):
            add(0, p, b, r, [conjugate_product(*lit(probe, p, b, r, c), *parts[c]) for c in range(2)])

        n = 4 * HALF
        units = n // CHUNK
        acc = [accs[(2 * j + u) * units:(2 * j + u + 1) * units] for u in range(2)]

        def compare_units():
            def convert():
                for c in range(2):
                    mj[c] = source[:, lanes(c)].astype(f32)

            return [convert] + [functools.partial(each_part, fj, compare, p, r) for p in range(2) for r in range(0, HALF, CHUNK)]

        def push(first, second):
            pltpu.matmul_push_rhs(first, j, 0)
            pltpu.matmul_push_rhs(second, j, 1)

        def feed(i, first, second, load):
            pltpu.matmul_acc_lhs(acc[0][i], first, j if load else None)
            pltpu.matmul_acc_lhs(acc[1][i], second, j if load else None)

        def rows(i):
            return slice(i * CHUNK, (i + 1) * CHUNK)

        def right_units(right):
            def unit(i):
                if i == 0:
                    push(right[0], right[1])
                feed(i, xj[0, rows(i), :], xj[1, rows(i), :], i == 0)

            return [functools.partial(unit, i) for i in range(units)]

        def back_units():
            def unit(t, i):
                if i == 0:
                    push(right_back[t * n:(t + 1) * n, :n], right_back[t * n:(t + 1) * n, n:])
                part = xf[rows(i), t * n:(t + 1) * n]
                feed(i, part, part, i == 0)

            return [functools.partial(unit, t, i) for t in range(2) for i in range(units)]

        def half_units(split):
            def unit(i):
                low = pltpu.matmul_pop(acc[0][i])
                high = pltpu.matmul_pop(acc[1][i])
                if split:
                    low, high = low + high, low - high
                m = n // 2
                p, start = divmod(i * CHUNK, m)
                for q in range(2):
                    where = slice(p * n + q * m + start, p * n + q * m + start + CHUNK)
                    hj[where, lanes(0)] = low[:, lanes(q)].astype(bf16)
                    hj[where, lanes(1)] = high[:, lanes(q)].astype(bf16)

            return [functools.partial(unit, i) for i in range(units)]

        order = [(p, r) for p in range(2) for r in range(0, HALF, CHUNK)]

        def left_units(left):
            def unit(i):
                if i == 0:
                    push(hj[:n, :], hj[n:, :])
                p, r = order[i // 2]
                start = (i % 2) * 2 * HALF + p * HALF + r
                feed(i, left[0, start:start + CHUNK, :], left[1, start:start + CHUNK, :], i == 0)

            return [functools.partial(unit, i) for i in range(units)]

        def use_units(use):
            def unit(i):
                p, r = order[i]
                e = [pltpu.matmul_pop(acc[0][2 * i + q]) for q in range(2)]
                o = [pltpu.matmul_pop(acc[1][2 * i + q]) for q in range(2)]
                use(p, 0, r, [(e[0][:, lanes(c)] + o[0][:, lanes(c)], e[1][:, lanes(c)] + o[1][:, lanes(c)]) for c in range(2)])
                use(p, 1, r, [(e[0][:, lanes(c)] - o[0][:, lanes(c)], e[1][:, lanes(c)] - o[1][:, lanes(c)]) for c in range(2)])

            return [functools.partial(unit, i) for i in range(len(order))]

        return compare_units(), [
            (back_units(), half_units(False)), (left_units(left_inverse), use_units(leave)),
            (right_units(right_forward), half_units(True)), (left_units(left_forward), use_units(gather)),
            (right_units(right_inverse), half_units(True)), (left_units(left_inverse), use_units(finish)),
        ]

    def step(k, carry):
        a = 2 * k
        b = jnp.minimum(2 * k + 1, live - 1)
        valid = 2 * k + 1 < live
        for copy in inputs(a):
            copy.wait()

        @pl.when(valid)
        def _():
            for copy in inputs(2 * k + 1):
                copy.wait()

        for ahead in (2, 3):
            @pl.when(2 * k + ahead < live)
            def _():
                for copy in inputs(2 * k + ahead):
                    copy.start()

        def both(*accs):
            first_compare, first = pattern(a, 0, None, accs)
            second_compare, second = pattern(b, 1, valid, accs)
            together(first_compare)
            together(first[0][0], second_compare)
            for s in range(len(first)):
                together(second[s][0], first[s][1])
                together(first[s + 1][0] if s + 1 < len(first) else [], second[s][1])

        n = 4 * HALF
        pl.run_scoped(both, *[
            pltpu.ACC(mxu_id=u)((CHUNK, n), f32) for _ in range(2) for u in range(2) for _ in range(n // CHUNK)
        ])
        return carry

    for s in range(2):
        @pl.when(live > s)
        def _():
            for copy in inputs(s):
                copy.start()
    lax.fori_loop(0, lax.div(live + 1, 2), step, 0)
    store = pltpu.make_async_copy(total.at[:, :, :dump], out, outsem)
    store.start()
    store.wait()


def gradient(count, slot, row, col, field, images, fars, waves, probe, tables):
    planes, cols, rows, width = field.shape
    n = probe.shape[1]
    return pl.pallas_call(
        grad_kernel,
        out_shape=jax.ShapeDtypeStruct(field.shape, f32),
        in_specs=[smem] * 4 + [vmem] + [anyspace] * 3 + [vmem] * 7,
        out_specs=anyspace,
        scratch_shapes=[
            pltpu.VMEM((planes, cols, rows + n, width), f32),
            pltpu.VMEM((2, 2, n, n), bf16),
            pltpu.VMEM((2, n, 2 * n), bf16),
            pltpu.VMEM((2, 2 * n, n), bf16),
            pltpu.VMEM((4, 2 * n, n), f32),
            pltpu.VMEM((4, n, 2 * n), f32),
            pltpu.VMEM((2, 2, n, width), f32),
            pltpu.VMEM((4, n, n), bf16),
            pltpu.SemaphoreType.DMA((4, 3)),
            pltpu.SemaphoreType.DMA,
        ],
        compiler_params=pltpu.CompilerParams(vmem_limit_bytes=VMEM_LIMIT),
        name="gradient",
    )(
        count, slot, row, col, field, images, fars, waves, probe, tables["right_forward"], tables["right_inverse"],
        tables["right_back"], tables["left_forward"], tables["left_inverse"], tables["kernel"],
    )


def reduce_kernel(tiles, slabs, cores, total, unsort, out, part, near, far, outgoing,
                  localsem, csend, crecv, zsend, zrecv, fsend, frecv):
    tile = lax.axis_index("tile")
    slab = lax.axis_index("slab")
    levels = slabs // cores
    core = lax.rem(slab, cores)
    level = lax.div(slab, cores)
    other = level * cores + (1 - core)
    following = lax.rem(tile + 1, tiles)
    preceding = lax.rem(tile + tiles - 1, tiles)
    barrier = pltpu.get_barrier_semaphore()

    def greet(t, s):
        pl.semaphore_signal(barrier, inc=1, device_id={"tile": t, "slab": s}, device_id_type=MESH)

    greet(tile, other)
    for d in range(1, levels):
        greet(tile, lax.rem(level + d, levels) * cores + core)
    for d in range(levels):
        place = lax.rem(level + d, levels) * cores + core
        greet(following, place)
        greet(preceding, place)
    pl.semaphore_wait(barrier, 1 + levels - 1 + 2 * levels)

    def block(which, d):
        return which * levels + lax.rem(level + d, levels)

    order = [(1, 2), (1, 1), (1, 3), (0, 2), (0, 1), (0, 3), (1, 0), (0, 0)]
    swaps = []
    takes = []
    for k, (which, d) in enumerate(order):
        b = block(which, d)
        copy = pltpu.make_async_remote_copy(
            src_ref=total.at[:, :, b, 1 - core], dst_ref=near.at[k], send_sem=csend.at[k], recv_sem=crecv.at[k],
            device_id={"tile": tile, "slab": other}, device_id_type=MESH,
        )
        copy.start()
        swaps.append(copy)
        take = pltpu.make_async_copy(total.at[:, :, b, core], part.at[k], localsem.at[k])
        take.start()
        takes.append(take)
    sends = []
    for k, (which, d) in enumerate(order):
        takes[k].wait()
        swaps[k].wait_recv()
        if (which, d) == (0, 0):
            continue
        outgoing[k] = (part[k] + near[k]).astype(bf16)
        place = lax.rem(level + d, levels) * cores + core
        if which == 0:
            copy = pltpu.make_async_remote_copy(
                src_ref=outgoing.at[k], dst_ref=far.at[d - 1], send_sem=zsend.at[d - 1], recv_sem=zrecv.at[d - 1],
                device_id={"tile": tile, "slab": place}, device_id_type=MESH,
            )
        else:
            copy = pltpu.make_async_remote_copy(
                src_ref=outgoing.at[k], dst_ref=far.at[levels - 1 + d], send_sem=fsend.at[d], recv_sem=frecv.at[d],
                device_id={"tile": following, "slab": place}, device_id_type=MESH,
            )
        copy.start()
        sends.append(copy)
    for copy in sends:
        copy.wait()
    for copy in swaps:
        copy.wait_send()
    last = len(order) - 1
    for p in range(4):
        for h in range(3):
            value = part[last, p, h] + near[last, p, h]
            for k in range(2 * levels - 1):
                value = value + far[k, p, h].astype(f32)
            out[p // 2, p % 2, :, lanes(h)] = rearrange(value, unsort[...])


def reduce(total, tiles, slabs):
    cores = 2
    levels = slabs // cores
    planes, cols, rows, lanes = total.shape
    each = rows // (2 * slabs)
    sem = pltpu.SemaphoreType.DMA
    count = 2 * levels
    total = total.reshape(planes, cols, rows // (cores * each), cores, each, lanes)
    return pl.pallas_call(
        functools.partial(reduce_kernel, tiles, slabs, cores),
        out_shape=jax.ShapeDtypeStruct((2, 2, each, cols * lanes), f32),
        in_specs=[anyspace, vmem],
        out_specs=vmem,
        scratch_shapes=[
            pltpu.VMEM((count, planes, cols, each, lanes), f32),
            pltpu.VMEM((count, planes, cols, each, lanes), f32),
            pltpu.VMEM((count - 1, planes, cols, each, lanes), bf16),
            pltpu.VMEM((count, planes, cols, each, lanes), bf16),
            sem((count,)),
            sem((count,)), sem((count,)),
            sem((levels - 1,)), sem((levels - 1,)),
            sem((levels,)), sem((levels,)),
        ],
        compiler_params=pltpu.CompilerParams(collective_id=1, has_side_effects=True, vmem_limit_bytes=VMEM_LIMIT),
        name="reduce",
    )(total, lane_order().T)


def shards(intensities, object_field, probe_wave, owner_tile, row_offset, col_offset):
    tiles = lax.axis_size("tile")
    slabs = lax.axis_size("slab")
    pick, count, slot, row, col = route(
        owner_tile, row_offset, col_offset, intensities.shape[0], tiles, slabs
    )
    tables = make_tables(intensities.shape[1])
    images, field, fars, waves, probe = exchange(
        intensities, object_field, probe_wave, pick, row, col, tables, tiles, slabs
    )
    total = gradient(count, slot, row, col, field, images, fars, waves, probe, tables)
    return reduce(total, tiles, slabs)


def solution(mesh):
    placed = (
        P(("tile", "slab"), None, None),
        P(None, None, ("tile", "slab"), None),
        P(),
        P(),
        P(),
        P(),
    )
    return jax.shard_map(
        shards,
        mesh=mesh,
        in_specs=placed,
        out_specs=P(None, None, ("tile", "slab"), None),
        check_vma=False,
    )
```

```python
import functools
import math

import jax
import jax.numpy as jnp
import numpy as np
from jax import lax
from jax.experimental import pallas as pl
from jax.experimental.pallas import tpu as pltpu
from jax.sharding import PartitionSpec as P

bf16 = jnp.bfloat16
f32 = jnp.float32
MESH = pl.DeviceIdType.MESH
K = 16
CAP = 2
COL_STEP = 128
CHIRP = 40.0
LANES = 128
HALF = 64
CHUNK = 16
VMEM_LIMIT = 60 * 2**20

smem = pl.BlockSpec(memory_space=pltpu.SMEM)
vmem = pl.BlockSpec(memory_space=pltpu.VMEM)
anyspace = pl.BlockSpec(memory_space=pl.ANY)


def make_tables(n):
    count = np.arange(n)
    angles = ((count[:, None] * count[None, :]) % n).astype(np.float32)
    angles = angles * np.float32(2.0 * math.pi / n)
    scale = np.float32(1.0 / math.sqrt(n))
    c = (np.cos(angles) * scale).astype(np.float32)
    s = (np.sin(angles) * scale).astype(np.float32)
    even = np.arange(0, n, 2)
    odd = even + 1
    low = np.concatenate([even[: n // 4], odd[: n // 4]])
    near = np.arange(n // 2)

    def left(sign, inputs):
        cc = c[np.ix_(low, inputs)]
        ss = s[np.ix_(low, inputs)] * np.float32(sign)
        return np.block([[cc, ss], [-ss, cc]])

    def right(sign, inputs, outputs):
        cc = c[np.ix_(inputs, outputs)]
        ss = s[np.ix_(inputs, outputs)] * np.float32(sign)
        return np.block([[cc, -ss], [ss, cc]])

    f = (((count + n // 2) % n) - n // 2).astype(np.float32) / np.float32(n)
    phases = np.float32(CHIRP) * (f[:, None] ** 2 + f[None, :] ** 2)
    kernel = np.stack([np.cos(phases), -np.sin(phases)]).astype(np.float32)
    kernel = kernel[:, np.concatenate([even, odd]), :][:, :, np.concatenate([low, low + n // 2])]

    def low_precision(a):
        return jnp.asarray(a.astype(np.float32), bf16)

    return dict(
        left_forward=low_precision(np.stack([left(1, even), left(1, odd)])),
        left_inverse=low_precision(np.stack([left(-1, even), left(-1, odd)])),
        right_forward=low_precision(np.stack([right(1, even, low), right(1, odd, low)])),
        right_inverse=low_precision(np.stack([right(-1, even, low), right(-1, odd, low)])),
        right_far=low_precision(np.stack([right(1, even, near), right(1, odd, near)])),
        right_back=low_precision(np.concatenate([right(-1, count, low), right(-1, count, low + n // 2)], 1)),
        kernel=jnp.asarray(kernel),
    )


def lane_order():
    order = np.concatenate([np.arange(0, LANES, 2), np.arange(1, LANES, 2)])
    return jnp.asarray(order[None, :] == np.arange(LANES)[:, None], bf16)


def rearrange(value, order):
    high = value.astype(bf16)
    rest = value - high.astype(f32)
    middle = rest.astype(bf16)
    low = (rest - middle.astype(f32)).astype(bf16)
    parts = [jnp.dot(part, order, preferred_element_type=f32) for part in (high, middle, low)]
    return parts[0] + (parts[1] + parts[2])


def route_kernel(tiles, slabs, reads, owner, rowoff, coloff, pick, count, slot, row, col, used):
    tile = lax.axis_index("tile")
    slab = lax.axis_index("slab")
    for t in range(tiles):
        used[t] = 0
    for k in range(tiles * CAP):
        pick[k] = 0
    for k in range(K + 1):
        slot[k] = 0
        row[k] = 0
        col[k] = 0
    for k in range(reads):
        dest = owner[(tile * slabs + slab) * reads + k]
        rank = used[dest]
        used[dest] = rank + 1
        pick[dest * CAP + rank] = k

    def sender(i, found):
        base = (i * slabs + slab) * reads

        def one(k, state):
            n, rank = state
            hit = owner[base + k] == tile
            slot[n] = jnp.where(hit, i * CAP + rank, 0)
            row[n] = rowoff[base + k]
            col[n] = coloff[base + k]
            step = hit.astype(jnp.int32)
            return n + step, rank + step

        return lax.fori_loop(0, reads, one, (found, jnp.int32(0)), unroll=True)[0]

    count[0] = lax.fori_loop(0, tiles, sender, jnp.int32(0))


def route(owner, rowoff, coloff, reads, tiles, slabs):
    sizes = (tiles * CAP, 1, K + 1, K + 1, K + 1)
    return pl.pallas_call(
        functools.partial(route_kernel, tiles, slabs, reads),
        out_shape=tuple(jax.ShapeDtypeStruct((size,), jnp.int32) for size in sizes),
        in_specs=[smem, smem, smem],
        out_specs=(smem,) * 5,
        scratch_shapes=[pltpu.SMEM((tiles,), jnp.int32)],
        name="route",
    )(owner, rowoff, coloff)


def product(ar, ai, br, bi):
    return ar * br - ai * bi, ar * bi + ai * br


def conjugate_product(ar, ai, br, bi):
    return ar * br + ai * bi, ar * bi - ai * br


def lanes(c):
    return slice(c * LANES, (c + 1) * LANES)


def rows_of(p, b, r):
    start = 2 * HALF * p + HALF * b + r
    return slice(start, start + CHUNK)


def spread_rows(start, p, b, r):
    return pl.ds(start + p + 2 * HALF * b + 2 * r, CHUNK, stride=2)


def window(field, s, top, left, p, b, r, c):
    where = spread_rows(top, p, b, r)
    return field[2 * s, left + c, where, :], field[2 * s + 1, left + c, where, :]


def put_natural(x, p, b, r, parts):
    for c in range(2):
        for q in range(2):
            x[rows_of(p, b, r), lanes(2 * q + c)] = parts[c][q].astype(bf16)


def put(x, p, b, r, parts):
    low = lax.broadcasted_iota(jnp.int32, (CHUNK, LANES), 1) < HALF
    for q in range(2):
        near, far = parts[0][q], parts[1][q]
        even = jnp.where(low, near, pltpu.roll(far, HALF, 1))
        odd = jnp.where(low, pltpu.roll(near, HALF, 1), far)
        x[0, rows_of(p, b, r), lanes(q)] = even.astype(bf16)
        x[1, rows_of(p, b, r), lanes(q)] = odd.astype(bf16)


def chirp(kernel, p, b, r, c):
    return kernel[0, rows_of(p, b, r), lanes(c)], kernel[1, rows_of(p, b, r), lanes(c)]


def lit(probe, p, b, r, c):
    where = spread_rows(0, p, b, r)
    return probe[c, where, :], probe[2 + c, where, :]


def each(y, use):
    for p in range(2):
        for r in range(0, HALF, CHUNK):
            e = [[y[HALF * k + r:HALF * k + r + CHUNK, lanes(c)] for k in (p, 2 + p)] for c in range(2)]
            o = [[y[HALF * k + r:HALF * k + r + CHUNK, lanes(c)] for k in (4 + p, 6 + p)] for c in range(2)]
            use(p, 0, r, [(e[c][0] + o[c][0], e[c][1] + o[c][1]) for c in range(2)])
            use(p, 1, r, [(e[c][0] - o[c][0], e[c][1] - o[c][1]) for c in range(2)])


def finish_transform(h, y, low, high, left):
    n = 4 * HALF
    m = n // 2
    for p in range(2):
        for q in range(2):
            where = slice(p * n + q * m, p * n + q * m + m)
            h[where, lanes(0)] = low[p * m:p * m + m, lanes(q)].astype(bf16)
            h[where, lanes(1)] = high[p * m:p * m + m, lanes(q)].astype(bf16)
    y[:n, :] = jnp.dot(left[0], h[:n, :], preferred_element_type=f32)
    y[n:, :] = jnp.dot(left[1], h[n:, :], preferred_element_type=f32)


def transform(x, h, y, right, left):
    even = jnp.dot(x[0], right[0], preferred_element_type=f32)
    odd = jnp.dot(x[1], right[1], preferred_element_type=f32)
    finish_transform(h, y, even + odd, even - odd, left)


def transform_natural(x, h, y, right, left):
    n = 4 * HALF
    half = jnp.dot(x[...], right[...], preferred_element_type=f32)
    finish_transform(h, y, half[:, :n], half[:, n:], left)


def interleave(first, second, transforms):
    first[0]()
    for t in range(transforms):
        first[2 * t + 1]()
        second[2 * t]()
        second[2 * t + 1]()
        first[2 * t + 2]()
    second[2 * transforms]()


XORDER = (1, 3, 2)
RELAY_STEPS = ((1, slice(3, 5)), (2, slice(5, 6)), (3, slice(6, 7)), (4, slice(7, 8)), (5, slice(8, 9)))
YORDER = (2, 1, 3)


def exchange_kernel(tiles, slabs, cores, rows, images, block_in, light, sort, pick, row, col,
                    right_forward, right_inverse, right_far, left_forward, left_inverse, kernel,
                    got, field_out, fars, waves, probe,
                    field, x, h, y, far, wave, pictures, packed, shard, localsem, outsem, insem,
                    stage, xsend, xrecv, ysend, yrecv, nsend, nrecv, zsend, zrecv, csend, crecv):
    tile = lax.axis_index("tile")
    slab = lax.axis_index("slab")
    levels = slabs // cores
    core = lax.rem(slab, cores)
    level = lax.div(slab, cores)
    other = level * cores + (1 - core)
    before = lax.rem(tile + tiles - 1, tiles)
    side = math.isqrt(tiles)
    barrier = pltpu.get_barrier_semaphore()

    def greet(t, s):
        pl.semaphore_signal(barrier, inc=1, device_id={"tile": t, "slab": s}, device_id_type=MESH)

    for d in range(1, tiles):
        greet(lax.rem(tile + d, tiles), slab)
    for d in range(1, levels):
        greet(tile, lax.rem(level + d, levels) * cores + core)
    greet(tile, other)
    reads = images.shape[0]
    loads = [pltpu.make_async_copy(images.at[k], pictures.at[k], insem.at[k]) for k in range(reads)]
    for load in loads:
        load.start()
    for s in range(2):
        for q in range(2):
            for c in range(3):
                shard[2 * s + q, c] = rearrange(block_in[s, q, :, lanes(c)], sort[...])
    for load in loads:
        load.wait()

    def fill(t, carry):
        for k in range(CAP):
            packed[t, k] = pictures[pick[t * CAP + k]]
        return carry

    lax.fori_loop(0, tiles, fill, 0)
    pl.semaphore_wait(barrier, tiles + levels - 1)

    height = rows * slabs

    def block(which, s):
        return field.at[:, :, pl.ds(pl.multiple_of(which * height + s * rows, rows), rows), :]

    copies = []
    rims = []

    def make(src, dst, send, recv, t, s):
        copy = pltpu.make_async_remote_copy(
            src_ref=src, dst_ref=dst, send_sem=send, recv_sem=recv,
            device_id={"tile": t, "slab": s}, device_id_type=MESH,
        )
        copies.append(copy)
        return copy

    def push(*parts):
        copy = make(*parts)
        copy.start()
        return copy

    def share(which, src, k):
        mine = block(which, slab)
        links = []
        for d in (2, 1, 3)[: levels - 1]:
            place = lax.rem(level + d, levels) * cores + core
            links.append((d, push(src, mine, zsend.at[which, d - 1], zrecv.at[which, d - 1], tile, place)))
        rims.append(push(src, mine, csend.at[which, 0], crecv.at[which, 0], tile, other))
        return links

    def pass_on(which, links):
        for d, copy in links:
            copy.wait_recv()
            s = lax.rem(level + levels - d, levels) * cores + core
            rims.append(push(block(which, s), block(which, s), csend.at[which, d], crecv.at[which, d], tile, other))

    ahead = push(shard, block(1, slab), nsend, nrecv, before, slab)
    own = share(0, shard, 0)
    grid_row, grid_col = lax.div(tile, side), lax.rem(tile, side)

    def at(dy, dx):
        return lax.rem(grid_row + dy + side, side) * side + lax.rem(grid_col + dx + side, side)

    steps = XORDER
    for dy in YORDER:
        push(packed.at[at(dy, 0)], got.at[tile], ysend.at[0, dy - 1], yrecv.at[0, dy - 1], at(dy, 0), slab)
    relays = []
    for dy in YORDER:
        for dx in steps:
            copy = push(packed.at[at(dy, dx)], stage.at[dy - 1, dx - 1], xsend.at[dy, dx - 1], xrecv.at[dy, dx - 1], at(0, dx), slab)
            relays.append((dy, dx, copy))
    for dx in steps:
        push(packed.at[at(0, dx)], got.at[tile], xsend.at[0, dx - 1], xrecv.at[0, dx - 1], at(0, dx), slab)
    keep = pltpu.make_async_copy(shard, block(0, slab), localsem.at[0])
    keep.start()
    second = pltpu.make_async_copy(packed.at[tile], got.at[tile], localsem.at[1])
    second.start()
    for g in range(4):
        probe[g] = rearrange(light[:, lanes(g)], sort[...])
    ahead.wait_recv()
    following = share(1, block(1, slab), 1)
    def relay(part):
        for (dy, dx, copy), onward in part:
            copy.wait_recv()
            onward.start()

    onwards = [
        make(stage.at[dy - 1, dx - 1], got.at[at(0, -dx)], ysend.at[dx, dy - 1], yrecv.at[dx, dy - 1], at(dy, 0), slab)
        for dy, dx, _ in relays
    ]
    relays = list(zip(relays, onwards))

    pass_on(0, own)
    relay(relays[:3])
    pass_on(1, following)
    done = [id(c) for _, c in own + following] + [id(ahead)] + [id(r[2]) for r, _ in relays]
    for copy in rims:
        copy.wait_recv()
        done.append(id(copy))
    keep.wait()
    store = pltpu.make_async_copy(field, field_out, localsem.at[0])
    store.start()

    def outputs(k, j):
        turn = lax.rem(k, 2)
        return (
            pltpu.make_async_copy(far.at[turn, j], fars.at[2 * k + j], outsem.at[turn, j, 0]),
            pltpu.make_async_copy(wave.at[turn, j], waves.at[2 * k + j], outsem.at[turn, j, 1]),
        )

    def pattern(k, j):
        top = row[2 * k + j]
        left = col[2 * k + j]
        turn = lax.rem(k, 2)
        xj, hj, yj, fj, wj = x.at[j], h.at[j], y.at[j], far.at[turn, j], wave.at[turn, j]

        def begin():
            for p in range(2):
                for b in range(2):
                    for r in range(0, HALF, CHUNK):
                        put(xj, p, b, r, [
                            product(*lit(probe, p, b, r, c), *window(field, 0, top, left, p, b, r, c)) for c in range(2)
                        ])

        def scatter(p, b, r, parts):
            put(xj, p, b, r, [product(*chirp(kernel, p, b, r, c), *parts[c]) for c in range(2)])

        def enter(p, b, r, parts):
            for c in range(2):
                wj[rows_of(p, b, r), lanes(c)] = parts[c][0]
                wj[rows_of(p, b, r), lanes(2 + c)] = parts[c][1]
            put(xj, p, b, r, [product(*parts[c], *window(field, 1, top, left, p, b, r, c)) for c in range(2)])

        return [
            begin, lambda: transform(xj, hj, yj, right_forward, left_forward), lambda: each(yj, scatter),
            lambda: transform(xj, hj, yj, right_inverse, left_inverse), lambda: each(yj, enter),
            lambda: transform(xj, hj, fj, right_far, left_forward), lambda: None,
        ]

    def step(k, carry):
        @pl.when(k >= 2)
        def _():
            for j in range(2):
                for copy in outputs(k - 2, j):
                    copy.wait()

        interleave(pattern(k, 0), pattern(k, 1), 3)
        for j in range(2):
            for copy in outputs(k, j):
                copy.start()

        for when, part in RELAY_STEPS:
            @pl.when(k == when)
            def _():
                relay(relays[part])

        return carry

    pairs = K // 2
    lax.fori_loop(0, pairs, step, 0)
    for k in (pairs - 2, pairs - 1):
        for j in range(2):
            for copy in outputs(k, j):
                copy.wait()
    store.wait()
    second.wait()
    for copy in copies:
        copy.wait_send()
        if id(copy) not in done:
            copy.wait_recv()


def exchange(images, block, light, pick, row, col, tables, tiles, slabs):
    reads, n, _ = images.shape
    rows = block.shape[2]
    planes, cols, width = 4, block.shape[3] // LANES, LANES
    cores = 2
    levels = slabs // cores
    side = math.isqrt(tiles)
    sem = pltpu.SemaphoreType.DMA
    extended = (planes, cols, 2 * rows * slabs, width)
    return pl.pallas_call(
        functools.partial(exchange_kernel, tiles, slabs, cores, rows),
        out_shape=(
            jax.ShapeDtypeStruct((tiles, CAP, n, n), bf16),
            jax.ShapeDtypeStruct(extended, f32),
            jax.ShapeDtypeStruct((K, 2 * n, n), f32),
            jax.ShapeDtypeStruct((K, n, 2 * n), f32),
            jax.ShapeDtypeStruct((4, n, width), f32),
        ),
        in_specs=[anyspace, vmem, vmem, vmem, smem, smem, smem] + [vmem] * 6,
        out_specs=(anyspace,) * 4 + (vmem,),
        scratch_shapes=[
            pltpu.VMEM(extended, f32),
            pltpu.VMEM((2, 2, n, n), bf16),
            pltpu.VMEM((2, 2 * n, n), bf16),
            pltpu.VMEM((2, 2 * n, n), f32),
            pltpu.VMEM((2, 2, 2 * n, n), f32),
            pltpu.VMEM((2, 2, n, 2 * n), f32),
            pltpu.VMEM((reads, n, n), bf16),
            pltpu.VMEM((tiles, CAP, n, n), bf16),
            pltpu.VMEM((planes, cols, rows, width), f32),
            sem((2,)),
            sem((2, 2, 2)),
            sem((reads,)),
            pltpu.VMEM((side - 1, side - 1, CAP, n, n), bf16),
            sem((side, side - 1)), sem((side, side - 1)),
            sem((side, side - 1)), sem((side, side - 1)),
            sem, sem,
            sem((2, levels - 1)), sem((2, levels - 1)),
            sem((2, levels)), sem((2, levels)),
        ],
        compiler_params=pltpu.CompilerParams(collective_id=0, has_side_effects=True, vmem_limit_bytes=VMEM_LIMIT),
        name="exchange",
    )(
        images, block, light, lane_order(), pick, row, col,
        tables["right_forward"], tables["right_inverse"], tables["right_far"],
        tables["left_forward"], tables["left_inverse"], tables["kernel"],
    )


def together(*groups):
    steps = max(len(group) for group in groups)
    for i in range(steps):
        for group in groups[::-1]:
            for unit in group[i * len(group) // steps:(i + 1) * len(group) // steps]:
                unit()


def each_part(y, use, p, r):
    e = [[y[HALF * k + r:HALF * k + r + CHUNK, lanes(c)] for k in (p, 2 + p)] for c in range(2)]
    o = [[y[HALF * k + r:HALF * k + r + CHUNK, lanes(c)] for k in (4 + p, 6 + p)] for c in range(2)]
    use(p, 0, r, [(e[c][0] + o[c][0], e[c][1] + o[c][1]) for c in range(2)])
    use(p, 1, r, [(e[c][0] - o[c][0], e[c][1] - o[c][1]) for c in range(2)])


def grad_kernel(count, slot, row, col, field, images, fars, waves, probe, right_forward, right_inverse, right_back, left_forward, left_inverse, kernel,
                out, total, x, xfull, h, far, wave, measured, image, insem, outsem):
    dump = field.shape[2]
    total[...] = jnp.zeros_like(total)
    live = count[0]

    def inputs(i):
        index = slot[i]
        place = lax.rem(i, 4)
        return (
            pltpu.make_async_copy(images.at[lax.div(index, CAP), lax.rem(index, CAP)], image.at[place], insem.at[place, 0]),
            pltpu.make_async_copy(fars.at[i], far.at[place], insem.at[place, 1]),
            pltpu.make_async_copy(waves.at[i], wave.at[place], insem.at[place, 2]),
        )

    def pattern(i, j, valid, accs):
        top = row[i]
        left = col[i]
        place = top if valid is None else jnp.where(valid, top, dump)
        at = lax.rem(i, 4)
        xj, xf, hj, mj = x.at[j], xfull.at[j], h.at[j], measured.at[j]
        wj, fj, source = wave.at[at], far.at[at], image.at[at]

        def add(s, p, b, r, parts):
            where = spread_rows(place, p, b, r)
            for c in range(2):
                total[2 * s, left + c, where, :] += parts[c][0]
                total[2 * s + 1, left + c, where, :] += parts[c][1]

        def compare(p, b, r, parts):
            scaled = []
            for c in range(2):
                re, im = parts[c]
                misfit = re * re + im * im - mj[c, spread_rows(0, p, b, r), :]
                scaled.append((re * misfit, im * misfit))
            put_natural(xf, p, b, r, scaled)

        def leave(p, b, r, parts):
            where = rows_of(p, b, r)
            add(1, p, b, r, [conjugate_product(wj[where, lanes(c)], wj[where, lanes(2 + c)], *parts[c]) for c in range(2)])
            put(xj, p, b, r, [conjugate_product(*window(field, 1, top, left, p, b, r, c), *parts[c]) for c in range(2)])

        def gather(p, b, r, parts):
            put(xj, p, b, r, [conjugate_product(*chirp(kernel, p, b, r, c), *parts[c]) for c in range(2)])

        def finish(p, b, r, parts):
            add(0, p, b, r, [conjugate_product(*lit(probe, p, b, r, c), *parts[c]) for c in range(2)])

        n = 4 * HALF
        units = n // CHUNK
        acc = [accs[(2 * j + u) * units:(2 * j + u + 1) * units] for u in range(2)]

        def compare_units():
            def convert():
                for c in range(2):
                    mj[c] = source[:, lanes(c)].astype(f32)

            return [convert] + [functools.partial(each_part, fj, compare, p, r) for p in range(2) for r in range(0, HALF, CHUNK)]

        def push(first, second):
            pltpu.matmul_push_rhs(first, j, 0)
            pltpu.matmul_push_rhs(second, j, 1)

        def feed(i, first, second, load):
            pltpu.matmul_acc_lhs(acc[0][i], first, j if load else None)
            pltpu.matmul_acc_lhs(acc[1][i], second, j if load else None)

        def rows(i):
            return slice(i * CHUNK, (i + 1) * CHUNK)

        def right_units(right):
            def unit(i):
                if i == 0:
                    push(right[0], right[1])
                feed(i, xj[0, rows(i), :], xj[1, rows(i), :], i == 0)

            return [functools.partial(unit, i) for i in range(units)]

        def back_units():
            def unit(t, i):
                if i == 0:
                    push(right_back[t * n:(t + 1) * n, :n], right_back[t * n:(t + 1) * n, n:])
                part = xf[rows(i), t * n:(t + 1) * n]
                feed(i, part, part, i == 0)

            return [functools.partial(unit, t, i) for t in range(2) for i in range(units)]

        def half_units(split):
            def unit(i):
                low = pltpu.matmul_pop(acc[0][i])
                high = pltpu.matmul_pop(acc[1][i])
                if split:
                    low, high = low + high, low - high
                m = n // 2
                p, start = divmod(i * CHUNK, m)
                for q in range(2):
                    where = slice(p * n + q * m + start, p * n + q * m + start + CHUNK)
                    hj[where, lanes(0)] = low[:, lanes(q)].astype(bf16)
                    hj[where, lanes(1)] = high[:, lanes(q)].astype(bf16)

            return [functools.partial(unit, i) for i in range(units)]

        order = [(p, r) for p in range(2) for r in range(0, HALF, CHUNK)]

        def left_units(left):
            def unit(i):
                if i == 0:
                    push(hj[:n, :], hj[n:, :])
                p, r = order[i // 2]
                start = (i % 2) * 2 * HALF + p * HALF + r
                feed(i, left[0, start:start + CHUNK, :], left[1, start:start + CHUNK, :], i == 0)

            return [functools.partial(unit, i) for i in range(units)]

        def use_units(use):
            def unit(i):
                p, r = order[i]
                e = [pltpu.matmul_pop(acc[0][2 * i + q]) for q in range(2)]
                o = [pltpu.matmul_pop(acc[1][2 * i + q]) for q in range(2)]
                use(p, 0, r, [(e[0][:, lanes(c)] + o[0][:, lanes(c)], e[1][:, lanes(c)] + o[1][:, lanes(c)]) for c in range(2)])
                use(p, 1, r, [(e[0][:, lanes(c)] - o[0][:, lanes(c)], e[1][:, lanes(c)] - o[1][:, lanes(c)]) for c in range(2)])

            return [functools.partial(unit, i) for i in range(len(order))]

        return compare_units(), [
            (back_units(), half_units(False)), (left_units(left_inverse), use_units(leave)),
            (right_units(right_forward), half_units(True)), (left_units(left_forward), use_units(gather)),
            (right_units(right_inverse), half_units(True)), (left_units(left_inverse), use_units(finish)),
        ]

    def step(k, carry):
        a = 2 * k
        b = jnp.minimum(2 * k + 1, live - 1)
        valid = 2 * k + 1 < live
        for copy in inputs(a):
            copy.wait()

        @pl.when(valid)
        def _():
            for copy in inputs(2 * k + 1):
                copy.wait()

        for ahead in (2, 3):
            @pl.when(2 * k + ahead < live)
            def _():
                for copy in inputs(2 * k + ahead):
                    copy.start()

        def both(*accs):
            first_compare, first = pattern(a, 0, None, accs)
            second_compare, second = pattern(b, 1, valid, accs)
            together(first_compare)
            together(first[0][0], second_compare)
            for s in range(len(first)):
                together(second[s][0], first[s][1])
                together(first[s + 1][0] if s + 1 < len(first) else [], second[s][1])

        n = 4 * HALF
        pl.run_scoped(both, *[
            pltpu.ACC(mxu_id=u)((CHUNK, n), f32) for _ in range(2) for u in range(2) for _ in range(n // CHUNK)
        ])
        return carry

    for s in range(2):
        @pl.when(live > s)
        def _():
            for copy in inputs(s):
                copy.start()
    lax.fori_loop(0, lax.div(live + 1, 2), step, 0)
    store = pltpu.make_async_copy(total.at[:, :, :dump], out, outsem)
    store.start()
    store.wait()


def gradient(count, slot, row, col, field, images, fars, waves, probe, tables):
    planes, cols, rows, width = field.shape
    n = probe.shape[1]
    return pl.pallas_call(
        grad_kernel,
        out_shape=jax.ShapeDtypeStruct(field.shape, f32),
        in_specs=[smem] * 4 + [vmem] + [anyspace] * 3 + [vmem] * 7,
        out_specs=anyspace,
        scratch_shapes=[
            pltpu.VMEM((planes, cols, rows + n, width), f32),
            pltpu.VMEM((2, 2, n, n), bf16),
            pltpu.VMEM((2, n, 2 * n), bf16),
            pltpu.VMEM((2, 2 * n, n), bf16),
            pltpu.VMEM((4, 2 * n, n), f32),
            pltpu.VMEM((4, n, 2 * n), f32),
            pltpu.VMEM((2, 2, n, width), f32),
            pltpu.VMEM((4, n, n), bf16),
            pltpu.SemaphoreType.DMA((4, 3)),
            pltpu.SemaphoreType.DMA,
        ],
        compiler_params=pltpu.CompilerParams(vmem_limit_bytes=VMEM_LIMIT),
        name="gradient",
    )(
        count, slot, row, col, field, images, fars, waves, probe, tables["right_forward"], tables["right_inverse"],
        tables["right_back"], tables["left_forward"], tables["left_inverse"], tables["kernel"],
    )


def reduce_kernel(tiles, slabs, cores, total, unsort, out, part, near, far, outgoing,
                  localsem, csend, crecv, zsend, zrecv, fsend, frecv):
    tile = lax.axis_index("tile")
    slab = lax.axis_index("slab")
    levels = slabs // cores
    core = lax.rem(slab, cores)
    level = lax.div(slab, cores)
    other = level * cores + (1 - core)
    following = lax.rem(tile + 1, tiles)
    preceding = lax.rem(tile + tiles - 1, tiles)
    barrier = pltpu.get_barrier_semaphore()

    def greet(t, s):
        pl.semaphore_signal(barrier, inc=1, device_id={"tile": t, "slab": s}, device_id_type=MESH)

    greet(tile, other)
    for d in range(1, levels):
        greet(tile, lax.rem(level + d, levels) * cores + core)
    for d in range(levels):
        place = lax.rem(level + d, levels) * cores + core
        greet(following, place)
        greet(preceding, place)
    def block(which, d):
        return which * levels + lax.rem(level + d, levels)

    order = [(1, 2), (1, 1), (1, 3), (0, 2), (0, 1), (0, 3), (1, 0), (0, 0)]
    takes = []
    for k, (which, d) in enumerate(order):
        take = pltpu.make_async_copy(total.at[:, :, block(which, d), core], part.at[k], localsem.at[k])
        take.start()
        takes.append(take)
    pl.semaphore_wait(barrier, 1 + levels - 1 + 2 * levels)

    swaps = []
    for k, (which, d) in enumerate(order):
        b = block(which, d)
        copy = pltpu.make_async_remote_copy(
            src_ref=total.at[:, :, b, 1 - core], dst_ref=near.at[k], send_sem=csend.at[k], recv_sem=crecv.at[k],
            device_id={"tile": tile, "slab": other}, device_id_type=MESH,
        )
        copy.start()
        swaps.append(copy)
    sends = []
    for k, (which, d) in enumerate(order):
        takes[k].wait()
        swaps[k].wait_recv()
        if (which, d) == (0, 0):
            continue
        outgoing[k] = (part[k] + near[k]).astype(bf16)
        place = lax.rem(level + d, levels) * cores + core
        if which == 0:
            copy = pltpu.make_async_remote_copy(
                src_ref=outgoing.at[k], dst_ref=far.at[d - 1], send_sem=zsend.at[d - 1], recv_sem=zrecv.at[d - 1],
                device_id={"tile": tile, "slab": place}, device_id_type=MESH,
            )
        else:
            copy = pltpu.make_async_remote_copy(
                src_ref=outgoing.at[k], dst_ref=far.at[levels - 1 + d], send_sem=fsend.at[d], recv_sem=frecv.at[d],
                device_id={"tile": following, "slab": place}, device_id_type=MESH,
            )
        copy.start()
        sends.append(copy)
    for copy in sends:
        copy.wait()
    for copy in swaps:
        copy.wait_send()
    last = len(order) - 1
    for p in range(4):
        for h in range(3):
            value = part[last, p, h] + near[last, p, h]
            for k in range(2 * levels - 1):
                value = value + far[k, p, h].astype(f32)
            out[p // 2, p % 2, :, lanes(h)] = rearrange(value, unsort[...])


def reduce(total, tiles, slabs):
    cores = 2
    levels = slabs // cores
    planes, cols, rows, lanes = total.shape
    each = rows // (2 * slabs)
    sem = pltpu.SemaphoreType.DMA
    count = 2 * levels
    total = total.reshape(planes, cols, rows // (cores * each), cores, each, lanes)
    return pl.pallas_call(
        functools.partial(reduce_kernel, tiles, slabs, cores),
        out_shape=jax.ShapeDtypeStruct((2, 2, each, cols * lanes), f32),
        in_specs=[anyspace, vmem],
        out_specs=vmem,
        scratch_shapes=[
            pltpu.VMEM((count, planes, cols, each, lanes), f32),
            pltpu.VMEM((count, planes, cols, each, lanes), f32),
            pltpu.VMEM((count - 1, planes, cols, each, lanes), bf16),
            pltpu.VMEM((count, planes, cols, each, lanes), bf16),
            sem((count,)),
            sem((count,)), sem((count,)),
            sem((levels - 1,)), sem((levels - 1,)),
            sem((levels,)), sem((levels,)),
        ],
        compiler_params=pltpu.CompilerParams(collective_id=1, has_side_effects=True, vmem_limit_bytes=VMEM_LIMIT),
        name="reduce",
    )(total, lane_order().T)


def shards(intensities, object_field, probe_wave, owner_tile, row_offset, col_offset):
    tiles = lax.axis_size("tile")
    slabs = lax.axis_size("slab")
    pick, count, slot, row, col = route(
        owner_tile, row_offset, col_offset, intensities.shape[0], tiles, slabs
    )
    tables = make_tables(intensities.shape[1])
    images, field, fars, waves, probe = exchange(
        intensities, object_field, probe_wave, pick, row, col, tables, tiles, slabs
    )
    total = gradient(count, slot, row, col, field, images, fars, waves, probe, tables)
    return reduce(total, tiles, slabs)


def solution(mesh):
    placed = (
        P(("tile", "slab"), None, None),
        P(None, None, ("tile", "slab"), None),
        P(),
        P(),
        P(),
        P(),
    )
    return jax.shard_map(
        shards,
        mesh=mesh,
        in_specs=placed,
        out_specs=P(None, None, ("tile", "slab"), None),
        check_vma=False,
    )
```

```python
import functools
import math

import jax
import jax.numpy as jnp
import numpy as np
from jax import lax
from jax.experimental import pallas as pl
from jax.experimental.pallas import tpu as pltpu
from jax.sharding import PartitionSpec as P

bf16 = jnp.bfloat16
f32 = jnp.float32
MESH = pl.DeviceIdType.MESH
K = 16
CAP = 2
COL_STEP = 128
CHIRP = 40.0
LANES = 128
HALF = 64
CHUNK = 16
VMEM_LIMIT = 60 * 2**20

smem = pl.BlockSpec(memory_space=pltpu.SMEM)
vmem = pl.BlockSpec(memory_space=pltpu.VMEM)
anyspace = pl.BlockSpec(memory_space=pl.ANY)


def make_tables(n):
    count = np.arange(n)
    angles = ((count[:, None] * count[None, :]) % n).astype(np.float32)
    angles = angles * np.float32(2.0 * math.pi / n)
    scale = np.float32(1.0 / math.sqrt(n))
    c = (np.cos(angles) * scale).astype(np.float32)
    s = (np.sin(angles) * scale).astype(np.float32)
    even = np.arange(0, n, 2)
    odd = even + 1
    low = np.concatenate([even[: n // 4], odd[: n // 4]])
    near = np.arange(n // 2)

    def left(sign, inputs):
        cc = c[np.ix_(low, inputs)]
        ss = s[np.ix_(low, inputs)] * np.float32(sign)
        return np.block([[cc, ss], [-ss, cc]])

    def right(sign, inputs, outputs):
        cc = c[np.ix_(inputs, outputs)]
        ss = s[np.ix_(inputs, outputs)] * np.float32(sign)
        return np.block([[cc, -ss], [ss, cc]])

    f = (((count + n // 2) % n) - n // 2).astype(np.float32) / np.float32(n)
    phases = np.float32(CHIRP) * (f[:, None] ** 2 + f[None, :] ** 2)
    kernel = np.stack([np.cos(phases), -np.sin(phases)]).astype(np.float32)
    kernel = kernel[:, np.concatenate([even, odd]), :][:, :, np.concatenate([low, low + n // 2])]

    def low_precision(a):
        return jnp.asarray(a.astype(np.float32), bf16)

    return dict(
        left_forward=low_precision(np.stack([left(1, even), left(1, odd)])),
        left_inverse=low_precision(np.stack([left(-1, even), left(-1, odd)])),
        right_forward=low_precision(np.stack([right(1, even, low), right(1, odd, low)])),
        right_inverse=low_precision(np.stack([right(-1, even, low), right(-1, odd, low)])),
        right_far=low_precision(np.stack([right(1, even, near), right(1, odd, near)])),
        right_back=low_precision(np.concatenate([right(-1, count, low), right(-1, count, low + n // 2)], 1)),
        kernel=jnp.asarray(kernel),
    )


def lane_order():
    order = np.concatenate([np.arange(0, LANES, 2), np.arange(1, LANES, 2)])
    return jnp.asarray(order[None, :] == np.arange(LANES)[:, None], bf16)


def rearrange(value, order):
    high = value.astype(bf16)
    rest = value - high.astype(f32)
    middle = rest.astype(bf16)
    low = (rest - middle.astype(f32)).astype(bf16)
    parts = [jnp.dot(part, order, preferred_element_type=f32) for part in (high, middle, low)]
    return parts[0] + (parts[1] + parts[2])


def route_kernel(tiles, slabs, reads, owner, rowoff, coloff, pick, count, slot, row, col, used):
    tile = lax.axis_index("tile")
    slab = lax.axis_index("slab")
    for t in range(tiles):
        used[t] = 0
    for k in range(tiles * CAP):
        pick[k] = 0
    for k in range(K + 1):
        slot[k] = 0
        row[k] = 0
        col[k] = 0
    for k in range(reads):
        dest = owner[(tile * slabs + slab) * reads + k]
        rank = used[dest]
        used[dest] = rank + 1
        pick[dest * CAP + rank] = k

    def sender(i, found):
        base = (i * slabs + slab) * reads

        def one(k, state):
            n, rank = state
            hit = owner[base + k] == tile
            slot[n] = jnp.where(hit, i * CAP + rank, 0)
            row[n] = rowoff[base + k]
            col[n] = coloff[base + k]
            step = hit.astype(jnp.int32)
            return n + step, rank + step

        return lax.fori_loop(0, reads, one, (found, jnp.int32(0)), unroll=True)[0]

    count[0] = lax.fori_loop(0, tiles, sender, jnp.int32(0))


def route(owner, rowoff, coloff, reads, tiles, slabs):
    sizes = (tiles * CAP, 1, K + 1, K + 1, K + 1)
    return pl.pallas_call(
        functools.partial(route_kernel, tiles, slabs, reads),
        out_shape=tuple(jax.ShapeDtypeStruct((size,), jnp.int32) for size in sizes),
        in_specs=[smem, smem, smem],
        out_specs=(smem,) * 5,
        scratch_shapes=[pltpu.SMEM((tiles,), jnp.int32)],
        name="route",
    )(owner, rowoff, coloff)


def product(ar, ai, br, bi):
    return ar * br - ai * bi, ar * bi + ai * br


def conjugate_product(ar, ai, br, bi):
    return ar * br + ai * bi, ar * bi - ai * br


def lanes(c):
    return slice(c * LANES, (c + 1) * LANES)


def rows_of(p, b, r):
    start = 2 * HALF * p + HALF * b + r
    return slice(start, start + CHUNK)


def spread_rows(start, p, b, r):
    return pl.ds(start + p + 2 * HALF * b + 2 * r, CHUNK, stride=2)


def window(field, s, top, left, p, b, r, c):
    where = spread_rows(top, p, b, r)
    return field[2 * s, left + c, where, :], field[2 * s + 1, left + c, where, :]


def put_natural(x, p, b, r, parts):
    for c in range(2):
        for q in range(2):
            x[rows_of(p, b, r), lanes(2 * q + c)] = parts[c][q].astype(bf16)


def put(x, p, b, r, parts):
    low = lax.broadcasted_iota(jnp.int32, (CHUNK, LANES), 1) < HALF
    for q in range(2):
        near, far = parts[0][q], parts[1][q]
        even = jnp.where(low, near, pltpu.roll(far, HALF, 1))
        odd = jnp.where(low, pltpu.roll(near, HALF, 1), far)
        x[0, rows_of(p, b, r), lanes(q)] = even.astype(bf16)
        x[1, rows_of(p, b, r), lanes(q)] = odd.astype(bf16)


def chirp(kernel, p, b, r, c):
    return kernel[0, rows_of(p, b, r), lanes(c)], kernel[1, rows_of(p, b, r), lanes(c)]


def lit(probe, p, b, r, c):
    where = spread_rows(0, p, b, r)
    return probe[c, where, :], probe[2 + c, where, :]


def each(y, use):
    for p in range(2):
        for r in range(0, HALF, CHUNK):
            e = [[y[HALF * k + r:HALF * k + r + CHUNK, lanes(c)] for k in (p, 2 + p)] for c in range(2)]
            o = [[y[HALF * k + r:HALF * k + r + CHUNK, lanes(c)] for k in (4 + p, 6 + p)] for c in range(2)]
            use(p, 0, r, [(e[c][0] + o[c][0], e[c][1] + o[c][1]) for c in range(2)])
            use(p, 1, r, [(e[c][0] - o[c][0], e[c][1] - o[c][1]) for c in range(2)])


def finish_transform(h, y, low, high, left):
    n = 4 * HALF
    m = n // 2
    for p in range(2):
        for q in range(2):
            where = slice(p * n + q * m, p * n + q * m + m)
            h[where, lanes(0)] = low[p * m:p * m + m, lanes(q)].astype(bf16)
            h[where, lanes(1)] = high[p * m:p * m + m, lanes(q)].astype(bf16)
    y[:n, :] = jnp.dot(left[0], h[:n, :], preferred_element_type=f32)
    y[n:, :] = jnp.dot(left[1], h[n:, :], preferred_element_type=f32)


def transform(x, h, y, right, left):
    even = jnp.dot(x[0], right[0], preferred_element_type=f32)
    odd = jnp.dot(x[1], right[1], preferred_element_type=f32)
    finish_transform(h, y, even + odd, even - odd, left)


def transform_natural(x, h, y, right, left):
    n = 4 * HALF
    half = jnp.dot(x[...], right[...], preferred_element_type=f32)
    finish_transform(h, y, half[:, :n], half[:, n:], left)


def interleave(first, second, transforms):
    first[0]()
    for t in range(transforms):
        first[2 * t + 1]()
        second[2 * t]()
        second[2 * t + 1]()
        first[2 * t + 2]()
    second[2 * transforms]()


XORDER = (1, 3, 2)
RELAY_STEPS = ((0, slice(3, 4)), (1, slice(4, 6)), (2, slice(6, 7)), (3, slice(7, 8)), (4, slice(8, 9)))
YORDER = (2, 1, 3)


def exchange_kernel(tiles, slabs, cores, rows, images, block_in, light, sort, pick, row, col,
                    right_forward, right_inverse, right_far, left_forward, left_inverse, kernel,
                    got, field_out, fars, waves, probe,
                    field, x, h, y, far, wave, pictures, packed, shard, localsem, outsem, insem,
                    stage, xsend, xrecv, ysend, yrecv, nsend, nrecv, zsend, zrecv, csend, crecv):
    tile = lax.axis_index("tile")
    slab = lax.axis_index("slab")
    levels = slabs // cores
    core = lax.rem(slab, cores)
    level = lax.div(slab, cores)
    other = level * cores + (1 - core)
    before = lax.rem(tile + tiles - 1, tiles)
    side = math.isqrt(tiles)
    barrier = pltpu.get_barrier_semaphore()

    def greet(t, s):
        pl.semaphore_signal(barrier, inc=1, device_id={"tile": t, "slab": s}, device_id_type=MESH)

    for d in range(1, tiles):
        greet(lax.rem(tile + d, tiles), slab)
    for d in range(1, levels):
        greet(tile, lax.rem(level + d, levels) * cores + core)
    greet(tile, other)
    reads = images.shape[0]
    loads = [pltpu.make_async_copy(images.at[k], pictures.at[k], insem.at[k]) for k in range(reads)]
    for load in loads:
        load.start()
    for s in range(2):
        for q in range(2):
            for c in range(3):
                shard[2 * s + q, c] = rearrange(block_in[s, q, :, lanes(c)], sort[...])
    for load in loads:
        load.wait()

    def fill(t, carry):
        for k in range(CAP):
            packed[t, k] = pictures[pick[t * CAP + k]]
        return carry

    lax.fori_loop(0, tiles, fill, 0)
    pl.semaphore_wait(barrier, tiles + levels - 1)

    height = rows * slabs

    def block(which, s):
        return field.at[:, :, pl.ds(pl.multiple_of(which * height + s * rows, rows), rows), :]

    copies = []
    rims = []

    def make(src, dst, send, recv, t, s):
        copy = pltpu.make_async_remote_copy(
            src_ref=src, dst_ref=dst, send_sem=send, recv_sem=recv,
            device_id={"tile": t, "slab": s}, device_id_type=MESH,
        )
        copies.append(copy)
        return copy

    def push(*parts):
        copy = make(*parts)
        copy.start()
        return copy

    def share(which, src, k):
        mine = block(which, slab)
        links = []
        for d in (2, 1, 3)[: levels - 1]:
            place = lax.rem(level + d, levels) * cores + core
            links.append((d, push(src, mine, zsend.at[which, d - 1], zrecv.at[which, d - 1], tile, place)))
        rims.append(push(src, mine, csend.at[which, 0], crecv.at[which, 0], tile, other))
        return links

    def pass_on(which, links):
        for d, copy in links:
            copy.wait_recv()
            s = lax.rem(level + levels - d, levels) * cores + core
            rims.append(push(block(which, s), block(which, s), csend.at[which, d], crecv.at[which, d], tile, other))

    ahead = push(shard, block(1, slab), nsend, nrecv, before, slab)
    own = share(0, shard, 0)
    grid_row, grid_col = lax.div(tile, side), lax.rem(tile, side)

    def at(dy, dx):
        return lax.rem(grid_row + dy + side, side) * side + lax.rem(grid_col + dx + side, side)

    steps = XORDER
    for dy in YORDER:
        push(packed.at[at(dy, 0)], got.at[tile], ysend.at[0, dy - 1], yrecv.at[0, dy - 1], at(dy, 0), slab)
    relays = []
    for dy in YORDER:
        for dx in steps:
            copy = push(packed.at[at(dy, dx)], stage.at[dy - 1, dx - 1], xsend.at[dy, dx - 1], xrecv.at[dy, dx - 1], at(0, dx), slab)
            relays.append((dy, dx, copy))
    for dx in steps:
        push(packed.at[at(0, dx)], got.at[tile], xsend.at[0, dx - 1], xrecv.at[0, dx - 1], at(0, dx), slab)
    keep = pltpu.make_async_copy(shard, block(0, slab), localsem.at[0])
    keep.start()
    second = pltpu.make_async_copy(packed.at[tile], got.at[tile], localsem.at[1])
    second.start()
    for g in range(4):
        probe[g] = rearrange(light[:, lanes(g)], sort[...])
    ahead.wait_recv()
    following = share(1, block(1, slab), 1)
    def relay(part):
        for (dy, dx, copy), onward in part:
            copy.wait_recv()
            onward.start()

    onwards = [
        make(stage.at[dy - 1, dx - 1], got.at[at(0, -dx)], ysend.at[dx, dy - 1], yrecv.at[dx, dy - 1], at(dy, 0), slab)
        for dy, dx, _ in relays
    ]
    relays = list(zip(relays, onwards))

    pass_on(0, own)
    relay(relays[:3])
    pass_on(1, following)
    done = [id(c) for _, c in own + following] + [id(ahead)] + [id(r[2]) for r, _ in relays]
    for copy in rims:
        copy.wait_recv()
        done.append(id(copy))
    keep.wait()
    store = pltpu.make_async_copy(field, field_out, localsem.at[0])
    store.start()

    def outputs(k, j):
        turn = lax.rem(k, 2)
        return (
            pltpu.make_async_copy(far.at[turn, j], fars.at[2 * k + j], outsem.at[turn, j, 0]),
            pltpu.make_async_copy(wave.at[turn, j], waves.at[2 * k + j], outsem.at[turn, j, 1]),
        )

    def pattern(k, j):
        top = row[2 * k + j]
        left = col[2 * k + j]
        turn = lax.rem(k, 2)
        xj, hj, yj, fj, wj = x.at[j], h.at[j], y.at[j], far.at[turn, j], wave.at[turn, j]

        def begin():
            for p in range(2):
                for b in range(2):
                    for r in range(0, HALF, CHUNK):
                        put(xj, p, b, r, [
                            product(*lit(probe, p, b, r, c), *window(field, 0, top, left, p, b, r, c)) for c in range(2)
                        ])

        def scatter(p, b, r, parts):
            put(xj, p, b, r, [product(*chirp(kernel, p, b, r, c), *parts[c]) for c in range(2)])

        def enter(p, b, r, parts):
            for c in range(2):
                wj[rows_of(p, b, r), lanes(c)] = parts[c][0]
                wj[rows_of(p, b, r), lanes(2 + c)] = parts[c][1]
            put(xj, p, b, r, [product(*parts[c], *window(field, 1, top, left, p, b, r, c)) for c in range(2)])

        return [
            begin, lambda: transform(xj, hj, yj, right_forward, left_forward), lambda: each(yj, scatter),
            lambda: transform(xj, hj, yj, right_inverse, left_inverse), lambda: each(yj, enter),
            lambda: transform(xj, hj, fj, right_far, left_forward), lambda: None,
        ]

    def step(k, carry):
        @pl.when(k >= 2)
        def _():
            for j in range(2):
                for copy in outputs(k - 2, j):
                    copy.wait()

        interleave(pattern(k, 0), pattern(k, 1), 3)
        for j in range(2):
            for copy in outputs(k, j):
                copy.start()

        for when, part in RELAY_STEPS:
            @pl.when(k == when)
            def _():
                relay(relays[part])

        return carry

    pairs = K // 2
    lax.fori_loop(0, pairs, step, 0)
    for k in (pairs - 2, pairs - 1):
        for j in range(2):
            for copy in outputs(k, j):
                copy.wait()
    store.wait()
    second.wait()
    for copy in copies:
        copy.wait_send()
        if id(copy) not in done:
            copy.wait_recv()


def exchange(images, block, light, pick, row, col, tables, tiles, slabs):
    reads, n, _ = images.shape
    rows = block.shape[2]
    planes, cols, width = 4, block.shape[3] // LANES, LANES
    cores = 2
    levels = slabs // cores
    side = math.isqrt(tiles)
    sem = pltpu.SemaphoreType.DMA
    extended = (planes, cols, 2 * rows * slabs, width)
    return pl.pallas_call(
        functools.partial(exchange_kernel, tiles, slabs, cores, rows),
        out_shape=(
            jax.ShapeDtypeStruct((tiles, CAP, n, n), bf16),
            jax.ShapeDtypeStruct(extended, f32),
            jax.ShapeDtypeStruct((K, 2 * n, n), f32),
            jax.ShapeDtypeStruct((K, n, 2 * n), f32),
            jax.ShapeDtypeStruct((4, n, width), f32),
        ),
        in_specs=[anyspace, vmem, vmem, vmem, smem, smem, smem] + [vmem] * 6,
        out_specs=(anyspace,) * 4 + (vmem,),
        scratch_shapes=[
            pltpu.VMEM(extended, f32),
            pltpu.VMEM((2, 2, n, n), bf16),
            pltpu.VMEM((2, 2 * n, n), bf16),
            pltpu.VMEM((2, 2 * n, n), f32),
            pltpu.VMEM((2, 2, 2 * n, n), f32),
            pltpu.VMEM((2, 2, n, 2 * n), f32),
            pltpu.VMEM((reads, n, n), bf16),
            pltpu.VMEM((tiles, CAP, n, n), bf16),
            pltpu.VMEM((planes, cols, rows, width), f32),
            sem((2,)),
            sem((2, 2, 2)),
            sem((reads,)),
            pltpu.VMEM((side - 1, side - 1, CAP, n, n), bf16),
            sem((side, side - 1)), sem((side, side - 1)),
            sem((side, side - 1)), sem((side, side - 1)),
            sem, sem,
            sem((2, levels - 1)), sem((2, levels - 1)),
            sem((2, levels)), sem((2, levels)),
        ],
        compiler_params=pltpu.CompilerParams(collective_id=0, has_side_effects=True, vmem_limit_bytes=VMEM_LIMIT),
        name="exchange",
    )(
        images, block, light, lane_order(), pick, row, col,
        tables["right_forward"], tables["right_inverse"], tables["right_far"],
        tables["left_forward"], tables["left_inverse"], tables["kernel"],
    )


def together(*groups):
    steps = max(len(group) for group in groups)
    for i in range(steps):
        for group in groups[::-1]:
            for unit in group[i * len(group) // steps:(i + 1) * len(group) // steps]:
                unit()


def each_part(y, use, p, r):
    e = [[y[HALF * k + r:HALF * k + r + CHUNK, lanes(c)] for k in (p, 2 + p)] for c in range(2)]
    o = [[y[HALF * k + r:HALF * k + r + CHUNK, lanes(c)] for k in (4 + p, 6 + p)] for c in range(2)]
    use(p, 0, r, [(e[c][0] + o[c][0], e[c][1] + o[c][1]) for c in range(2)])
    use(p, 1, r, [(e[c][0] - o[c][0], e[c][1] - o[c][1]) for c in range(2)])


def grad_kernel(count, slot, row, col, field, images, fars, waves, probe, right_forward, right_inverse, right_back, left_forward, left_inverse, kernel,
                out, total, x, xfull, h, far, wave, measured, image, insem, outsem):
    dump = field.shape[2]
    total[...] = jnp.zeros_like(total)
    live = count[0]

    def inputs(i):
        index = slot[i]
        place = lax.rem(i, 4)
        return (
            pltpu.make_async_copy(images.at[lax.div(index, CAP), lax.rem(index, CAP)], image.at[place], insem.at[place, 0]),
            pltpu.make_async_copy(fars.at[i], far.at[place], insem.at[place, 1]),
            pltpu.make_async_copy(waves.at[i], wave.at[place], insem.at[place, 2]),
        )

    def pattern(i, j, valid, accs):
        top = row[i]
        left = col[i]
        place = top if valid is None else jnp.where(valid, top, dump)
        at = lax.rem(i, 4)
        xj, xf, hj, mj = x.at[j], xfull.at[j], h.at[j], measured.at[j]
        wj, fj, source = wave.at[at], far.at[at], image.at[at]

        def add(s, p, b, r, parts):
            where = spread_rows(place, p, b, r)
            for c in range(2):
                total[2 * s, left + c, where, :] += parts[c][0]
                total[2 * s + 1, left + c, where, :] += parts[c][1]

        def compare(p, b, r, parts):
            scaled = []
            for c in range(2):
                re, im = parts[c]
                misfit = re * re + im * im - mj[c, spread_rows(0, p, b, r), :]
                scaled.append((re * misfit, im * misfit))
            put_natural(xf, p, b, r, scaled)

        def leave(p, b, r, parts):
            where = rows_of(p, b, r)
            add(1, p, b, r, [conjugate_product(wj[where, lanes(c)], wj[where, lanes(2 + c)], *parts[c]) for c in range(2)])
            put(xj, p, b, r, [conjugate_product(*window(field, 1, top, left, p, b, r, c), *parts[c]) for c in range(2)])

        def gather(p, b, r, parts):
            put(xj, p, b, r, [conjugate_product(*chirp(kernel, p, b, r, c), *parts[c]) for c in range(2)])

        def finish(p, b, r, parts):
            add(0, p, b, r, [conjugate_product(*lit(probe, p, b, r, c), *parts[c]) for c in range(2)])

        n = 4 * HALF
        units = n // CHUNK
        acc = [accs[(2 * j + u) * units:(2 * j + u + 1) * units] for u in range(2)]

        def compare_units():
            def convert():
                for c in range(2):
                    mj[c] = source[:, lanes(c)].astype(f32)

            return [convert] + [functools.partial(each_part, fj, compare, p, r) for p in range(2) for r in range(0, HALF, CHUNK)]

        def push(first, second):
            pltpu.matmul_push_rhs(first, j, 0)
            pltpu.matmul_push_rhs(second, j, 1)

        def feed(i, first, second, load):
            pltpu.matmul_acc_lhs(acc[0][i], first, j if load else None)
            pltpu.matmul_acc_lhs(acc[1][i], second, j if load else None)

        def rows(i):
            return slice(i * CHUNK, (i + 1) * CHUNK)

        def right_units(right):
            def unit(i):
                if i == 0:
                    push(right[0], right[1])
                feed(i, xj[0, rows(i), :], xj[1, rows(i), :], i == 0)

            return [functools.partial(unit, i) for i in range(units)]

        def back_units():
            def unit(t, i):
                if i == 0:
                    push(right_back[t * n:(t + 1) * n, :n], right_back[t * n:(t + 1) * n, n:])
                part = xf[rows(i), t * n:(t + 1) * n]
                feed(i, part, part, i == 0)

            return [functools.partial(unit, t, i) for t in range(2) for i in range(units)]

        def half_units(split):
            def unit(i):
                low = pltpu.matmul_pop(acc[0][i])
                high = pltpu.matmul_pop(acc[1][i])
                if split:
                    low, high = low + high, low - high
                m = n // 2
                p, start = divmod(i * CHUNK, m)
                for q in range(2):
                    where = slice(p * n + q * m + start, p * n + q * m + start + CHUNK)
                    hj[where, lanes(0)] = low[:, lanes(q)].astype(bf16)
                    hj[where, lanes(1)] = high[:, lanes(q)].astype(bf16)

            return [functools.partial(unit, i) for i in range(units)]

        order = [(p, r) for p in range(2) for r in range(0, HALF, CHUNK)]

        def left_units(left):
            def unit(i):
                if i == 0:
                    push(hj[:n, :], hj[n:, :])
                p, r = order[i // 2]
                start = (i % 2) * 2 * HALF + p * HALF + r
                feed(i, left[0, start:start + CHUNK, :], left[1, start:start + CHUNK, :], i == 0)

            return [functools.partial(unit, i) for i in range(units)]

        def use_units(use):
            def unit(i):
                p, r = order[i]
                e = [pltpu.matmul_pop(acc[0][2 * i + q]) for q in range(2)]
                o = [pltpu.matmul_pop(acc[1][2 * i + q]) for q in range(2)]
                use(p, 0, r, [(e[0][:, lanes(c)] + o[0][:, lanes(c)], e[1][:, lanes(c)] + o[1][:, lanes(c)]) for c in range(2)])
                use(p, 1, r, [(e[0][:, lanes(c)] - o[0][:, lanes(c)], e[1][:, lanes(c)] - o[1][:, lanes(c)]) for c in range(2)])

            return [functools.partial(unit, i) for i in range(len(order))]

        return compare_units(), [
            (back_units(), half_units(False)), (left_units(left_inverse), use_units(leave)),
            (right_units(right_forward), half_units(True)), (left_units(left_forward), use_units(gather)),
            (right_units(right_inverse), half_units(True)), (left_units(left_inverse), use_units(finish)),
        ]

    def step(k, carry):
        a = 2 * k
        b = jnp.minimum(2 * k + 1, live - 1)
        valid = 2 * k + 1 < live
        for copy in inputs(a):
            copy.wait()

        @pl.when(valid)
        def _():
            for copy in inputs(2 * k + 1):
                copy.wait()

        for ahead in (2, 3):
            @pl.when(2 * k + ahead < live)
            def _():
                for copy in inputs(2 * k + ahead):
                    copy.start()

        def both(*accs):
            first_compare, first = pattern(a, 0, None, accs)
            second_compare, second = pattern(b, 1, valid, accs)
            together(first_compare)
            together(first[0][0], second_compare)
            for s in range(len(first)):
                together(second[s][0], first[s][1])
                together(first[s + 1][0] if s + 1 < len(first) else [], second[s][1])

        n = 4 * HALF
        pl.run_scoped(both, *[
            pltpu.ACC(mxu_id=u)((CHUNK, n), f32) for _ in range(2) for u in range(2) for _ in range(n // CHUNK)
        ])
        return carry

    for s in range(2):
        @pl.when(live > s)
        def _():
            for copy in inputs(s):
                copy.start()
    lax.fori_loop(0, lax.div(live + 1, 2), step, 0)
    store = pltpu.make_async_copy(total.at[:, :, :dump], out, outsem)
    store.start()
    store.wait()


def gradient(count, slot, row, col, field, images, fars, waves, probe, tables):
    planes, cols, rows, width = field.shape
    n = probe.shape[1]
    return pl.pallas_call(
        grad_kernel,
        out_shape=jax.ShapeDtypeStruct(field.shape, f32),
        in_specs=[smem] * 4 + [vmem] + [anyspace] * 3 + [vmem] * 7,
        out_specs=anyspace,
        scratch_shapes=[
            pltpu.VMEM((planes, cols, rows + n, width), f32),
            pltpu.VMEM((2, 2, n, n), bf16),
            pltpu.VMEM((2, n, 2 * n), bf16),
            pltpu.VMEM((2, 2 * n, n), bf16),
            pltpu.VMEM((4, 2 * n, n), f32),
            pltpu.VMEM((4, n, 2 * n), f32),
            pltpu.VMEM((2, 2, n, width), f32),
            pltpu.VMEM((4, n, n), bf16),
            pltpu.SemaphoreType.DMA((4, 3)),
            pltpu.SemaphoreType.DMA,
        ],
        compiler_params=pltpu.CompilerParams(vmem_limit_bytes=VMEM_LIMIT),
        name="gradient",
    )(
        count, slot, row, col, field, images, fars, waves, probe, tables["right_forward"], tables["right_inverse"],
        tables["right_back"], tables["left_forward"], tables["left_inverse"], tables["kernel"],
    )


def reduce_kernel(tiles, slabs, cores, total, unsort, out, part, near, far, outgoing,
                  localsem, csend, crecv, zsend, zrecv, fsend, frecv):
    tile = lax.axis_index("tile")
    slab = lax.axis_index("slab")
    levels = slabs // cores
    core = lax.rem(slab, cores)
    level = lax.div(slab, cores)
    other = level * cores + (1 - core)
    following = lax.rem(tile + 1, tiles)
    preceding = lax.rem(tile + tiles - 1, tiles)
    barrier = pltpu.get_barrier_semaphore()

    def greet(t, s):
        pl.semaphore_signal(barrier, inc=1, device_id={"tile": t, "slab": s}, device_id_type=MESH)

    greet(tile, other)
    for d in range(1, levels):
        greet(tile, lax.rem(level + d, levels) * cores + core)
    for d in range(levels):
        place = lax.rem(level + d, levels) * cores + core
        greet(following, place)
        greet(preceding, place)
    def block(which, d):
        return which * levels + lax.rem(level + d, levels)

    order = [(1, 2), (1, 1), (1, 3), (0, 2), (0, 1), (0, 3), (1, 0), (0, 0)]
    takes = []
    for k, (which, d) in enumerate(order):
        take = pltpu.make_async_copy(total.at[:, :, block(which, d), core], part.at[k], localsem.at[k])
        take.start()
        takes.append(take)
    pl.semaphore_wait(barrier, 1 + levels - 1 + 2 * levels)

    swaps = []
    for k, (which, d) in enumerate(order):
        b = block(which, d)
        copy = pltpu.make_async_remote_copy(
            src_ref=total.at[:, :, b, 1 - core], dst_ref=near.at[k], send_sem=csend.at[k], recv_sem=crecv.at[k],
            device_id={"tile": tile, "slab": other}, device_id_type=MESH,
        )
        copy.start()
        swaps.append(copy)
    sends = []
    for k, (which, d) in enumerate(order):
        takes[k].wait()
        swaps[k].wait_recv()
        if (which, d) == (0, 0):
            continue
        outgoing[k] = (part[k] + near[k]).astype(bf16)
        place = lax.rem(level + d, levels) * cores + core
        if which == 0:
            copy = pltpu.make_async_remote_copy(
                src_ref=outgoing.at[k], dst_ref=far.at[d - 1], send_sem=zsend.at[d - 1], recv_sem=zrecv.at[d - 1],
                device_id={"tile": tile, "slab": place}, device_id_type=MESH,
            )
        else:
            copy = pltpu.make_async_remote_copy(
                src_ref=outgoing.at[k], dst_ref=far.at[levels - 1 + d], send_sem=fsend.at[d], recv_sem=frecv.at[d],
                device_id={"tile": following, "slab": place}, device_id_type=MESH,
            )
        copy.start()
        sends.append(copy)
    for copy in sends:
        copy.wait()
    for copy in swaps:
        copy.wait_send()
    last = len(order) - 1
    for p in range(4):
        for h in range(3):
            value = part[last, p, h] + near[last, p, h]
            for k in range(2 * levels - 1):
                value = value + far[k, p, h].astype(f32)
            out[p // 2, p % 2, :, lanes(h)] = rearrange(value, unsort[...])


def reduce(total, tiles, slabs):
    cores = 2
    levels = slabs // cores
    planes, cols, rows, lanes = total.shape
    each = rows // (2 * slabs)
    sem = pltpu.SemaphoreType.DMA
    count = 2 * levels
    total = total.reshape(planes, cols, rows // (cores * each), cores, each, lanes)
    return pl.pallas_call(
        functools.partial(reduce_kernel, tiles, slabs, cores),
        out_shape=jax.ShapeDtypeStruct((2, 2, each, cols * lanes), f32),
        in_specs=[anyspace, vmem],
        out_specs=vmem,
        scratch_shapes=[
            pltpu.VMEM((count, planes, cols, each, lanes), f32),
            pltpu.VMEM((count, planes, cols, each, lanes), f32),
            pltpu.VMEM((count - 1, planes, cols, each, lanes), bf16),
            pltpu.VMEM((count, planes, cols, each, lanes), bf16),
            sem((count,)),
            sem((count,)), sem((count,)),
            sem((levels - 1,)), sem((levels - 1,)),
            sem((levels,)), sem((levels,)),
        ],
        compiler_params=pltpu.CompilerParams(collective_id=1, has_side_effects=True, vmem_limit_bytes=VMEM_LIMIT),
        name="reduce",
    )(total, lane_order().T)


def shards(intensities, object_field, probe_wave, owner_tile, row_offset, col_offset):
    tiles = lax.axis_size("tile")
    slabs = lax.axis_size("slab")
    pick, count, slot, row, col = route(
        owner_tile, row_offset, col_offset, intensities.shape[0], tiles, slabs
    )
    tables = make_tables(intensities.shape[1])
    images, field, fars, waves, probe = exchange(
        intensities, object_field, probe_wave, pick, row, col, tables, tiles, slabs
    )
    total = gradient(count, slot, row, col, field, images, fars, waves, probe, tables)
    return reduce(total, tiles, slabs)


def solution(mesh):
    placed = (
        P(("tile", "slab"), None, None),
        P(None, None, ("tile", "slab"), None),
        P(),
        P(),
        P(),
        P(),
    )
    return jax.shard_map(
        shards,
        mesh=mesh,
        in_specs=placed,
        out_specs=P(None, None, ("tile", "slab"), None),
        check_vma=False,
    )
```
